32 devices in a mesh: dp: 8 (over z, y), seq: 4 (over x, core).
Axes of the slice: x: 2, y: 2, z: 4, core: 2. Of those that a mesh axis runs over, the one named last changes fastest.
Arguments:
- hidden_in: bfloat16 [8, 512, 768], P('dp', 'seq'), may hold values from -6 to 6
- segments: int32 [8, 512], P('dp'), may hold values from 0 to 3, never falling along the last dimension, each value on 1 to 256 neighbouring positions
- norm_gain: bfloat16 [768], P(('dp', 'seq')), may hold values from 0.5 to 1.5
- in_weight: bfloat16 [768, 3352], P(('dp', 'seq')), may hold values from -0.21875 to 0.21875
- conv_weight: bfloat16 [4, 1792], P(None, ('dp', 'seq')), may hold values from -0.5 to 0.5
- conv_bias: bfloat16 [1792], P(('dp', 'seq')), may hold values from -0.5 to 0.5
- step_bias: float32 [24], replicated, may hold values from -4.5 to -1
- decay_log: float32 [24], replicated, may hold values from -4 to 1.5
- skip_weight: float32 [24], replicated, may hold values from 0.5 to 1.5
- gate_gain: bfloat16 [1536], P(('dp', 'seq')), may hold values from 0.5 to 1.5
- out_weight: bfloat16 [1536, 768], P(('dp', 'seq')), may hold values from -0.15625 to 0.15625
- out_grad: bfloat16 [8, 512, 768], P('dp', 'seq'), may hold values from -6 to 6
Outputs:
- output: float32 [8, 512, 768], P('dp', 'seq')
- grad_hidden: float32 [8, 512, 768], P('dp', 'seq')
- grad_norm_gain: float32 [768], P(('dp', 'seq'))
- grad_in_weight: float32 [768, 3352], P(('dp', 'seq'))
- grad_conv_weight: float32 [4, 1792], P(None, ('dp', 'seq'))
- grad_conv_bias: float32 [1792], P(('dp', 'seq'))
- grad_step_bias: float32 [24], replicated
- grad_decay_log: float32 [24], replicated
- grad_skip_weight: float32 [24], replicated
- grad_gate_gain: float32 [1536], P(('dp', 'seq'))
- grad_out_weight: float32 [1536, 768], P(('dp', 'seq'))
The draws below stay inside these ranges and needn't reach their ends.
Inputs may be any that keep to these rules, and one draw needn't show every extreme that they name: `segments`: within each row the segment numbers never fall and start at 0; each segment has 1 to 256 tokens and one has exactly 256.
All inputs are finite; a program needn't handle non-finite values.
Results may differ from the reference program's by a relative error of at most 0.007.
Values may be sent and summed in bfloat16 or wider, within the bound.
No kernel may reach another device: no remote copies, remote signals or barrier semaphores. Data moves between devices by JAX's collectives and lax.ppermute only.
A program may use at most 128 MiB of HBM per device.

```python
import math
import jax
import jax.numpy as jnp
import numpy as np
from jax import lax

D = 768
INNER = 1536
HEADS = 24
HEAD_DIM = 64
STATE = 128
CONV = 4
PIECE = 128
PROJ = 3352
CHANNELS = 1792
LEN = 512
ROWS = 8


def block_levels(stream_key, extent, pieces, smallest, largest):
    loudness = 1.0
    for dim, shards_of in pieces:
        draws = jax.random.uniform(jax.random.fold_in(jax.random.fold_in(stream_key, 6), dim), (shards_of,), jnp.float32, smallest / len(pieces), largest / len(pieces))
        loudness = loudness * jnp.repeat(jnp.exp(draws), extent[dim] // shards_of).reshape((-1,) + (1,) * (len(extent) - 1 - dim))
    return loudness


def profile(amount, total, bound, slope):
    loads = [(1 << 20) // math.isqrt(grade ** slope) + 1 for grade in range(2, amount + 1)]
    rest, counts = total - bound - (amount - 1), [1] * (amount - 1)
    while rest > 0:
        candidates = [i for i in range(amount - 1) if counts[i] < bound]
        whole, remaining = sum([loads[i] for i in candidates]), rest
        for i in candidates:
            extra = min(bound - counts[i], max(1, remaining * loads[i] // whole), rest)
            counts[i] = counts[i] + extra
            rest = rest - extra
    return np.array([bound] + counts)


def ragged_sizes(own_key, count, total, limit, slope):
    if count == 2:
        one = jax.random.randint(own_key, (), max(1, total - limit), min(limit, total - 1) + 1)
        return jnp.stack([one, total - one])
    lengths = jnp.asarray(profile(count, total, limit, slope), jnp.int32)
    couples = (count - 1) // 2
    giver, receiver = lengths[1:1 + 2 * couples:2], lengths[2:2 + 2 * couples:2]
    margin = jnp.minimum(giver - 1, limit - receiver)
    shifted = jax.random.randint(jax.random.fold_in(own_key, 1), (couples,), 0, 1 << 20) % (margin + 1)
    lengths = lengths.at[1:1 + 2 * couples:2].set(giver - shifted).at[2:2 + 2 * couples:2].set(receiver + shifted)
    return lengths[jax.random.permutation(jax.random.fold_in(own_key, 2), count)]


def scatter_about(key, extent, width, limit, pieces=(), kind=jnp.bfloat16):
    level = block_levels(key, extent, pieces, -0.22, 0.18) if pieces else 1.0
    values = jax.random.normal(key, extent, jnp.float32) * width * level
    return jnp.minimum(jnp.maximum(values, -limit), limit).astype(kind)


def setup_inputs(seed: int = 0) -> dict:
    streams_of = jax.random.split(jax.random.key(seed), 13)
    hidden_in = scatter_about(streams_of[0], (ROWS, LEN, D), 1.0, 6.0, ((0, 8), (1, 4)))
    segments = jax.vmap(lambda own: jnp.searchsorted(jnp.cumsum(ragged_sizes(own, 4, LEN, LEN // 2, 0)), jnp.arange(LEN), side="right"))(jax.random.split(streams_of[1], ROWS)).reshape((ROWS, LEN)).astype(jnp.int32)
    norm_gain = jnp.clip(1.0 + 0.1 * jax.random.normal(streams_of[2], (D,), jnp.float32), 0.5, 1.5).astype(jnp.bfloat16)
    in_weight = scatter_about(streams_of[3], (D, PROJ), D ** -0.5, 0.21875, ((0, 32),))
    conv_weight = jnp.clip(jax.random.uniform(streams_of[4], (CONV, CHANNELS), jnp.float32, -0.5, 0.5) * block_levels(streams_of[4], (CONV, CHANNELS), ((1, 32),), -0.4, 0.0), -0.5, 0.5).astype(jnp.bfloat16)
    conv_bias = jnp.clip(jax.random.uniform(streams_of[5], (CHANNELS,), jnp.float32, -0.5, 0.5) * block_levels(streams_of[5], (CHANNELS,), ((0, 32),), -0.4, 0.0), -0.5, 0.5).astype(jnp.bfloat16)
    step_bias = jnp.clip(jax.random.uniform(streams_of[6], (HEADS,), jnp.float32, -4.5, -1.0), -4.5, -1.0)
    decay_log = jnp.clip(jax.random.uniform(streams_of[7], (HEADS,), jnp.float32, -4.0, 1.5), -4.0, 1.5)
    skip_weight = jnp.clip(jax.random.uniform(streams_of[8], (HEADS,), jnp.float32, 0.5, 1.5), 0.5, 1.5)
    gate_gain = jnp.clip(1.0 + 0.1 * jax.random.normal(streams_of[9], (INNER,), jnp.float32), 0.5, 1.5).astype(jnp.bfloat16)
    out_weight = scatter_about(streams_of[10], (INNER, D), INNER ** -0.5, 0.15625, ((0, 32),))
    out_grad = scatter_about(streams_of[11], (ROWS, LEN, D), 1.0, 6.0, ((0, 8), (1, 4)))
    return dict(hidden_in=hidden_in, segments=segments, norm_gain=norm_gain, in_weight=in_weight, conv_weight=conv_weight, conv_bias=conv_bias, step_bias=step_bias, decay_log=decay_log, skip_weight=skip_weight, gate_gain=gate_gain, out_weight=out_weight, out_grad=out_grad)


EPSILON = 1e-05
PRECISE = lax.Precision.HIGHEST

def conv_block(window_in, segment_window, conv_taps, conv_shift):
    length_now = window_in.shape[0] - (CONV - 1)
    running = jnp.zeros((length_now, window_in.shape[1]), jnp.float32) + conv_shift[None, :]
    for offset in range(CONV):
        same_segment = (segment_window[offset:offset + length_now] == segment_window[CONV - 1:]).astype(jnp.float32)
        running = running + conv_taps[offset][None, :] * window_in[offset:offset + length_now] * same_segment[:, None]
    return jax.nn.silu(running)

def ssd_core(channels, raw_steps, segment_now, segment_before, bias_step, log_rate, skip_term):
    length_now = channels.shape[0]
    inner_width = channels.shape[1] - 2 * STATE
    values = channels[:, :inner_width].reshape(length_now, HEADS, HEAD_DIM)
    keys_b = channels[:, inner_width:inner_width + STATE]
    query_c = channels[:, inner_width + STATE:]
    step_size = jax.nn.softplus(raw_steps + bias_step[None, :])
    log_decay = step_size * (-jnp.exp(log_rate))[None, :]
    cumulative = jnp.cumsum(log_decay, axis=0)
    places = jnp.arange(length_now)
    pair_mask = ((places[:, None] >= places[None, :]) & (segment_now[:, None] == segment_now[None, :]))[:, :, None]
    gap_log = cumulative[:, None, :] - cumulative[None, :, :]
    decay_pair = jnp.where(pair_mask, jnp.exp(jnp.where(pair_mask, gap_log, 0.0)), 0.0)
    scores = jnp.dot(query_c, keys_b.T, precision=PRECISE, preferred_element_type=jnp.float32)
    mixing = scores[:, :, None] * decay_pair * step_size[None, :, :]
    inner_out = jnp.einsum('tsh,shp->thp', mixing, values, precision=PRECISE)
    local_out = inner_out + skip_term[None, :, None] * values
    entry_gate = jnp.exp(cumulative) * (segment_now == segment_before).astype(jnp.float32)[:, None]
    last_log = cumulative[length_now - 1]
    tail_weight = jnp.exp(last_log[None, :] - cumulative) * (segment_now == segment_now[length_now - 1]).astype(jnp.float32)[:, None] * step_size
    weighted = values * tail_weight[:, :, None]
    fresh_state = jnp.einsum('shp,sn->hpn', weighted, keys_b, precision=PRECISE)
    through = jnp.exp(last_log) * (segment_now[length_now - 1] == segment_before).astype(jnp.float32)
    return (local_out, through, fresh_state, entry_gate, query_c)

def gated_norm(mixed_flat, gate_half, gain_vec):
    product = mixed_flat * jax.nn.silu(gate_half)
    scale_inv = lax.rsqrt(lax.optimization_barrier(jnp.mean(product * product, axis=-1, keepdims=True)) + EPSILON)
    return product * scale_inv * gain_vec[None, :]

def pre_norm(widened, gain_vec):
    scale_inv = lax.rsqrt(lax.optimization_barrier(jnp.mean(widened * widened, axis=-1, keepdims=True)) + EPSILON)
    return widened * scale_inv * gain_vec[None, :]

def middle(projected, segment_row, conv_taps, conv_shift, bias_step, log_rate, skip_term, gain_vec):
    inner_width = HEADS * HEAD_DIM
    gate_half = projected[:, :inner_width]
    conv_input = projected[:, inner_width:inner_width + CHANNELS]
    raw_steps = projected[:, inner_width + CHANNELS:]
    window_in = jnp.concatenate([jnp.zeros((CONV - 1, CHANNELS), jnp.float32), conv_input], axis=0)
    segment_window = jnp.concatenate([jnp.full((CONV - 1,), -1, jnp.int32), segment_row.astype(jnp.int32)], axis=0)
    channels = conv_block(window_in, segment_window, conv_taps, conv_shift)
    blocks = LEN // PIECE
    block_channels = channels.reshape(blocks, PIECE, CHANNELS)
    block_raw = raw_steps.reshape(blocks, PIECE, HEADS)
    block_segments = segment_row.astype(jnp.int32).reshape(blocks, PIECE)
    before = segment_window[(CONV - 2 + PIECE * jnp.arange(blocks)).astype(jnp.int32)]

    def advance(carried, inputs):
        block_in, raw_in, segment_in, prior = inputs
        local_out, through, fresh_state, entry_gate, query_c = ssd_core(block_in, raw_in, segment_in, prior, bias_step, log_rate, skip_term)
        mixed = local_out + jnp.einsum('tn,hpn->thp', query_c, carried, precision=PRECISE) * entry_gate[:, :, None]
        return (through[:, None, None] * carried + fresh_state, mixed)
    start_state = jnp.zeros((HEADS, HEAD_DIM, STATE), jnp.float32)
    _, mixed_all = lax.scan(advance, start_state, (block_channels, block_raw, block_segments, before))
    return gated_norm(mixed_all.reshape(LEN, inner_width), gate_half, gain_vec)

def reference(hidden_in, segments, norm_gain, in_weight, conv_weight, conv_bias, step_bias, decay_log, skip_weight, gate_gain, out_weight, out_grad):
    norm_gain32 = norm_gain.astype(jnp.float32)
    conv_taps = conv_weight.astype(jnp.float32)
    conv_shift = conv_bias.astype(jnp.float32)
    gate_gain32 = gate_gain.astype(jnp.float32)

    def per_row(totals, inputs):
        row_in, segment_row, cotangent = inputs
        widened = row_in.astype(jnp.float32)
        normed_f, norm_back = jax.vjp(pre_norm, widened, norm_gain32)
        normed = normed_f.astype(jnp.bfloat16)
        projected = jnp.dot(normed, in_weight, preferred_element_type=jnp.float32)

        def mid_piece(proj_in, taps_in, shift_in, bias_in, rate_in, skip_in, gain_in):
            return middle(proj_in, segment_row, taps_in, shift_in, bias_in, rate_in, skip_in, gain_in)
        gated_f, mid_back = jax.vjp(mid_piece, projected, conv_taps, conv_shift, step_bias, decay_log, skip_weight, gate_gain32)
        gated_out = gated_f.astype(jnp.bfloat16)
        result = widened + jnp.dot(gated_out, out_weight, preferred_element_type=jnp.float32)
        grad_out_w = jnp.dot(gated_out.T, cotangent, preferred_element_type=jnp.float32)
        d_gated = jnp.dot(cotangent, out_weight.T, preferred_element_type=jnp.float32)
        d_proj32, d_taps, d_shift, d_bias, d_rate, d_skip, d_gain = mid_back(d_gated)
        d_projected = d_proj32.astype(jnp.bfloat16)
        grad_in_w = jnp.dot(normed.T, d_projected, preferred_element_type=jnp.float32)
        d_normed = jnp.dot(d_projected, in_weight.T, preferred_element_type=jnp.float32)
        d_wide, d_norm_gain = norm_back(d_normed)
        grad_row = cotangent.astype(jnp.float32) + d_wide
        adding = (d_norm_gain, grad_in_w, d_taps, d_shift, d_bias, d_rate, d_skip, d_gain, grad_out_w)
        totals = jax.tree.map(lambda left_part, right_part: left_part + right_part, totals, adding)
        return (totals, (result, grad_row))
    start = (jnp.zeros((D,), jnp.float32), jnp.zeros((D, PROJ), jnp.float32), jnp.zeros((CONV, CHANNELS), jnp.float32), jnp.zeros((CHANNELS,), jnp.float32), jnp.zeros((HEADS,), jnp.float32), jnp.zeros((HEADS,), jnp.float32), jnp.zeros((HEADS,), jnp.float32), jnp.zeros((INNER,), jnp.float32), jnp.zeros((INNER, D), jnp.float32))
    totals, (output, grad_hidden) = lax.scan(per_row, start, (hidden_in, segments, out_grad))
    g_norm, g_in, g_taps, g_shift, g_bias, g_rate, g_skip, g_gain, g_out = totals
    return (output, grad_hidden, g_norm, g_in, g_taps, g_shift, g_bias, g_rate, g_skip, g_gain, g_out)
```

```python
import jax
import jax.numpy as jnp
from jax import lax
from jax.experimental import pallas as pl
from jax.experimental.pallas import tpu as pltpu
from jax.sharding import PartitionSpec as P

HEAD_DIM = 64
STATE = 128
CONV = 4
CHUNK = 128
LANES = 128
EPSILON = 1e-05
FULL = lax.Precision.HIGHEST
F32 = jnp.float32
BF16 = jnp.bfloat16


def swap(x, axis, offset):
    count = lax.axis_size(axis)
    return lax.ppermute(x, axis, [(i, i ^ offset) for i in range(count)])


def tree_sum(parts):
    while len(parts) > 1:
        parts = [parts[i] + parts[i + 1] for i in range(0, len(parts), 2)]
    return parts[0]


def in_order(pieces, place):
    stacked = jnp.stack(pieces)
    return [lax.dynamic_index_in_dim(stacked, j ^ place, 0, False) for j in range(len(pieces))]


def gather_xor(x, axis):
    return [x] + [swap(x, axis, k) for k in range(1, lax.axis_size(axis))]


def scatter_xor(blocks, axis):
    place = lax.axis_index(axis)
    return [
        swap(lax.dynamic_index_in_dim(blocks, place ^ k, 0, False), axis, k)
        if k
        else lax.dynamic_index_in_dim(blocks, place, 0, False)
        for k in range(lax.axis_size(axis))
    ]


def inner_of(count):
    inner = 1
    while 2 * inner * inner < count:
        inner *= 2
    return inner


def gather_dp(x):
    count = lax.axis_size("dp")
    inner = inner_of(count)
    far = [x] + [swap(x, "dp", k * inner) for k in range(1, count // inner)]
    near = [[piece] + [swap(piece, "dp", j) for j in range(1, inner)] for piece in far]
    return [near[m // inner][m % inner] for m in range(count)]


def reduce_dp(grads):
    count = lax.axis_size("dp")
    inner = inner_of(count)
    place = lax.axis_index("dp")
    outer_place, inner_place = place // inner, place % inner
    shaped = grads.reshape(count // inner, inner, *grads.shape[1:])
    parts = []
    for j in range(inner):
        slab = lax.dynamic_index_in_dim(shaped, inner_place ^ j, 1, False)
        parts.append(swap(slab, "dp", j) if j else slab)
    near = tree_sum([p.astype(F32) for p in parts]).astype(BF16)
    parts = []
    for k in range(count // inner):
        slab = lax.dynamic_index_in_dim(near, outer_place ^ k, 0, False)
        parts.append(swap(slab, "dp", k * inner) if k else slab)
    return tree_sum([p.astype(F32) for p in parts])


def dot(a, b, ca, cb, precision=None):
    return lax.dot_general(
        a, b, (((ca,), (cb,)), ((), ())), precision=precision, preferred_element_type=F32
    )


def mm(a, b):
    return dot(a, b, 1, 0, FULL)


def mm_nt(a, b):
    return dot(a, b, 1, 1, FULL)


def mm_tn(a, b):
    return dot(a, b, 0, 0, FULL)


def softplus(x):
    small = jnp.exp(-jnp.abs(x))
    up = 1.0 + small
    down = up - 1.0
    log1p = jnp.where(down == 0.0, small, jnp.log(up) * (small / jnp.where(down == 0.0, 1.0, down)))
    return jnp.maximum(x, 0.0) + log1p


def expand_matrix(width):
    head = lax.broadcasted_iota(jnp.int32, (LANES, width), 0)
    column = lax.broadcasted_iota(jnp.int32, (LANES, width), 1)
    return (column // HEAD_DIM == head).astype(F32)


def triangle(lower):
    row = lax.broadcasted_iota(jnp.int32, (CHUNK, CHUNK), 0)
    column = lax.broadcasted_iota(jnp.int32, (CHUNK, CHUNK), 1)
    return row >= column if lower else row <= column


def masks_of(segment_col, segment_rows, i):
    far = (segment_col == segment_rows[i]).astype(F32)
    near = (segment_col == segment_rows[i + 1]).astype(F32)
    own = (segment_col == segment_rows[i + 2]) & triangle(True)
    return far, near, own


def lane_halves():
    lane = lax.broadcasted_iota(jnp.int32, (1, LANES), 1)
    low = (lane < HEAD_DIM).astype(F32)
    return low, 1.0 - low


def rms_inverse(x):
    return lax.rsqrt(jnp.mean(x * x, axis=-1, keepdims=True) + EPSILON)


def gain_row(weights, lane_of_gain):
    tail = weights[:, weights.shape[1] - LANES :]
    pick = (lax.broadcasted_iota(jnp.int32, (8, LANES), 1) == lane_of_gain).astype(BF16)
    return dot(pick, tail, 1, 1)[:1]


def decays(raw, heads):
    step = softplus(raw + heads[0:1])
    return step, step * (-jnp.exp(heads[1:2]))


def fill_sources(i, v, step, decay, expand, vd, vt, ecx):
    cumulative = mm(triangle(True).astype(F32), decay)
    step_x = mm(step, expand)
    cum_x = mm(cumulative, expand)
    last = cum_x[CHUNK - 1 :]
    vd_now = v * step_x
    vd[pl.ds(i * CHUNK, CHUNK), :] = vd_now
    vt[pl.ds((i + 2) * CHUNK, CHUNK), :] = vd_now * jnp.exp(last - cum_x)
    ecx[pl.ds(i * CHUNK + 8, CHUNK), :] = jnp.exp(cum_x)
    return cumulative, step_x, cum_x, last


def head_decay(cumulative, cumulative_t, own, h):
    gap = cumulative[:, h : h + 1] - cumulative_t[h : h + 1, :]
    return jnp.exp(jnp.where(own, gap, -1e30))


def forward_kernel(width, lane_of_gain):
    heads_here = width // HEAD_DIM

    def body(x_ref, w_ref, conv_ref, same_ref, seg_ref, segr_ref, head_ref, normed_ref, proj_ref, pre_ref, y_ref, bpad, vd, vt, ecx):
        x = x_ref[...].astype(F32)
        gain = gain_row(w_ref[...], lane_of_gain)
        normed_ref[...] = (x * rms_inverse(x) * gain).astype(BF16)
        proj_ref[...] = dot(normed_ref[...], w_ref[...], 1, 0)
        channels = width + 2 * STATE
        u = proj_ref[:, :channels]
        running = conv_ref[CONV : CONV + 1, :] + conv_ref[CONV - 1 : CONV, :] * u
        for back in range(1, CONV):
            tap = conv_ref[CONV - 1 - back : CONV - back, :]
            running = running + tap * pltpu.roll(u, back, 0) * same_ref[:, back : back + 1]
        pre_ref[...] = running
        bpad[pl.ds(0, 2 * CHUNK), :] = jnp.zeros((2 * CHUNK, STATE), F32)
        vt[pl.ds(0, 2 * CHUNK), :] = jnp.zeros((2 * CHUNK, width), F32)
        ecx[pl.ds(0, 8), :] = jnp.zeros((8, width), F32)
        b_pre = running[:, width : width + STATE]
        bpad[pl.ds(2 * CHUNK, x.shape[0]), :] = b_pre * jax.nn.sigmoid(b_pre)
        expand = expand_matrix(width)
        low, high = lane_halves()
        heads = head_ref[...]
        skip_x = mm(jnp.broadcast_to(heads[2:3], (8, LANES)), expand)[:1]

        def chunk(i, carry):
            rows = pl.ds(pl.multiple_of(i * CHUNK, CHUNK), CHUNK)
            v_pre = pre_ref[rows, :width]
            c_pre = pre_ref[rows, width + STATE :]
            v = v_pre * jax.nn.sigmoid(v_pre)
            c = c_pre * jax.nn.sigmoid(c_pre)
            step, decay = decays(proj_ref[rows, channels:], heads)
            cumulative, _, _, _ = fill_sources(i, v, step, decay, expand, vd, vt, ecx)
            cumulative_t = cumulative.T
            far, near, own = masks_of(seg_ref[rows, :], segr_ref, i)
            window = pl.ds(pl.multiple_of(i * CHUNK, CHUNK), 3 * CHUNK)
            scores = mm_nt(c, bpad[window, :])
            s_far = scores[:, :CHUNK] * far
            s_near = scores[:, CHUNK : 2 * CHUNK] * near
            s_own = scores[:, 2 * CHUNK :]
            ecx_now = ecx[pl.ds(pl.multiple_of(i * CHUNK, 8) + 8, CHUNK), :]
            last_before = ecx[pl.ds(pl.multiple_of(i * CHUNK, 8), 8), :][7:8]
            vt_far = vt[rows, :] * last_before
            vt_near = vt[pl.ds(pl.multiple_of((i + 1) * CHUNK, CHUNK), CHUNK), :]
            off = mm(s_far, vt_far) + mm(s_near, vt_near)
            y_ref[rows, :] = off * ecx_now + skip_x * v
            for pair in range(heads_here // 2):
                lanes = slice(pair * LANES, (pair + 1) * LANES)
                n0 = s_own * head_decay(cumulative, cumulative_t, own, 2 * pair)
                n1 = s_own * head_decay(cumulative, cumulative_t, own, 2 * pair + 1)
                vp = vd[rows, lanes]
                both = mm(jnp.concatenate([n0, n1], 1), jnp.concatenate([vp * low, vp * high], 0))
                y_ref[rows, lanes] = y_ref[rows, lanes] + both
            return carry

        lax.fori_loop(0, x.shape[0] // CHUNK, chunk, 0)

    return body


def gate_kernel(width):
    def body(normed_ref, wg_ref, og_ref, wo_ref, y_ref, gain_ref, gate_ref, dg_ref, stats_ref):
        gate = dot(normed_ref[...], wg_ref[...], 1, 0)
        gate_ref[...] = gate
        d_gated = dot(og_ref[...], wo_ref[...], 1, 1)
        dg_ref[...] = d_gated
        v = y_ref[...] * (gate * jax.nn.sigmoid(gate))
        squares = jnp.sum(v * v, axis=1, keepdims=True)
        cross = jnp.sum(v * (d_gated * gain_ref[...]), axis=1, keepdims=True)
        lane = lax.broadcasted_iota(jnp.int32, (CHUNK, LANES), 1)
        for i in range(stats_ref.shape[0]):
            rows = slice(i * CHUNK, (i + 1) * CHUNK)
            both = jnp.where(lane == 0, squares[rows], jnp.where(lane == 1, cross[rows], 0.0))
            stats_ref[i] = both.T[:8]

    return body


def out_kernel(width, whole_width):
    def body(stats_ref, normed_ref, gate_ref, dg_ref, y_ref, gain_ref, og_ref, wo_ref, out_ref, gout_ref, ggate_ref, dgate_ref, dy_ref, ggain_ref):
        columns = []
        for i in range(stats_ref.shape[0]):
            square = jnp.concatenate([stats_ref[i], jnp.zeros((CHUNK - 8, LANES), F32)], 0)
            columns.append(square.T)
        columns = jnp.concatenate(columns, 0)
        inverse = lax.rsqrt(columns[:, 0:1] / whole_width + EPSILON)
        cross = columns[:, 1:2] / whole_width
        gate = gate_ref[...]
        sig = jax.nn.sigmoid(gate)
        silu = gate * sig
        y = y_ref[...]
        v = y * silu
        gain = gain_ref[...]
        scaled = v * inverse
        gated = (scaled * gain).astype(BF16)
        out_ref[...] = dot(gated, wo_ref[...], 1, 0).astype(BF16)
        gout_ref[...] = dot(gated, og_ref[...], 0, 0).astype(BF16)
        d_gated = dg_ref[...]
        ggain_ref[...] = jnp.broadcast_to(jnp.sum(d_gated * scaled, axis=0, keepdims=True), (8, width))
        dv = inverse * (d_gated * gain - v * (inverse * inverse * cross))
        dy_ref[...] = dv * silu
        dgate = (dv * y * (sig * (1.0 + gate * (1.0 - sig)))).astype(BF16)
        dgate_ref[...] = dgate
        ggate_ref[...] = dot(normed_ref[...], dgate, 0, 0).astype(BF16)

    return body


def backward_kernel(width, lane_of_gain):
    heads_here = width // HEAD_DIM

    def body(x_ref, normed_ref, w_ref, wg_ref, conv_ref, same_ref, seg_ref, segr_ref, head_ref, proj_ref, pre_ref, y_ref, dy_ref, dgate_ref, gin_ref, dn_ref, conv_grad_ref, head_grad_ref, norm_grad_ref, bpad, vd, vt, ecx, tailx, stepx, cums, ua, db, dpre, draw):
        length = x_ref.shape[0]
        chunks = length // CHUNK
        channels = width + 2 * STATE
        expand = expand_matrix(width)
        low, high = lane_halves()
        heads = head_ref[...]
        rate = jnp.exp(heads[1:2])
        skip_x = mm(jnp.broadcast_to(heads[2:3], (8, LANES)), expand)[:1]
        bpad[pl.ds(0, 2 * CHUNK), :] = jnp.zeros((2 * CHUNK, STATE), F32)
        vt[pl.ds(0, 2 * CHUNK), :] = jnp.zeros((2 * CHUNK, width), F32)
        tailx[pl.ds(0, 2 * CHUNK), :] = jnp.zeros((2 * CHUNK, width), F32)
        ecx[pl.ds(0, 8), :] = jnp.zeros((8, width), F32)
        b_pre = pre_ref[:, width : width + STATE]
        bpad[pl.ds(2 * CHUNK, length), :] = b_pre * jax.nn.sigmoid(b_pre)
        ua[...] = jnp.zeros(ua.shape, F32)
        db[...] = jnp.zeros(db.shape, F32)

        def prepare(i, carry):
            rows = pl.ds(pl.multiple_of(i * CHUNK, CHUNK), CHUNK)
            v_pre = pre_ref[rows, :width]
            v = v_pre * jax.nn.sigmoid(v_pre)
            step, decay = decays(proj_ref[rows, channels:], heads)
            cumulative, step_x, cum_x, last = fill_sources(i, v, step, decay, expand, vd, vt, ecx)
            cums[rows, :] = cumulative
            stepx[rows, :] = step_x
            tailx[pl.ds(pl.multiple_of((i + 2) * CHUNK, CHUNK), CHUNK), :] = jnp.exp(last - cum_x)
            return carry

        lax.fori_loop(0, chunks, prepare, 0)

        def chunk(turn, carry):
            later, g_bias, g_rate, g_skip = carry
            i = chunks - 1 - turn
            rows = pl.ds(pl.multiple_of(i * CHUNK, CHUNK), CHUNK)
            rows_near = pl.ds(pl.multiple_of((i + 1) * CHUNK, CHUNK), CHUNK)
            rows_own = pl.ds(pl.multiple_of((i + 2) * CHUNK, CHUNK), CHUNK)
            window = pl.ds(pl.multiple_of(i * CHUNK, CHUNK), 3 * CHUNK)
            v_pre = pre_ref[rows, :width]
            v_sig = jax.nn.sigmoid(v_pre)
            v = v_pre * v_sig
            c_pre = pre_ref[rows, width + STATE :]
            c_sig = jax.nn.sigmoid(c_pre)
            c = c_pre * c_sig
            raw = proj_ref[rows, channels:]
            step, decay = decays(raw, heads)
            cumulative = cums[rows, :]
            cumulative_t = cumulative.T
            far, near, own = masks_of(seg_ref[rows, :], segr_ref, i)
            b_window = bpad[window, :]
            scores = mm_nt(c, b_window)
            s_far = scores[:, :CHUNK] * far
            s_near = scores[:, CHUNK : 2 * CHUNK] * near
            s_own = scores[:, 2 * CHUNK :]
            dy = dy_ref[rows, :]
            dye = dy * ecx[pl.ds(pl.multiple_of(i * CHUNK, 8) + 8, CHUNK), :]
            dye_far = dye * ecx[pl.ds(pl.multiple_of(i * CHUNK, 8), 8), :][7:8]
            ds_far = mm_nt(dye_far, vt[rows, :]) * far
            ds_near = mm_nt(dye, vt[rows_near, :]) * near
            ua[rows, :] = ua[rows, :] + tailx[rows, :] * mm_tn(s_far, dye_far)
            ua[rows_near, :] = ua[rows_near, :] + tailx[rows_near, :] * mm_tn(s_near, dye)
            ds_own = jnp.zeros((CHUNK, CHUNK), F32)
            for pair in range(heads_here // 2):
                lanes = slice(pair * LANES, (pair + 1) * LANES)
                d0 = head_decay(cumulative, cumulative_t, own, 2 * pair)
                d1 = head_decay(cumulative, cumulative_t, own, 2 * pair + 1)
                dyp = dy_ref[rows, lanes]
                split = jnp.concatenate([dyp * low, dyp * high], 0)
                dm = mm_nt(split, vd[rows, lanes])
                ds_own = ds_own + dm[:CHUNK] * d0 + dm[CHUNK:] * d1
                u_pair = mm_tn(jnp.concatenate([s_own * d0, s_own * d1], 0), split)
                ua[rows_own, lanes] = ua[rows_own, lanes] + u_pair
            ds_all = jnp.concatenate([ds_far, ds_near, ds_own], 1)
            dc = mm(ds_all, b_window)
            db[window, :] = db[window, :] + mm_tn(ds_all, c)
            u_total = ua[rows_own, :]
            received = dot(dy * (y_ref[rows, :] - skip_x * v), expand, 1, 1, FULL)
            d_step = dot(v * u_total, expand, 1, 1, FULL)
            gap = received - step * d_step
            d_decay = mm(triangle(False).astype(F32), gap) + later
            d_step = d_step - d_decay * rate
            d_raw = d_step * jax.nn.sigmoid(raw + heads[0:1])
            draw[rows, :] = d_raw
            dv = stepx[rows, :] * u_total + skip_x * dy
            dpre[rows, :width] = dv * (v_sig * (1.0 + v_pre * (1.0 - v_sig)))
            b_pre = pre_ref[rows, width : width + STATE]
            b_sig = jax.nn.sigmoid(b_pre)
            dpre[rows, width : width + STATE] = db[rows_own, :] * (b_sig * (1.0 + b_pre * (1.0 - b_sig)))
            dpre[rows, width + STATE :] = dc * (c_sig * (1.0 + c_pre * (1.0 - c_sig)))
            g_skip = g_skip + jnp.sum(dot(dy * v, expand, 1, 1, FULL), axis=0, keepdims=True)
            g_bias = g_bias + jnp.sum(d_raw, axis=0, keepdims=True)
            g_rate = g_rate + jnp.sum(d_decay * decay, axis=0, keepdims=True)
            return (later + jnp.sum(gap, axis=0, keepdims=True), g_bias, g_rate, g_skip)

        none = jnp.zeros((1, LANES), F32)
        _, g_bias, g_rate, g_skip = lax.fori_loop(0, chunks, chunk, (none, none, none, none))
        head_grad_ref[...] = jnp.concatenate([g_bias, g_rate, g_skip, jnp.zeros((5, LANES), F32)], 0)
        u = proj_ref[:, :channels]
        d = dpre[...]
        du = conv_ref[CONV - 1 : CONV, :] * d
        taps = [jnp.sum(d * u, axis=0, keepdims=True)]
        for back in range(1, CONV):
            masked = d * same_ref[:, back : back + 1]
            taps.insert(0, jnp.sum(masked * pltpu.roll(u, back, 0), axis=0, keepdims=True))
            du = du + conv_ref[CONV - 1 - back : CONV - back, :] * pltpu.roll(masked, length - back, 0)
        taps.append(jnp.sum(d, axis=0, keepdims=True))
        taps.append(jnp.zeros((8 - CONV - 1, channels), F32))
        conv_grad_ref[...] = jnp.concatenate(taps, 0)
        d_proj = jnp.concatenate([du, draw[...]], 1).astype(BF16)
        gin_ref[...] = dot(normed_ref[...], d_proj, 0, 0).astype(BF16)
        dn = dot(d_proj, w_ref[...], 1, 1) + dot(dgate_ref[...], wg_ref[...], 1, 1)
        dn_ref[...] = dn.astype(BF16)
        x = x_ref[...].astype(F32)
        norm_grad_ref[...] = jnp.broadcast_to(
            jnp.sum(dn * (x * rms_inverse(x)), axis=0, keepdims=True), (8, x.shape[1])
        )

    return body


def call(body, outs, scratch, *operands):
    vmem = pl.BlockSpec(memory_space=pltpu.VMEM)
    return pl.pallas_call(
        body,
        out_shape=[jax.ShapeDtypeStruct(shape, kind) for shape, kind in outs],
        in_specs=[vmem] * len(operands),
        out_specs=[vmem] * len(outs),
        scratch_shapes=[pltpu.VMEM(shape, F32) for shape in scratch],
        compiler_params=pltpu.CompilerParams(vmem_limit_bytes=50 * 2**20),
    )(*operands)


def slots(flat, rows):
    owners, count = flat.shape
    lanes = -(-count // rows)
    return jnp.pad(flat, ((0, 0), (0, lanes * rows - count))).reshape(owners * rows, lanes)


def on_device(
    hidden_in,
    segments,
    norm_gain,
    in_weight,
    conv_weight,
    conv_bias,
    step_bias,
    decay_log,
    skip_weight,
    gate_gain,
    out_weight,
    out_grad,
):
    row_count, piece, model = hidden_in.shape
    assert row_count == 1
    seq_n, dp_n = lax.axis_size("seq"), lax.axis_size("dp")
    owners = seq_n * dp_n
    place, dp_place = lax.axis_index("seq"), lax.axis_index("dp")
    length = piece * seq_n
    head_count = step_bias.shape[0]
    inner = head_count * HEAD_DIM
    heads_here = head_count // seq_n
    width = inner // seq_n
    channels = width + 2 * STATE
    cols = channels + LANES
    rows = in_weight.shape[0]
    conv_here = conv_bias.shape[0]
    gate_here = gate_gain.shape[0]

    conv_flat = jnp.concatenate([conv_weight.reshape(1, -1), conv_bias.reshape(1, -1)], 1)
    conv_slots = slots(conv_flat, rows)
    gate_slots = slots(gate_gain.reshape(1, -1), rows)
    conv_lanes, gate_lanes = conv_slots.shape[1], gate_slots.shape[1]
    rest = LANES - heads_here - 1 - conv_lanes - gate_lanes
    shared = [norm_gain[:, None], conv_slots, gate_slots, jnp.zeros((rows, rest), BF16)]
    both_states = in_weight[:, 2 * inner : 2 * inner + 2 * STATE]
    to_send = []
    for j in range(seq_n):
        first = 2 * inner + 2 * STATE + j * heads_here
        to_send.append(
            jnp.concatenate(
                [in_weight[:, inner + j * width : inner + (j + 1) * width], both_states]
                + [in_weight[:, first : first + heads_here]]
                + shared
                + [in_weight[:, j * width : (j + 1) * width]],
                axis=1,
            )
        )
    mine = jnp.concatenate(in_order(scatter_xor(jnp.stack(to_send), "seq"), place), 0)
    first_part, gate_part = mine[:, :cols], mine[:, cols:]
    w_first = jnp.concatenate(in_order(gather_dp(first_part), dp_place), 0)

    acts = in_order(gather_xor(jnp.stack([hidden_in[0], out_grad[0]]), "seq"), place)
    x_row = jnp.concatenate([a[0] for a in acts], 0)
    og_row = jnp.concatenate([a[1] for a in acts], 0)

    def linear(d, s):
        return d * seq_n + s

    to_heads = [(b, linear(b % dp_n, b // dp_n)) for b in range(owners)]
    out_block = lax.ppermute(out_weight, ("dp", "seq"), to_heads)
    out_rows = out_block.shape[0]
    folded = jnp.concatenate(
        [out_block[:, k * width : (k + 1) * width] for k in range(model // width)], 0
    )
    second = jnp.concatenate([gate_part, folded], 1)
    w_second = in_order(gather_dp(second), dp_place)
    w_gate = jnp.concatenate([p[:, :width] for p in w_second], 0)
    w_out = jnp.concatenate(
        [
            jnp.concatenate(
                [p[k * out_rows : (k + 1) * out_rows, width:] for k in range(model // width)], 1
            )
            for p in w_second
        ],
        0,
    )

    tail = w_first[:, channels:]
    at = heads_here + 1
    conv_all = tail[:, at : at + conv_lanes].reshape(owners, rows * conv_lanes)
    conv_all = conv_all[:, : (CONV + 1) * conv_here].reshape(owners, CONV + 1, conv_here)
    conv_all = conv_all.transpose(1, 0, 2).reshape(CONV + 1, owners * conv_here)
    conv_mine = jnp.concatenate(
        [
            lax.dynamic_slice_in_dim(conv_all[:, :inner], place * width, width, 1),
            conv_all[:, inner:],
        ],
        1,
    )
    conv_mine = jnp.pad(conv_mine.astype(F32), ((0, 8 - CONV - 1), (0, 0)))
    at = at + conv_lanes
    gain_all = tail[:, at : at + gate_lanes].reshape(owners, rows * gate_lanes)[:, :gate_here]
    gain_mine = lax.dynamic_slice_in_dim(gain_all.reshape(1, inner), place * width, width, 1)
    gain_mine = gain_mine.astype(F32)

    head_params = jnp.stack([step_bias, decay_log, skip_weight])
    head_params = lax.dynamic_slice_in_dim(head_params, place * heads_here, heads_here, 1)
    head_params = jnp.pad(head_params, ((0, 5), (0, LANES - heads_here)))
    row_segments = segments[0]
    same = [jnp.ones((length,), F32)]
    for back in range(1, CONV):
        matches = (row_segments[back:] == row_segments[:-back]).astype(F32)
        same.append(jnp.concatenate([jnp.zeros((back,), F32), matches]))
    same = jnp.pad(jnp.stack(same, 1), ((0, 0), (0, 8 - CONV)))
    segment_col = row_segments[:, None]
    padded = jnp.concatenate([jnp.full((2 * CHUNK,), -1, jnp.int32), row_segments])
    segment_rows = padded.reshape(-1, 1, CHUNK)

    chunks = length // CHUNK
    tall = length + 2 * CHUNK
    sources = [(tall, STATE), (length, width), (tall, width), (length + 8, width)]
    normed, proj, pre, y = call(
        forward_kernel(width, heads_here),
        [((length, model), BF16), ((length, cols), F32), ((length, channels), F32), ((length, width), F32)],
        sources,
        x_row, w_first, conv_mine, same, segment_col, segment_rows, head_params,
    )
    gate, d_gated, stats = call(
        gate_kernel(width),
        [((length, width), F32), ((length, width), F32), ((chunks, 8, LANES), F32)],
        [],
        normed, w_gate, og_row, w_out, y, gain_mine,
    )
    step = 1
    while step < seq_n:
        stats = stats + swap(stats, "seq", step)
        step *= 2
    out_part, g_out, g_gate, d_gate, dy, g_gain = call(
        out_kernel(width, inner),
        [((length, model), BF16), ((width, model), BF16), ((model, width), BF16)]
        + [((length, width), BF16), ((length, width), F32), ((8, width), F32)],
        [],
        stats, normed, gate, d_gated, y, gain_mine, og_row, w_out,
    )

    g_out = g_out.reshape(dp_n, out_rows, model)
    g_out = jnp.concatenate(
        [g_out[:, :, k * width : (k + 1) * width] for k in range(model // width)], 1
    )
    early = reduce_dp(jnp.concatenate([g_gate.reshape(dp_n, -1, width), g_out], 2))
    own_out = early[:, width:]
    own_out = jnp.concatenate(
        [own_out[k * out_rows : (k + 1) * out_rows] for k in range(model // width)], 1
    )
    back_pairs = [(target, source) for source, target in to_heads]
    grad_out_w = lax.ppermute(own_out, ("dp", "seq"), back_pairs)
    result = tree_sum(
        [p.astype(F32) for p in scatter_xor(out_part.reshape(seq_n, piece, model), "seq")]
    )
    result = hidden_in[0].astype(F32) + result

    g_in, dn, conv_grad, head_grad, norm_grad = call(
        backward_kernel(width, heads_here),
        [((model, cols), BF16), ((length, model), BF16), ((8, channels), F32)]
        + [((8, LANES), F32), ((8, model), F32)],
        sources
        + [(tall, width), (length, width), (length, LANES), (tall, width), (tall, STATE)]
        + [(length, channels), (length, LANES)],
        x_row, normed, w_first, w_gate, conv_mine, same, segment_col, segment_rows, head_params,
        proj, pre, y, dy, d_gate,
    )

    conv_full = jnp.zeros((CONV + 1, inner), F32)
    conv_full = lax.dynamic_update_slice_in_dim(
        conv_full, conv_grad[: CONV + 1, :width], place * width, 1
    )
    conv_full = jnp.concatenate([conv_full, conv_grad[: CONV + 1, width:]], 1)
    conv_full = conv_full.reshape(CONV + 1, owners, conv_here).transpose(1, 0, 2)
    gain_full = lax.dynamic_update_slice_in_dim(
        jnp.zeros((inner,), F32), g_gain[0], place * width, 0
    )
    heads_full = lax.dynamic_update_slice_in_dim(
        jnp.zeros((3, head_count), F32), head_grad[:3, :heads_here], place * heads_here, 1
    )
    small = jnp.concatenate(
        [
            norm_grad[0].reshape(owners, rows),
            conv_full.reshape(owners, -1),
            gain_full.reshape(owners, gate_here),
            jnp.broadcast_to(heads_full.reshape(1, -1), (owners, 3 * head_count)),
        ],
        1,
    )
    small_count = small.shape[1]
    small = slots(small, rows).astype(BF16)
    small_lanes = small.shape[1]
    tail_block = g_in[:, channels:] + jnp.pad(
        small, ((0, 0), (heads_here, LANES - heads_here - small_lanes))
    )
    late = jnp.concatenate([g_in[:, :channels], tail_block], 1).reshape(dp_n, -1, cols)
    late = reduce_dp(late)
    dn_parts = scatter_xor(dn.reshape(seq_n, piece, model), "seq")
    d_normed = tree_sum([p.astype(F32) for p in dn_parts])

    both = jnp.concatenate([late, early[:, :width]], 1).reshape(seq_n, rows, cols + width)
    parts = scatter_xor(both, "seq")
    ordered = in_order(parts, place)
    grad_in_w = jnp.concatenate(
        [b[:, cols:] for b in ordered]
        + [b[:, :width] for b in ordered]
        + [tree_sum([p[:, width:channels] for p in parts])]
        + [b[:, channels : channels + heads_here] for b in ordered],
        1,
    )
    first = channels + heads_here
    small = tree_sum([p[:, first : first + small_lanes] for p in parts])
    small = small.reshape(-1)[:small_count]
    at = rows
    grad_norm = small[:at]
    conv_own = small[at : at + (CONV + 1) * conv_here].reshape(CONV + 1, conv_here)
    at += (CONV + 1) * conv_here
    grad_gain = small[at : at + gate_here]
    at += gate_here
    head_own = small[at:].reshape(3, head_count)

    widened = hidden_in[0].astype(F32)
    inverse = lax.rsqrt(jnp.mean(widened * widened, axis=-1, keepdims=True) + EPSILON)
    gain_full_row = tail[:, heads_here].astype(F32)[None, :]
    scaled = d_normed * gain_full_row
    along = jnp.mean(scaled * widened, axis=-1, keepdims=True)
    grad_hidden = out_grad[0].astype(F32) + inverse * (scaled - widened * (inverse * inverse * along))
    return (
        result[None],
        grad_hidden[None],
        grad_norm,
        grad_in_w,
        conv_own[:CONV],
        conv_own[CONV],
        head_own[0],
        head_own[1],
        head_own[2],
        grad_gain,
        grad_out_w,
    )


def solution(mesh):
    in_specs = (
        P("dp", "seq", None),
        P("dp", None),
        P(("dp", "seq")),
        P(("dp", "seq"), None),
        P(None, ("dp", "seq")),
        P(("dp", "seq")),
        P(),
        P(),
        P(),
        P(("dp", "seq")),
        P(("dp", "seq"), None),
        P("dp", "seq", None),
    )
    out_specs = (
        P("dp", "seq", None),
        P("dp", "seq", None),
        P(("dp", "seq")),
        P(("dp", "seq"), None),
        P(None, ("dp", "seq")),
        P(("dp", "seq")),
        P(),
        P(),
        P(),
        P(("dp", "seq")),
        P(("dp", "seq"), None),
    )
    return jax.shard_map(
        on_device, mesh=mesh, in_specs=in_specs, out_specs=out_specs, check_vma=False
    )
```

```python
import jax
import jax.numpy as jnp
from jax import lax
from jax.experimental import pallas as pl
from jax.experimental.pallas import tpu as pltpu
from jax.sharding import PartitionSpec as P

HEAD_DIM = 64
STATE = 128
CONV = 4
CHUNK = 128
VMEM_LIMIT = 56 * 2**20
LANES = 128
EPSILON = 1e-05
FULL = lax.Precision.HIGHEST
MOST = lax.Precision.HIGH
F32 = jnp.float32
BF16 = jnp.bfloat16


def swap(x, axis, offset):
    count = lax.axis_size(axis)
    return lax.ppermute(x, axis, [(i, i ^ offset) for i in range(count)])


def tree_sum(parts):
    while len(parts) > 1:
        parts = [parts[i] + parts[i + 1] for i in range(0, len(parts), 2)]
    return parts[0]


def in_order(pieces, place):
    stacked = jnp.stack(pieces)
    return [lax.dynamic_index_in_dim(stacked, j ^ place, 0, False) for j in range(len(pieces))]


def gather_xor(x, axis):
    return [x] + [swap(x, axis, k) for k in range(1, lax.axis_size(axis))]


def scatter_xor(blocks, axis):
    place = lax.axis_index(axis)
    return [
        swap(lax.dynamic_index_in_dim(blocks, place ^ k, 0, False), axis, k)
        if k
        else lax.dynamic_index_in_dim(blocks, place, 0, False)
        for k in range(lax.axis_size(axis))
    ]


def inner_of(count):
    inner = 1
    while 2 * inner * inner < count:
        inner *= 2
    return inner


def far_offsets():
    count = lax.axis_size("dp")
    inner = inner_of(count)
    return [k * inner for k in range(1, count // inner)]


def gather_far(x):
    return [x] + [swap(x, "dp", k) for k in far_offsets()]


def gather_near(far):
    inner = inner_of(lax.axis_size("dp"))
    near = [[piece] + [swap(piece, "dp", j) for j in range(1, inner)] for piece in far]
    return [piece for group in near for piece in group]


def reduce_near(grads):
    count = lax.axis_size("dp")
    inner = inner_of(count)
    inner_place = lax.axis_index("dp") % inner
    shaped = grads.reshape(count // inner, inner, *grads.shape[1:])
    parts = []
    for j in range(inner):
        slab = lax.dynamic_index_in_dim(shaped, inner_place ^ j, 1, False)
        parts.append(swap(slab, "dp", j) if j else slab)
    return tree_sum([p.astype(F32) for p in parts]).astype(BF16)


def reduce_far(near):
    outer_place = lax.axis_index("dp") // inner_of(lax.axis_size("dp"))
    parts = [lax.dynamic_index_in_dim(near, outer_place, 0, False)]
    for k, offset in enumerate(far_offsets()):
        slab = lax.dynamic_index_in_dim(near, outer_place ^ (k + 1), 0, False)
        parts.append(swap(slab, "dp", offset))
    return tree_sum([p.astype(F32) for p in parts])


def dot(a, b, ca, cb, precision=None):
    return lax.dot_general(
        a, b, (((ca,), (cb,)), ((), ())), precision=precision, preferred_element_type=F32
    )


def exact(a, b):
    return dot(a, b, 1, 0, FULL)


def mm(a, b):
    return dot(a, b, 1, 0, MOST)


def mm_nt(a, b):
    return dot(a, b, 1, 1, MOST)


def mm_tn(a, b):
    return dot(a, b, 0, 0, MOST)


def softplus(x):
    small = jnp.exp(-jnp.abs(x))
    up = 1.0 + small
    down = up - 1.0
    log1p = jnp.where(down == 0.0, small, jnp.log(up) * (small / jnp.where(down == 0.0, 1.0, down)))
    return jnp.maximum(x, 0.0) + log1p


def expand_matrix(width):
    head = lax.broadcasted_iota(jnp.int32, (LANES, width), 0)
    column = lax.broadcasted_iota(jnp.int32, (LANES, width), 1)
    return (column // HEAD_DIM == head).astype(F32)


def triangle(lower):
    row = lax.broadcasted_iota(jnp.int32, (CHUNK, CHUNK), 0)
    column = lax.broadcasted_iota(jnp.int32, (CHUNK, CHUNK), 1)
    return row >= column if lower else row <= column


def head_rows(bias_ref, decay_ref, skip_ref, heads_here):
    rows = jnp.concatenate([bias_ref[...], decay_ref[...], skip_ref[...]], 0)
    count = rows.shape[1]
    rows = jnp.concatenate([rows, jnp.zeros((3, LANES - count), F32)], 1)
    rows = jnp.concatenate([rows, jnp.zeros((5, LANES), F32)], 0)
    place = lax.axis_index("seq")
    mine = rows
    for j in range(1, count // heads_here):
        moved = jnp.concatenate([rows[:, j * heads_here :], rows[:, : j * heads_here]], 1)
        mine = jnp.where(place == j, moved, mine)
    return mine


def spread_segments(seg_ref, seg_col, seg_row):
    seg_row[:, : 2 * CHUNK] = jnp.full((8, 2 * CHUNK), -1.0, F32)
    for i in range(seg_ref.shape[1] // CHUNK):
        now = seg_ref[:, i * CHUNK : (i + 1) * CHUNK].astype(F32)
        seg_row[:, (i + 2) * CHUNK : (i + 3) * CHUNK] = jnp.broadcast_to(now, (8, CHUNK))
        seg_col[i * CHUNK : (i + 1) * CHUNK, :] = jnp.broadcast_to(now, (CHUNK, CHUNK)).T


def same_segment(seg_col, back, width):
    now = seg_col[...]
    row = lax.broadcasted_iota(jnp.int32, now.shape, 0)
    same = ((now == pltpu.roll(now, back, 0)) & (row >= back)).astype(F32)
    return jnp.concatenate([same] * (width // LANES), 1)


def masks_of(seg_col, seg_row, i):
    column = seg_col[pl.ds(pl.multiple_of(i * CHUNK, CHUNK), CHUNK), :]

    def row(j):
        return seg_row[:, pl.ds(pl.multiple_of((i + j) * CHUNK, CHUNK), CHUNK)][:1]

    far = (column == row(0)).astype(F32)
    near = (column == row(1)).astype(F32)
    own = (column == row(2)) & triangle(True)
    return far, near, own


def lane_halves():
    lane = lax.broadcasted_iota(jnp.int32, (1, LANES), 1)
    low = (lane < HEAD_DIM).astype(F32)
    return low, 1.0 - low


def rms_inverse(x):
    return lax.rsqrt(jnp.mean(x * x, axis=-1, keepdims=True) + EPSILON)


def gain_row(weights, lane_of_gain):
    tail = weights[:, weights.shape[1] - LANES :]
    pick = (lax.broadcasted_iota(jnp.int32, (8, LANES), 1) == lane_of_gain).astype(BF16)
    return dot(pick, tail, 1, 1)[:1]


def decays(raw, heads):
    step = softplus(raw + heads[0:1])
    return step, step * (-jnp.exp(heads[1:2]))


def fill_sources(i, v, step, decay, expand, vd, vt, ecx):
    cumulative = exact(triangle(True).astype(F32), decay)
    step_x = exact(step, expand)
    cum_x = exact(cumulative, expand)
    last = cum_x[CHUNK - 1 :]
    vd_now = v * step_x
    vd[pl.ds(i * CHUNK, CHUNK), :] = vd_now
    vt[pl.ds((i + 2) * CHUNK, CHUNK), :] = vd_now * jnp.exp(last - cum_x)
    ecx[pl.ds(i * CHUNK + 8, CHUNK), :] = jnp.exp(cum_x)
    return cumulative, step_x, cum_x, last


def head_decay(cumulative, cumulative_t, own, h):
    gap = cumulative[:, h : h + 1] - cumulative_t[h : h + 1, :]
    return jnp.exp(jnp.where(own, gap, -1e30))


def put_in_order(pieces, place, target, source=None, lanes=None):
    for m, piece in enumerate(pieces):
        source_rows = slice(0, piece.shape[0]) if source is None else source
        rows = source_rows.stop - source_rows.start
        start = pl.multiple_of((place ^ m) * rows, rows)
        if lanes is None:
            target[pl.ds(start, rows), :] = piece[...]
        else:
            target[pl.ds(start, rows), lanes[0]] = piece[source_rows, lanes[1]]


def dp_index(pieces):
    return lax.axis_index("dp") if len(pieces) > 1 else 0


def put_second(pieces, place, wg_ref=None, wo_ref=None):
    rows, both = pieces[0].shape
    width = both // 2
    if wg_ref is not None:
        put_in_order(pieces, place, wg_ref, slice(0, rows), (slice(0, width), slice(0, width)))
    if wo_ref is not None:
        folds = wo_ref.shape[1] // width
        part = rows // folds
        for k in range(folds):
            to = (slice(k * width, (k + 1) * width), slice(width, 2 * width))
            put_in_order(pieces, place, wo_ref, slice(k * part, (k + 1) * part), to)


def small_spots(rows, lengths):
    group = min(rows, len(lengths))
    return [(i % group, (i // group) * max(lengths)) for i in range(len(lengths))]


def pack_kernel(width, inner, heads_here, count):
    def body(w_ref, taps_ref, shift_ref, gate_ref, norm_ref, *refs):
        outs, blocks = refs[:-1], refs[-1]
        rows = w_ref.shape[0]
        stride = blocks.shape[0] // count
        states = 2 * inner + 2 * STATE
        norm = jnp.concatenate([norm_ref[...].astype(F32), jnp.zeros((1, LANES - rows), F32)], 1)
        column = jnp.broadcast_to(norm, (LANES, LANES)).T[:rows]
        taps = taps_ref[...].astype(F32)
        vectors = [taps[i : i + 1] for i in range(CONV)]
        vectors += [shift_ref[...].astype(F32), gate_ref[...].astype(F32)]
        spots = small_spots(rows, [v.shape[1] for v in vectors])
        lane = lax.broadcasted_iota(jnp.int32, (rows, LANES), 1)
        row = lax.broadcasted_iota(jnp.int32, (rows, LANES), 0)
        shared = jnp.where(lane == heads_here, column, 0.0)
        for vector, (at_row, at_lane) in zip(vectors, spots):
            start = heads_here + 1 + at_lane
            pieces = [jnp.zeros((1, start), F32), vector]
            pieces.append(jnp.zeros((1, LANES - start - vector.shape[1]), F32))
            shared = shared + jnp.where(row == at_row, jnp.concatenate(pieces, 1), 0.0)
        for j in range(count):
            at = slice(j * stride, j * stride + rows)
            first = states + j * heads_here
            blocks[at, :width] = w_ref[:, inner + j * width : inner + (j + 1) * width].astype(F32)
            blocks[at, width : width + 2 * STATE] = w_ref[:, 2 * inner : states].astype(F32)
            steps = w_ref[:, first : first + heads_here].astype(F32)
            tail = jnp.concatenate([steps, shared[:, heads_here:]], 1)
            blocks[at, width + 2 * STATE : width + 2 * STATE + LANES] = tail
            gate = w_ref[:, j * width : (j + 1) * width].astype(F32)
            blocks[at, width + 2 * STATE + LANES :] = gate
        for k in range(count):
            start = pl.multiple_of((lax.axis_index("seq") ^ k) * stride, stride)
            outs[k][...] = blocks[pl.ds(start, rows), :].astype(BF16)

    return body


def forward_kernel(width, lane_of_gain, x_count, w_count):
    heads_here = width // HEAD_DIM

    def body(*refs):
        x_pieces, refs = refs[:x_count], refs[x_count:]
        w_pieces, refs = refs[:w_count], refs[w_count:]
        conv_ref, seg_ref, bias_ref, decay_ref, skip_ref, normed_ref, proj_ref, pre_ref, y_ref, bpad, vd, vt, ecx, seg_col, seg_row, x_ref, w_ref = refs
        put_in_order(x_pieces, lax.axis_index("seq"), x_ref)
        put_in_order(w_pieces, dp_index(w_pieces), w_ref)
        x = x_ref[...].astype(F32)
        gain = gain_row(w_ref[...], lane_of_gain)
        normed_ref[...] = (x * rms_inverse(x) * gain).astype(BF16)
        proj_ref[...] = dot(normed_ref[...], w_ref[...], 1, 0)
        spread_segments(seg_ref, seg_col, seg_row)
        channels = width + 2 * STATE
        u = proj_ref[:, :channels]
        running = conv_ref[CONV : CONV + 1, :] + conv_ref[CONV - 1 : CONV, :] * u
        for back in range(1, CONV):
            tap = conv_ref[CONV - 1 - back : CONV - back, :]
            running = running + tap * pltpu.roll(u, back, 0) * same_segment(seg_col, back, channels)
        pre_ref[...] = running
        bpad[pl.ds(0, 2 * CHUNK), :] = jnp.zeros((2 * CHUNK, STATE), F32)
        vt[pl.ds(0, 2 * CHUNK), :] = jnp.zeros((2 * CHUNK, width), F32)
        ecx[pl.ds(0, 8), :] = jnp.zeros((8, width), F32)
        b_pre = running[:, width : width + STATE]
        bpad[pl.ds(2 * CHUNK, x.shape[0]), :] = b_pre * jax.nn.sigmoid(b_pre)
        expand = expand_matrix(width)
        low, high = lane_halves()
        heads = head_rows(bias_ref, decay_ref, skip_ref, heads_here)
        skip_x = exact(jnp.broadcast_to(heads[2:3], (8, LANES)), expand)[:1]

        def chunk(i, carry):
            rows = pl.ds(pl.multiple_of(i * CHUNK, CHUNK), CHUNK)
            v_pre = pre_ref[rows, :width]
            c_pre = pre_ref[rows, width + STATE :]
            v = v_pre * jax.nn.sigmoid(v_pre)
            c = c_pre * jax.nn.sigmoid(c_pre)
            step, decay = decays(proj_ref[rows, channels:], heads)
            cumulative, _, _, _ = fill_sources(i, v, step, decay, expand, vd, vt, ecx)
            cumulative_t = cumulative.T
            far, near, own = masks_of(seg_col, seg_row, i)
            window = pl.ds(pl.multiple_of(i * CHUNK, CHUNK), 3 * CHUNK)
            scores = mm_nt(c, bpad[window, :])
            s_far = scores[:, :CHUNK] * far
            s_near = scores[:, CHUNK : 2 * CHUNK] * near
            s_own = scores[:, 2 * CHUNK :]
            ecx_now = ecx[pl.ds(pl.multiple_of(i * CHUNK, 8) + 8, CHUNK), :]
            last_before = ecx[pl.ds(pl.multiple_of(i * CHUNK, 8), 8), :][7:8]
            vt_far = vt[rows, :] * last_before
            vt_near = vt[pl.ds(pl.multiple_of((i + 1) * CHUNK, CHUNK), CHUNK), :]
            off = mm(s_far, vt_far) + mm(s_near, vt_near)
            y_ref[rows, :] = off * ecx_now + skip_x * v
            for pair in range(heads_here // 2):
                lanes = slice(pair * LANES, (pair + 1) * LANES)
                n0 = s_own * head_decay(cumulative, cumulative_t, own, 2 * pair)
                n1 = s_own * head_decay(cumulative, cumulative_t, own, 2 * pair + 1)
                vp = vd[rows, lanes]
                both = mm(jnp.concatenate([n0, n1], 1), jnp.concatenate([vp * low, vp * high], 0))
                y_ref[rows, lanes] = y_ref[rows, lanes] + both
            return carry

        lax.fori_loop(0, x.shape[0] // CHUNK, chunk, 0)

    return body


def gate_kernel(og_count, w_count):
    def body(*refs):
        og_pieces, refs = refs[:og_count], refs[og_count:]
        w_pieces, refs = refs[:w_count], refs[w_count:]
        normed_ref, y_ref, gain_ref, gate_ref, dg_ref, stats_ref, og_ref, wg_ref, wo_ref = refs
        put_in_order(og_pieces, lax.axis_index("seq"), og_ref)
        put_second(w_pieces, dp_index(w_pieces), wg_ref, wo_ref)
        gate = dot(normed_ref[...], wg_ref[...], 1, 0)
        gate_ref[...] = gate
        d_gated = dot(og_ref[...], wo_ref[...], 1, 1)
        dg_ref[...] = d_gated
        v = y_ref[...] * (gate * jax.nn.sigmoid(gate))
        squares = jnp.sum(v * v, axis=1, keepdims=True)
        cross = jnp.sum(v * (d_gated * gain_ref[...]), axis=1, keepdims=True)
        lane = lax.broadcasted_iota(jnp.int32, (CHUNK, LANES), 1)
        for i in range(stats_ref.shape[0]):
            rows = slice(i * CHUNK, (i + 1) * CHUNK)
            both = jnp.where(lane == 0, squares[rows], jnp.where(lane == 1, cross[rows], 0.0))
            stats_ref[i] = both.T[:8]

    return body


def out_kernel(width, whole_width, og_count, w_count):
    def body(*refs):
        og_pieces, refs = refs[:og_count], refs[og_count:]
        w_pieces, refs = refs[:w_count], refs[w_count:]
        stats, refs = refs[:og_count], refs[og_count:]
        normed_ref, gate_ref, dg_ref, y_ref, gain_ref, out_ref, gout_ref, ggate_ref, dgate_ref, dy_ref, ggain_ref, og_ref, wo_ref = refs
        put_in_order(og_pieces, lax.axis_index("seq"), og_ref)
        put_second(w_pieces, dp_index(w_pieces), None, wo_ref)
        columns = []
        for i in range(stats[0].shape[0]):
            total = tree_sum([part[i] for part in stats])
            square = jnp.concatenate([total, jnp.zeros((CHUNK - 8, LANES), F32)], 0)
            columns.append(square.T)
        columns = jnp.concatenate(columns, 0)
        inverse = lax.rsqrt(columns[:, 0:1] / whole_width + EPSILON)
        cross = columns[:, 1:2] / whole_width
        gate = gate_ref[...]
        sig = jax.nn.sigmoid(gate)
        silu = gate * sig
        y = y_ref[...]
        v = y * silu
        gain = gain_ref[...]
        scaled = v * inverse
        gated = (scaled * gain).astype(BF16)
        out_ref[...] = dot(gated, wo_ref[...], 1, 0).astype(BF16)
        gout_ref[...] = dot(gated, og_ref[...], 0, 0).astype(BF16)
        d_gated = dg_ref[...]
        ggain_ref[...] = jnp.broadcast_to(jnp.sum(d_gated * scaled, axis=0, keepdims=True), (8, width))
        dv = inverse * (d_gated * gain - v * (inverse * inverse * cross))
        dy_ref[...] = dv * silu
        dgate = (dv * y * (sig * (1.0 + gate * (1.0 - sig)))).astype(BF16)
        dgate_ref[...] = dgate
        ggate_ref[...] = dot(normed_ref[...], dgate, 0, 0).astype(BF16)

    return body


def mixer_back_kernel(width):
    heads_here = width // HEAD_DIM

    def body(conv_ref, seg_ref, bias_ref, decay_ref, skip_ref, proj_ref, pre_ref, y_ref, dy_ref, dconv_ref, draw, conv_grad_ref, head_grad_ref, bpad, vd, vt, ecx, seg_col, seg_row, tailx, stepx, cums, ua, db, dpre):
        length = proj_ref.shape[0]
        spread_segments(seg_ref, seg_col, seg_row)
        chunks = length // CHUNK
        channels = width + 2 * STATE
        expand = expand_matrix(width)
        low, high = lane_halves()
        heads = head_rows(bias_ref, decay_ref, skip_ref, heads_here)
        rate = jnp.exp(heads[1:2])
        skip_x = exact(jnp.broadcast_to(heads[2:3], (8, LANES)), expand)[:1]
        bpad[pl.ds(0, 2 * CHUNK), :] = jnp.zeros((2 * CHUNK, STATE), F32)
        vt[pl.ds(0, 2 * CHUNK), :] = jnp.zeros((2 * CHUNK, width), F32)
        tailx[pl.ds(0, 2 * CHUNK), :] = jnp.zeros((2 * CHUNK, width), F32)
        ecx[pl.ds(0, 8), :] = jnp.zeros((8, width), F32)
        b_pre = pre_ref[:, width : width + STATE]
        bpad[pl.ds(2 * CHUNK, length), :] = b_pre * jax.nn.sigmoid(b_pre)
        ua[...] = jnp.zeros(ua.shape, F32)
        db[...] = jnp.zeros(db.shape, F32)

        def prepare(i, carry):
            rows = pl.ds(pl.multiple_of(i * CHUNK, CHUNK), CHUNK)
            v_pre = pre_ref[rows, :width]
            v = v_pre * jax.nn.sigmoid(v_pre)
            step, decay = decays(proj_ref[rows, channels:], heads)
            cumulative, step_x, cum_x, last = fill_sources(i, v, step, decay, expand, vd, vt, ecx)
            cums[rows, :] = cumulative
            stepx[rows, :] = step_x
            tailx[pl.ds(pl.multiple_of((i + 2) * CHUNK, CHUNK), CHUNK), :] = jnp.exp(last - cum_x)
            return carry

        lax.fori_loop(0, chunks, prepare, 0)

        def chunk(turn, carry):
            later, g_bias, g_rate, g_skip = carry
            i = chunks - 1 - turn
            rows = pl.ds(pl.multiple_of(i * CHUNK, CHUNK), CHUNK)
            rows_near = pl.ds(pl.multiple_of((i + 1) * CHUNK, CHUNK), CHUNK)
            rows_own = pl.ds(pl.multiple_of((i + 2) * CHUNK, CHUNK), CHUNK)
            window = pl.ds(pl.multiple_of(i * CHUNK, CHUNK), 3 * CHUNK)
            v_pre = pre_ref[rows, :width]
            v_sig = jax.nn.sigmoid(v_pre)
            v = v_pre * v_sig
            c_pre = pre_ref[rows, width + STATE :]
            c_sig = jax.nn.sigmoid(c_pre)
            c = c_pre * c_sig
            raw = proj_ref[rows, channels:]
            step, decay = decays(raw, heads)
            cumulative = cums[rows, :]
            cumulative_t = cumulative.T
            far, near, own = masks_of(seg_col, seg_row, i)
            b_window = bpad[window, :]
            scores = mm_nt(c, b_window)
            s_far = scores[:, :CHUNK] * far
            s_near = scores[:, CHUNK : 2 * CHUNK] * near
            s_own = scores[:, 2 * CHUNK :]
            dy = dy_ref[rows, :]
            dye = dy * ecx[pl.ds(pl.multiple_of(i * CHUNK, 8) + 8, CHUNK), :]
            dye_far = dye * ecx[pl.ds(pl.multiple_of(i * CHUNK, 8), 8), :][7:8]
            ds_far = mm_nt(dye_far, vt[rows, :]) * far
            ds_near = mm_nt(dye, vt[rows_near, :]) * near
            ua[rows, :] = ua[rows, :] + tailx[rows, :] * mm_tn(s_far, dye_far)
            ua[rows_near, :] = ua[rows_near, :] + tailx[rows_near, :] * mm_tn(s_near, dye)
            ds_own = jnp.zeros((CHUNK, CHUNK), F32)
            for pair in range(heads_here // 2):
                lanes = slice(pair * LANES, (pair + 1) * LANES)
                d0 = head_decay(cumulative, cumulative_t, own, 2 * pair)
                d1 = head_decay(cumulative, cumulative_t, own, 2 * pair + 1)
                dyp = dy_ref[rows, lanes]
                split = jnp.concatenate([dyp * low, dyp * high], 0)
                dm = mm_nt(split, vd[rows, lanes])
                ds_own = ds_own + dm[:CHUNK] * d0 + dm[CHUNK:] * d1
                u_pair = mm_tn(jnp.concatenate([s_own * d0, s_own * d1], 0), split)
                ua[rows_own, lanes] = ua[rows_own, lanes] + u_pair
            ds_all = jnp.concatenate([ds_far, ds_near, ds_own], 1)
            dc = mm(ds_all, b_window)
            db[window, :] = db[window, :] + mm_tn(ds_all, c)
            u_total = ua[rows_own, :]
            received = dot(dy * (y_ref[rows, :] - skip_x * v), expand, 1, 1, FULL)
            d_step = dot(v * u_total, expand, 1, 1, FULL)
            gap = received - step * d_step
            d_decay = exact(triangle(False).astype(F32), gap) + later
            d_step = d_step - d_decay * rate
            d_raw = d_step * jax.nn.sigmoid(raw + heads[0:1])
            draw[rows, :] = d_raw.astype(BF16)
            dv = stepx[rows, :] * u_total + skip_x * dy
            dpre[rows, :width] = dv * (v_sig * (1.0 + v_pre * (1.0 - v_sig)))
            b_pre = pre_ref[rows, width : width + STATE]
            b_sig = jax.nn.sigmoid(b_pre)
            dpre[rows, width : width + STATE] = db[rows_own, :] * (b_sig * (1.0 + b_pre * (1.0 - b_sig)))
            dpre[rows, width + STATE :] = dc * (c_sig * (1.0 + c_pre * (1.0 - c_sig)))
            g_skip = g_skip + jnp.sum(dot(dy * v, expand, 1, 1, FULL), axis=0, keepdims=True)
            g_bias = g_bias + jnp.sum(d_raw, axis=0, keepdims=True)
            g_rate = g_rate + jnp.sum(d_decay * decay, axis=0, keepdims=True)
            return (later + jnp.sum(gap, axis=0, keepdims=True), g_bias, g_rate, g_skip)

        none = jnp.zeros((1, LANES), F32)
        _, g_bias, g_rate, g_skip = lax.fori_loop(0, chunks, chunk, (none, none, none, none))
        head_grad_ref[...] = jnp.concatenate([g_bias, g_rate, g_skip, jnp.zeros((5, LANES), F32)], 0)
        u = proj_ref[:, :channels]
        d = dpre[...]
        du = conv_ref[CONV - 1 : CONV, :] * d
        taps = [jnp.sum(d * u, axis=0, keepdims=True)]
        for back in range(1, CONV):
            masked = d * same_segment(seg_col, back, channels)
            taps.insert(0, jnp.sum(masked * pltpu.roll(u, back, 0), axis=0, keepdims=True))
            du = du + conv_ref[CONV - 1 - back : CONV - back, :] * pltpu.roll(masked, length - back, 0)
        taps.append(jnp.sum(d, axis=0, keepdims=True))
        taps.append(jnp.zeros((8 - CONV - 1, channels), F32))
        conv_grad_ref[...] = jnp.concatenate(taps, 0)
        dconv_ref[...] = du.astype(BF16)

    return body


def weight_back_kernel(x_count, w_count):
    def body(*refs):
        x_pieces, refs = refs[:x_count], refs[x_count:]
        w_pieces, refs = refs[:w_count], refs[w_count:]
        g_pieces, refs = refs[:w_count], refs[w_count:]
        normed_ref, dconv_ref, draw_ref, dgate_ref, gin_ref, dn_ref, norm_grad_ref, x_ref, w_ref, wg_ref = refs
        put_in_order(x_pieces, lax.axis_index("seq"), x_ref)
        put_in_order(w_pieces, dp_index(w_pieces), w_ref)
        put_second(g_pieces, dp_index(w_pieces), wg_ref)
        channels = dconv_ref.shape[1]
        dconv, draw = dconv_ref[...], draw_ref[...]
        dn = dot(dconv, w_ref[:, :channels], 1, 1) + dot(draw, w_ref[:, channels:], 1, 1)
        dn = dn + dot(dgate_ref[...], wg_ref[...], 1, 1)
        dn_ref[...] = dn.astype(BF16)
        gin_ref[:, :channels] = dot(normed_ref[...], dconv, 0, 0).astype(BF16)
        x = x_ref[...].astype(F32)
        along = jnp.sum(dn * (x * rms_inverse(x)), axis=0, keepdims=True)
        norm_grad_ref[...] = along
        gin_ref[:, channels:] = dot(normed_ref[...], draw, 0, 0).astype(BF16)

    return body


def call(body, outs, scratch, *operands):
    vmem = pl.BlockSpec(memory_space=pltpu.VMEM)
    return pl.pallas_call(
        body,
        out_shape=[jax.ShapeDtypeStruct(shape, kind) for shape, kind in outs],
        in_specs=[vmem] * len(operands),
        out_specs=[vmem] * len(outs),
        scratch_shapes=[
            pltpu.VMEM(*shape) if isinstance(shape[0], tuple) else pltpu.VMEM(shape, F32)
            for shape in scratch
        ],
        compiler_params=pltpu.CompilerParams(vmem_limit_bytes=VMEM_LIMIT),
    )(*operands)


def slots(flat, rows):
    owners, count = flat.shape
    lanes = -(-count // rows)
    return jnp.pad(flat, ((0, 0), (0, lanes * rows - count))).reshape(owners * rows, lanes)


def on_device(
    hidden_in,
    segments,
    norm_gain,
    in_weight,
    conv_weight,
    conv_bias,
    step_bias,
    decay_log,
    skip_weight,
    gate_gain,
    out_weight,
    out_grad,
):
    row_count, piece, model = hidden_in.shape
    assert row_count == 1
    seq_n, dp_n = lax.axis_size("seq"), lax.axis_size("dp")
    owners = seq_n * dp_n
    place, dp_place = lax.axis_index("seq"), lax.axis_index("dp")
    length = piece * seq_n
    head_count = step_bias.shape[0]
    inner = head_count * HEAD_DIM
    heads_here = head_count // seq_n
    width = inner // seq_n
    channels = width + 2 * STATE
    cols = channels + LANES
    rows = in_weight.shape[0]
    conv_here = conv_bias.shape[0]
    gate_here = gate_gain.shape[0]

    stride = -(-rows // 16) * 16
    blocks = call(
        pack_kernel(width, inner, heads_here, seq_n),
        [((rows, cols + width), BF16)] * seq_n,
        [(seq_n * stride, cols + width)],
        in_weight, conv_weight, conv_bias[None], gate_gain[None], norm_gain[None],
    )
    blocks = [b if k == 0 else swap(b, "seq", k) for k, b in enumerate(blocks)]
    mine = jnp.concatenate(in_order(blocks, place), 0)
    first_part, gate_part = mine[:, :cols], mine[:, cols:]
    far_first = gather_far(first_part)
    x_pieces = gather_xor(hidden_in[0], "seq")
    og_pieces = gather_xor(out_grad[0], "seq")

    def linear(d, s):
        return d * seq_n + s

    to_heads = [(b, linear(b % dp_n, b // dp_n)) for b in range(owners)]
    out_block = lax.ppermute(out_weight, ("dp", "seq"), to_heads)
    out_rows = out_block.shape[0]
    folded = jnp.concatenate(
        [out_block[:, k * width : (k + 1) * width] for k in range(model // width)], 0
    )
    second = jnp.concatenate([gate_part, folded], 1)
    far_second = gather_far(second)
    w_first = gather_near(far_first)
    w_second = gather_near(far_second)
    split_here = not out_rows % 16
    if not split_here:
        w_first = [jnp.concatenate(in_order(w_first, dp_place), 0)]
        w_second = in_order(w_second, dp_place)
        folds = [slice(k * out_rows, (k + 1) * out_rows) for k in range(model // width)]
        w_out = jnp.concatenate([p[f, width:] for f in folds for p in w_second], 0)
        w_second = [
            jnp.concatenate([jnp.concatenate([p[:, :width] for p in w_second], 0), w_out], 1)
        ]
    if len(w_first) > 1:
        tail = jnp.concatenate(in_order([p[:, channels:] for p in w_first], dp_place), 0)
    else:
        tail = w_first[0][:, channels:]
    tail = tail.reshape(owners, rows, LANES)
    lengths = [conv_here] * (CONV + 1) + [gate_here]
    spots = small_spots(rows, lengths)
    if rows >= len(lengths):
        conv_all = tail[:, : CONV + 1, heads_here + 1 : heads_here + 1 + conv_here]
        conv_all = conv_all.transpose(1, 0, 2).reshape(CONV + 1, owners * conv_here)
    else:
        conv_all = []
        for r, lane in spots[: CONV + 1]:
            first = heads_here + 1 + lane
            conv_all.append(tail[:, r, first : first + conv_here].reshape(1, -1))
        conv_all = jnp.concatenate(conv_all, 0)
    conv_mine = jnp.concatenate(
        [
            lax.dynamic_slice_in_dim(conv_all[:, :inner], place * width, width, 1),
            conv_all[:, inner:],
        ],
        1,
    )
    conv_mine = jnp.pad(conv_mine.astype(F32), ((0, 8 - CONV - 1), (0, 0)))
    first = heads_here + 1 + spots[-1][1]
    gain_all = tail[:, spots[-1][0], first : first + gate_here]
    gain_mine = lax.dynamic_slice_in_dim(gain_all.reshape(1, inner), place * width, width, 1)
    gain_mine = gain_mine.astype(F32)

    head_params = (step_bias[None], decay_log[None], skip_weight[None])

    chunks = length // CHUNK
    tall = length + 2 * CHUNK
    sources = [(tall, STATE), (length, width), (tall, width), (length + 8, width)]
    sources += [(length, LANES), (8, tall)]
    normed, proj, pre, y = call(
        forward_kernel(width, heads_here, len(x_pieces), len(w_first)),
        [((length, model), BF16)]
        + [((length, cols), F32), ((length, channels), F32), ((length, width), F32)],
        sources + [((length, model), BF16), ((model, cols), BF16)],
        *x_pieces, *w_first, conv_mine, segments, *head_params,
    )
    og_scratch, wg_scratch = ((length, model), BF16), ((model, width), BF16)
    wo_scratch = ((width, model), BF16)
    gate, d_gated, stats = call(
        gate_kernel(len(og_pieces), len(w_second)),
        [((length, width), F32), ((length, width), F32), ((chunks, 8, LANES), F32)],
        [og_scratch, wg_scratch, wo_scratch],
        *og_pieces, *w_second, normed, y, gain_mine,
    )
    stats = gather_xor(stats, "seq")
    out_part, g_out, g_gate, d_gate, dy, g_gain = call(
        out_kernel(width, inner, len(og_pieces), len(w_second)),
        [((length, model), BF16), ((width, model), BF16), ((model, width), BF16)]
        + [((length, width), BF16), ((length, width), F32), ((8, width), F32)],
        [og_scratch, wo_scratch],
        *og_pieces, *w_second, *stats, normed, gate, d_gated, y, gain_mine,
    )

    g_out = g_out.reshape(dp_n, out_rows, model)
    g_out = jnp.concatenate(
        [g_out[:, :, k * width : (k + 1) * width] for k in range(model // width)], 1
    )
    near_early = jnp.concatenate([g_gate.reshape(dp_n, -1, width), g_out], 2)
    near_early = reduce_near(near_early)
    result = tree_sum(
        [p.astype(F32) for p in scatter_xor(out_part.reshape(seq_n, piece, model), "seq")]
    )
    result = hidden_in[0].astype(F32) + result

    dconv, draw, conv_grad, head_grad = call(
        mixer_back_kernel(width),
        [((length, channels), BF16), ((length, LANES), BF16)]
        + [((8, channels), F32), ((8, LANES), F32)],
        sources
        + [(tall, width), (length, width), (length, LANES), (tall, width), (tall, STATE)]
        + [(length, channels)],
        conv_mine, segments, *head_params, proj, pre, y, dy,
    )

    g_in, dn, norm_grad = call(
        weight_back_kernel(len(x_pieces), len(w_first)),
        [((model, cols), BF16), ((length, model), BF16), ((1, model), F32)],
        [((length, model), BF16), ((model, cols), BF16), wg_scratch],
        *x_pieces, *w_first, *w_second, normed, dconv, draw, d_gate,
    )
    near_late = reduce_near(g_in.reshape(dp_n, -1, cols))
    early = reduce_far(near_early)
    conv_full = jnp.zeros((CONV + 1, inner), F32)
    conv_full = lax.dynamic_update_slice_in_dim(
        conv_full, conv_grad[: CONV + 1, :width], place * width, 1
    )
    conv_full = jnp.concatenate([conv_full, conv_grad[: CONV + 1, width:]], 1)
    conv_full = conv_full.reshape(CONV + 1, owners, conv_here).transpose(1, 0, 2)
    gain_full = lax.dynamic_update_slice_in_dim(
        jnp.zeros((inner,), F32), g_gain[0], place * width, 0
    )
    heads_full = lax.dynamic_update_slice_in_dim(
        jnp.zeros((3, head_count), F32), head_grad[:3, :heads_here], place * heads_here, 1
    )
    small = jnp.concatenate(
        [
            norm_grad.reshape(owners, rows),
            conv_full.reshape(owners, -1),
            gain_full.reshape(owners, gate_here),
            jnp.broadcast_to(heads_full.reshape(1, -1), (owners, 3 * head_count)),
        ],
        1,
    )
    small_count = small.shape[1]
    small = slots(small, rows)
    small_lanes = small.shape[1]
    small = jnp.pad(small, ((0, 0), (heads_here, LANES - heads_here - small_lanes))).astype(BF16)
    near_small = reduce_near(small.reshape(dp_n, -1, LANES))
    near_late = near_late + jnp.pad(near_small, ((0, 0), (0, 0), (channels, 0)))
    late = reduce_far(near_late)
    own_out = early[:, width:]
    own_out = jnp.concatenate(
        [own_out[k * out_rows : (k + 1) * out_rows] for k in range(model // width)], 1
    )
    back_pairs = [(target, source) for source, target in to_heads]
    grad_out_w = lax.ppermute(own_out, ("dp", "seq"), back_pairs)
    dn_parts = scatter_xor(dn.reshape(seq_n, piece, model), "seq")
    d_normed = tree_sum([p.astype(F32) for p in dn_parts])

    both = jnp.concatenate([late, early[:, :width]], 1).reshape(seq_n, rows, cols + width)
    parts = [p.astype(F32) for p in scatter_xor(both.astype(BF16), "seq")]
    ordered = in_order(parts, place)
    grad_in_w = jnp.concatenate(
        [b[:, cols:] for b in ordered]
        + [b[:, :width] for b in ordered]
        + [tree_sum([p[:, width:channels] for p in parts])]
        + [b[:, channels : channels + heads_here] for b in ordered],
        1,
    )
    first = channels + heads_here
    small = tree_sum([p[:, first : first + small_lanes] for p in parts])
    small = small.reshape(-1)[:small_count]
    grad_norm = small[:rows]
    at = rows
    conv_own = small[at : at + (CONV + 1) * conv_here].reshape(CONV + 1, conv_here)
    at += (CONV + 1) * conv_here
    grad_gain = small[at : at + gate_here]
    at += gate_here
    head_own = small[at:].reshape(3, head_count)

    widened = hidden_in[0].astype(F32)
    inverse = lax.rsqrt(jnp.mean(widened * widened, axis=-1, keepdims=True) + EPSILON)
    gain_full_row = tail[:, :, heads_here].reshape(1, -1).astype(F32)
    scaled = d_normed * gain_full_row
    along = jnp.mean(scaled * widened, axis=-1, keepdims=True)
    grad_hidden = out_grad[0].astype(F32) + inverse * (scaled - widened * (inverse * inverse * along))
    return (
        result[None],
        grad_hidden[None],
        grad_norm,
        grad_in_w,
        conv_own[:CONV],
        conv_own[CONV],
        head_own[0],
        head_own[1],
        head_own[2],
        grad_gain,
        grad_out_w,
    )


def solution(mesh):
    in_specs = (
        P("dp", "seq", None),
        P("dp", None),
        P(("dp", "seq")),
        P(("dp", "seq"), None),
        P(None, ("dp", "seq")),
        P(("dp", "seq")),
        P(),
        P(),
        P(),
        P(("dp", "seq")),
        P(("dp", "seq"), None),
        P("dp", "seq", None),
    )
    out_specs = (
        P("dp", "seq", None),
        P("dp", "seq", None),
        P(("dp", "seq")),
        P(("dp", "seq"), None),
        P(None, ("dp", "seq")),
        P(("dp", "seq")),
        P(),
        P(),
        P(),
        P(("dp", "seq")),
        P(("dp", "seq"), None),
    )

    return jax.shard_map(
        on_device, mesh=mesh, in_specs=in_specs, out_specs=out_specs, check_vma=False
    )
```

```python
import jax
import jax.numpy as jnp
from jax import lax
from jax.experimental import pallas as pl
from jax.experimental.pallas import tpu as pltpu
from jax.sharding import PartitionSpec as P

HEAD_DIM = 64
STATE = 128
CONV = 4
CHUNK = 128
VMEM_LIMIT = 56 * 2**20
LANES = 128
EPSILON = 1e-05
FULL = lax.Precision.HIGHEST
MOST = lax.Precision.HIGH
F32 = jnp.float32
BF16 = jnp.bfloat16


def swap(x, axis, offset):
    count = lax.axis_size(axis)
    return lax.ppermute(x, axis, [(i, i ^ offset) for i in range(count)])


def tree_sum(parts):
    while len(parts) > 1:
        parts = [parts[i] + parts[i + 1] for i in range(0, len(parts), 2)]
    return parts[0]


def in_order(pieces, place):
    stacked = jnp.stack(pieces)
    return [lax.dynamic_index_in_dim(stacked, j ^ place, 0, False) for j in range(len(pieces))]


def gather_xor(x, axis):
    return [x] + [swap(x, axis, k) for k in range(1, lax.axis_size(axis))]


def scatter_xor(blocks, axis):
    place = lax.axis_index(axis)
    return [
        swap(lax.dynamic_index_in_dim(blocks, place ^ k, 0, False), axis, k)
        if k
        else lax.dynamic_index_in_dim(blocks, place, 0, False)
        for k in range(lax.axis_size(axis))
    ]


def inner_of(count):
    inner = 1
    while 2 * inner * inner < count:
        inner *= 2
    return inner


def far_offsets():
    count = lax.axis_size("dp")
    inner = inner_of(count)
    return [k * inner for k in range(1, count // inner)]


def gather_far(x):
    return [x] + [swap(x, "dp", k) for k in far_offsets()]


def gather_near(far):
    inner = inner_of(lax.axis_size("dp"))
    near = [[piece] + [swap(piece, "dp", j) for j in range(1, inner)] for piece in far]
    return [piece for group in near for piece in group]


def reduce_slabs(slabs):
    parts = [swap(p, "dp", j) if j else p for j, p in enumerate(slabs)]
    return tree_sum([p.astype(F32) for p in parts]).astype(BF16)


def reduce_near(grads):
    count = lax.axis_size("dp")
    inner = inner_of(count)
    inner_place = lax.axis_index("dp") % inner
    shaped = grads.reshape(count // inner, inner, *grads.shape[1:])
    parts = []
    for j in range(inner):
        slab = lax.dynamic_index_in_dim(shaped, inner_place ^ j, 1, False)
        parts.append(swap(slab, "dp", j) if j else slab)
    return tree_sum([p.astype(F32) for p in parts]).astype(BF16)


def reduce_far(near):
    outer_place = lax.axis_index("dp") // inner_of(lax.axis_size("dp"))
    parts = [lax.dynamic_index_in_dim(near, outer_place, 0, False)]
    for k, offset in enumerate(far_offsets()):
        slab = lax.dynamic_index_in_dim(near, outer_place ^ (k + 1), 0, False)
        parts.append(swap(slab, "dp", offset))
    return tree_sum([p.astype(F32) for p in parts])


def dot(a, b, ca, cb, precision=None):
    return lax.dot_general(
        a, b, (((ca,), (cb,)), ((), ())), precision=precision, preferred_element_type=F32
    )


def exact(a, b):
    return dot(a, b, 1, 0, FULL)


def mm(a, b):
    return dot(a, b, 1, 0, MOST)


def mm_nt(a, b):
    return dot(a, b, 1, 1, MOST)


def mm_tn(a, b):
    return dot(a, b, 0, 0, MOST)


def softplus(x):
    small = jnp.exp(-jnp.abs(x))
    up = 1.0 + small
    down = up - 1.0
    log1p = jnp.where(down == 0.0, small, jnp.log(up) * (small / jnp.where(down == 0.0, 1.0, down)))
    return jnp.maximum(x, 0.0) + log1p


def expand_matrix(width):
    head = lax.broadcasted_iota(jnp.int32, (LANES, width), 0)
    column = lax.broadcasted_iota(jnp.int32, (LANES, width), 1)
    return (column // HEAD_DIM == head).astype(F32)


def triangle(lower):
    row = lax.broadcasted_iota(jnp.int32, (CHUNK, CHUNK), 0)
    column = lax.broadcasted_iota(jnp.int32, (CHUNK, CHUNK), 1)
    return row >= column if lower else row <= column


def head_rows(bias_ref, decay_ref, skip_ref, heads_here):
    rows = jnp.concatenate([bias_ref[...], decay_ref[...], skip_ref[...]], 0)
    count = rows.shape[1]
    rows = jnp.concatenate([rows, jnp.zeros((3, LANES - count), F32)], 1)
    rows = jnp.concatenate([rows, jnp.zeros((5, LANES), F32)], 0)
    place = lax.axis_index("seq")
    mine = rows
    for j in range(1, count // heads_here):
        moved = jnp.concatenate([rows[:, j * heads_here :], rows[:, : j * heads_here]], 1)
        mine = jnp.where(place == j, moved, mine)
    return mine


def spread_segments(seg_ref, seg_col, seg_row):
    seg_row[:, : 2 * CHUNK] = jnp.full((8, 2 * CHUNK), -1.0, F32)
    for i in range(seg_ref.shape[1] // CHUNK):
        now = seg_ref[:, i * CHUNK : (i + 1) * CHUNK].astype(F32)
        seg_row[:, (i + 2) * CHUNK : (i + 3) * CHUNK] = jnp.broadcast_to(now, (8, CHUNK))
        seg_col[i * CHUNK : (i + 1) * CHUNK, :] = jnp.broadcast_to(now, (CHUNK, CHUNK)).T


def same_segment(seg_col, back, width):
    now = seg_col[...]
    row = lax.broadcasted_iota(jnp.int32, now.shape, 0)
    same = ((now == pltpu.roll(now, back, 0)) & (row >= back)).astype(F32)
    return jnp.concatenate([same] * (width // LANES), 1)


def masks_of(seg_col, seg_row, i):
    column = seg_col[pl.ds(i * CHUNK, CHUNK), :]

    def row(j):
        return seg_row[:, pl.ds((i + j) * CHUNK, CHUNK)][:1]

    far = (column == row(0)).astype(F32)
    near = (column == row(1)).astype(F32)
    own = (column == row(2)) & triangle(True)
    return far, near, own


def lane_halves():
    lane = lax.broadcasted_iota(jnp.int32, (1, LANES), 1)
    low = (lane < HEAD_DIM).astype(F32)
    return low, 1.0 - low


def rms_inverse(x):
    return lax.rsqrt(jnp.mean(x * x, axis=-1, keepdims=True) + EPSILON)


def gain_row(weights, lane_of_gain):
    tail = weights[:, weights.shape[1] - LANES :]
    pick = (lax.broadcasted_iota(jnp.int32, (8, LANES), 1) == lane_of_gain).astype(BF16)
    return dot(pick, tail, 1, 1)[:1]


def decays(raw, heads):
    step = softplus(raw + heads[0:1])
    return step, step * (-jnp.exp(heads[1:2]))


def spread_heads(columns, low, width):
    pairs = []
    for pair in range(width // LANES):
        first = columns[:, 2 * pair : 2 * pair + 1]
        second = columns[:, 2 * pair + 1 : 2 * pair + 2]
        pairs.append(jnp.where(low > 0.0, first, second))
    return jnp.concatenate(pairs, 1)


def fill_sources(i, v, step, decay, low, vd, vt, ecx):
    cumulative = exact(triangle(True).astype(F32), decay)
    step_x = spread_heads(step, low, v.shape[1])
    cum_x = spread_heads(cumulative, low, v.shape[1])
    last = cum_x[CHUNK - 1 :]
    vd_now = v * step_x
    vd[pl.ds(i * CHUNK, CHUNK), :] = vd_now
    vt[pl.ds((i + 2) * CHUNK, CHUNK), :] = vd_now * jnp.exp(last - cum_x)
    ecx[pl.ds(i * CHUNK + 8, CHUNK), :] = jnp.exp(cum_x)
    return cumulative, step_x, cum_x, last


def head_decay(cumulative, cumulative_t, own, h):
    gap = cumulative[:, h : h + 1] - cumulative_t[h : h + 1, :]
    return jnp.exp(jnp.where(own, gap, -1e30))


def put_in_order(pieces, place, target, source=None, lanes=None):
    for m, piece in enumerate(pieces):
        source_rows = slice(0, piece.shape[0]) if source is None else source
        rows = source_rows.stop - source_rows.start
        start = pl.multiple_of((place ^ m) * rows, rows)
        if lanes is None:
            target[pl.ds(start, rows), :] = piece[...]
        else:
            target[pl.ds(start, rows), lanes[0]] = piece[source_rows, lanes[1]]


def dp_index(pieces):
    return lax.axis_index("dp") if len(pieces) > 1 else 0


def put_second(pieces, place, wg_ref=None, wo_ref=None):
    rows, both = pieces[0].shape
    width = both // 2
    if wg_ref is not None:
        put_in_order(pieces, place, wg_ref, slice(0, rows), (slice(0, width), slice(0, width)))
    if wo_ref is not None:
        folds = wo_ref.shape[1] // width
        part = rows // folds
        for k in range(folds):
            to = (slice(k * width, (k + 1) * width), slice(width, 2 * width))
            put_in_order(pieces, place, wo_ref, slice(k * part, (k + 1) * part), to)


def small_spots(rows, lengths):
    group = min(rows, len(lengths))
    return [(i % group, (i // group) * max(lengths)) for i in range(len(lengths))]


def store_slabs(values, outs):
    if len(outs[0].shape) == 2:
        outs[0][...] = values[...].astype(BF16)
        return
    inner, (outer, rows, _) = len(outs), outs[0].shape
    place = lax.axis_index("dp") % inner if inner > 1 else 0
    for j, out in enumerate(outs):
        for o in range(outer):
            start = (o * inner + (place ^ j)) * rows
            if inner > 1:
                start = pl.multiple_of(start, rows)
            out[o] = values[pl.ds(start, rows), :].astype(BF16)


def store_pieces(values, outs):
    rows = outs[0].shape[0]
    for k, out in enumerate(outs):
        start = pl.multiple_of((lax.axis_index("seq") ^ k) * rows, rows)
        out[...] = values[pl.ds(start, rows), :].astype(BF16)


def finish_kernel(width, inner, heads_here, lengths, spots):
    def body(*refs):
        count = inner // width
        parts, refs = refs[:count], refs[count:]
        grad_ref, outs, blocks = refs[0], refs[1:-1], refs[-1]
        rows = grad_ref.shape[0]
        stride = blocks.shape[0] // count
        states, tail = width, width + 2 * STATE
        for k, part in enumerate(parts):
            start = pl.multiple_of((lax.axis_index("seq") ^ k) * stride, stride)
            blocks[pl.ds(start, rows), :] = part[...].astype(F32)
        steps = []
        for j in range(count):
            at = slice(j * stride, j * stride + rows)
            grad_ref[:, j * width : (j + 1) * width] = blocks[at, tail + LANES :]
            grad_ref[:, inner + j * width : inner + (j + 1) * width] = blocks[at, :width]
            steps.append(blocks[at, tail : tail + heads_here])
        both = tree_sum([part[:, states:tail].astype(F32) for part in parts])
        grad_ref[:, 2 * inner : 2 * inner + 2 * STATE] = both
        grad_ref[:, 2 * inner + 2 * STATE :] = jnp.concatenate(steps, 1)
        total = tree_sum([part[:, tail : tail + LANES].astype(F32) for part in parts])
        found = []
        for length, (row, lane) in zip(lengths, spots):
            first = heads_here + lane
            found.append(total[row : row + 1, first : first + length])
        outs[0][...] = jnp.concatenate(found[:CONV], 0)
        for out, vector in zip(outs[1:], found[CONV:]):
            out[...] = vector

    return body


def pack_kernel(width, inner, heads_here, count):
    def body(w_ref, taps_ref, shift_ref, gate_ref, norm_ref, *refs):
        outs, blocks = refs[:-1], refs[-1]
        rows = w_ref.shape[0]
        stride = blocks.shape[0] // count
        states = 2 * inner + 2 * STATE
        norm = jnp.concatenate([norm_ref[...].astype(F32), jnp.zeros((1, LANES - rows), F32)], 1)
        column = jnp.broadcast_to(norm, (LANES, LANES)).T[:rows]
        taps = taps_ref[...].astype(F32)
        vectors = [taps[i : i + 1] for i in range(CONV)]
        vectors += [shift_ref[...].astype(F32), gate_ref[...].astype(F32)]
        spots = small_spots(rows, [v.shape[1] for v in vectors])
        lane = lax.broadcasted_iota(jnp.int32, (rows, LANES), 1)
        row = lax.broadcasted_iota(jnp.int32, (rows, LANES), 0)
        shared = jnp.where(lane == heads_here, column, 0.0)
        for vector, (at_row, at_lane) in zip(vectors, spots):
            start = heads_here + 1 + at_lane
            pieces = [jnp.zeros((1, start), F32), vector]
            pieces.append(jnp.zeros((1, LANES - start - vector.shape[1]), F32))
            shared = shared + jnp.where(row == at_row, jnp.concatenate(pieces, 1), 0.0)
        for j in range(count):
            at = slice(j * stride, j * stride + rows)
            first = states + j * heads_here
            blocks[at, :width] = w_ref[:, inner + j * width : inner + (j + 1) * width].astype(F32)
            blocks[at, width : width + 2 * STATE] = w_ref[:, 2 * inner : states].astype(F32)
            steps = w_ref[:, first : first + heads_here].astype(F32)
            tail = jnp.concatenate([steps, shared[:, heads_here:]], 1)
            blocks[at, width + 2 * STATE : width + 2 * STATE + LANES] = tail
            gate = w_ref[:, j * width : (j + 1) * width].astype(F32)
            blocks[at, width + 2 * STATE + LANES :] = gate
        for k in range(count):
            start = pl.multiple_of((lax.axis_index("seq") ^ k) * stride, stride)
            outs[k][...] = blocks[pl.ds(start, rows), :].astype(BF16)

    return body


def forward_kernel(width, lane_of_gain, x_count, w_count):
    heads_here = width // HEAD_DIM

    def body(*refs):
        x_pieces, refs = refs[:x_count], refs[x_count:]
        w_pieces, refs = refs[:w_count], refs[w_count:]
        conv_ref, seg_ref, bias_ref, decay_ref, skip_ref, normed_ref, proj_ref, pre_ref, y_ref, bpad, vd, vt, ecx, seg_col, seg_row, x_ref, w_ref = refs
        put_in_order(x_pieces, lax.axis_index("seq"), x_ref)
        put_in_order(w_pieces, dp_index(w_pieces), w_ref)
        x = x_ref[...].astype(F32)
        gain = gain_row(w_ref[...], lane_of_gain)
        normed_ref[...] = (x * rms_inverse(x) * gain).astype(BF16)
        proj_ref[...] = dot(normed_ref[...], w_ref[...], 1, 0)
        spread_segments(seg_ref, seg_col, seg_row)
        channels = width + 2 * STATE
        u = proj_ref[:, :channels]
        running = conv_ref[CONV : CONV + 1, :] + conv_ref[CONV - 1 : CONV, :] * u
        for back in range(1, CONV):
            tap = conv_ref[CONV - 1 - back : CONV - back, :]
            running = running + tap * pltpu.roll(u, back, 0) * same_segment(seg_col, back, channels)
        pre_ref[...] = running
        bpad[pl.ds(0, 2 * CHUNK), :] = jnp.zeros((2 * CHUNK, STATE), F32)
        vt[pl.ds(0, 2 * CHUNK), :] = jnp.zeros((2 * CHUNK, width), F32)
        ecx[pl.ds(0, 8), :] = jnp.zeros((8, width), F32)
        b_pre = running[:, width : width + STATE]
        bpad[pl.ds(2 * CHUNK, x.shape[0]), :] = b_pre * jax.nn.sigmoid(b_pre)
        expand = expand_matrix(width)
        low, high = lane_halves()
        heads = head_rows(bias_ref, decay_ref, skip_ref, heads_here)
        skip_x = exact(jnp.broadcast_to(heads[2:3], (8, LANES)), expand)[:1]

        def chunk(i, carry):
            rows = pl.ds(i * CHUNK, CHUNK)
            v_pre = pre_ref[rows, :width]
            c_pre = pre_ref[rows, width + STATE :]
            v = v_pre * jax.nn.sigmoid(v_pre)
            c = c_pre * jax.nn.sigmoid(c_pre)
            step, decay = decays(proj_ref[rows, channels:], heads)
            cumulative, _, _, _ = fill_sources(i, v, step, decay, low, vd, vt, ecx)
            cumulative_t = cumulative.T
            far, near, own = masks_of(seg_col, seg_row, i)
            window = pl.ds(i * CHUNK, 3 * CHUNK)
            scores = mm_nt(c, bpad[window, :])
            s_far = scores[:, :CHUNK] * far
            s_near = scores[:, CHUNK : 2 * CHUNK] * near
            s_own = scores[:, 2 * CHUNK :]
            ecx_now = ecx[pl.ds(i * CHUNK + 8, CHUNK), :]
            last_before = ecx[pl.ds(i * CHUNK, 8), :][7:8]
            vt_far = vt[rows, :] * last_before
            vt_near = vt[pl.ds((i + 1) * CHUNK, CHUNK), :]
            off = mm(s_far, vt_far) + mm(s_near, vt_near)
            y_ref[rows, :] = off * ecx_now + skip_x * v
            for pair in range(heads_here // 2):
                lanes = slice(pair * LANES, (pair + 1) * LANES)
                n0 = s_own * head_decay(cumulative, cumulative_t, own, 2 * pair)
                n1 = s_own * head_decay(cumulative, cumulative_t, own, 2 * pair + 1)
                vp = vd[rows, lanes]
                both = mm(jnp.concatenate([n0, n1], 1), jnp.concatenate([vp * low, vp * high], 0))
                y_ref[rows, lanes] = y_ref[rows, lanes] + both
            return carry

        for turn in range(x.shape[0] // CHUNK):
            chunk(turn, 0)

    return body


def gate_kernel(og_count, w_count):
    def body(*refs):
        og_pieces, refs = refs[:og_count], refs[og_count:]
        w_pieces, refs = refs[:w_count], refs[w_count:]
        normed_ref, y_ref, gain_ref, gate_ref, dg_ref, stats_ref, og_ref, wg_ref, wo_ref = refs
        put_in_order(og_pieces, lax.axis_index("seq"), og_ref)
        put_second(w_pieces, dp_index(w_pieces), wg_ref, wo_ref)
        gate = dot(normed_ref[...], wg_ref[...], 1, 0)
        gate_ref[...] = gate
        d_gated = dot(og_ref[...], wo_ref[...], 1, 1)
        dg_ref[...] = d_gated
        v = y_ref[...] * (gate * jax.nn.sigmoid(gate))
        squares = jnp.sum(v * v, axis=1, keepdims=True)
        cross = jnp.sum(v * (d_gated * gain_ref[...]), axis=1, keepdims=True)
        lane = lax.broadcasted_iota(jnp.int32, (CHUNK, LANES), 1)
        for i in range(stats_ref.shape[0]):
            rows = slice(i * CHUNK, (i + 1) * CHUNK)
            both = jnp.where(lane == 0, squares[rows], jnp.where(lane == 1, cross[rows], 0.0))
            stats_ref[i] = both.T[:8]

    return body


def out_kernel(width, whole_width, og_count, w_count, slab_count, block_rows):
    def body(*refs):
        og_pieces, refs = refs[:og_count], refs[og_count:]
        w_pieces, refs = refs[:w_count], refs[w_count:]
        stats, refs = refs[:og_count], refs[og_count:]
        normed_ref, gate_ref, dg_ref, y_ref, gain_ref = refs[:5]
        out_refs, refs = refs[5 : 5 + og_count], refs[5 + og_count :]
        slabs, refs = refs[:slab_count], refs[slab_count:]
        dgate_ref, dy_ref, ggain_ref, og_ref, wo_ref, out_all, grad_all = refs
        put_in_order(og_pieces, lax.axis_index("seq"), og_ref)
        put_second(w_pieces, dp_index(w_pieces), None, wo_ref)
        columns = []
        for i in range(stats[0].shape[0]):
            total = tree_sum([part[i] for part in stats])
            square = jnp.concatenate([total, jnp.zeros((CHUNK - 8, LANES), F32)], 0)
            columns.append(square.T)
        columns = jnp.concatenate(columns, 0)
        inverse = lax.rsqrt(columns[:, 0:1] / whole_width + EPSILON)
        cross = columns[:, 1:2] / whole_width
        gate = gate_ref[...]
        sig = jax.nn.sigmoid(gate)
        silu = gate * sig
        y = y_ref[...]
        v = y * silu
        gain = gain_ref[...]
        scaled = v * inverse
        gated = (scaled * gain).astype(BF16)
        out_all[...] = dot(gated, wo_ref[...], 1, 0)
        store_pieces(out_all, out_refs)
        rows = block_rows
        folds = og_ref.shape[1] // width
        part = rows // folds
        g_out = dot(gated, og_ref[...], 0, 0)
        for d in range(grad_all.shape[0] // rows):
            for k in range(folds):
                to = slice(d * rows + k * part, d * rows + (k + 1) * part)
                grad_all[to, width:] = g_out[d * part : (d + 1) * part, k * width : (k + 1) * width]
        d_gated = dg_ref[...]
        ggain_ref[...] = jnp.broadcast_to(jnp.sum(d_gated * scaled, axis=0, keepdims=True), (8, width))
        dv = inverse * (d_gated * gain - v * (inverse * inverse * cross))
        dy_ref[...] = dv * silu
        dgate = (dv * y * (sig * (1.0 + gate * (1.0 - sig)))).astype(BF16)
        dgate_ref[...] = dgate
        grad_all[:, :width] = dot(normed_ref[...], dgate, 0, 0)
        store_slabs(grad_all, slabs)

    return body


def mixer_back_kernel(width):
    heads_here = width // HEAD_DIM

    def body(conv_ref, seg_ref, bias_ref, decay_ref, skip_ref, proj_ref, pre_ref, y_ref, dy_ref, dconv_ref, draw, conv_grad_ref, head_grad_ref, bpad, vd, vt, ecx, seg_col, seg_row, tailx, stepx, cums, ua, db, dpre):
        length = proj_ref.shape[0]
        spread_segments(seg_ref, seg_col, seg_row)
        chunks = length // CHUNK
        channels = width + 2 * STATE
        expand = expand_matrix(width)
        low, high = lane_halves()
        heads = head_rows(bias_ref, decay_ref, skip_ref, heads_here)
        rate = jnp.exp(heads[1:2])
        skip_x = exact(jnp.broadcast_to(heads[2:3], (8, LANES)), expand)[:1]
        bpad[pl.ds(0, 2 * CHUNK), :] = jnp.zeros((2 * CHUNK, STATE), F32)
        vt[pl.ds(0, 2 * CHUNK), :] = jnp.zeros((2 * CHUNK, width), F32)
        tailx[pl.ds(0, 2 * CHUNK), :] = jnp.zeros((2 * CHUNK, width), F32)
        ecx[pl.ds(0, 8), :] = jnp.zeros((8, width), F32)
        b_pre = pre_ref[:, width : width + STATE]
        bpad[pl.ds(2 * CHUNK, length), :] = b_pre * jax.nn.sigmoid(b_pre)
        ua[...] = jnp.zeros(ua.shape, F32)
        db[...] = jnp.zeros(db.shape, F32)

        def prepare(i, carry):
            rows = pl.ds(i * CHUNK, CHUNK)
            v_pre = pre_ref[rows, :width]
            v = v_pre * jax.nn.sigmoid(v_pre)
            step, decay = decays(proj_ref[rows, channels:], heads)
            cumulative, step_x, cum_x, last = fill_sources(i, v, step, decay, low, vd, vt, ecx)
            cums[rows, :] = cumulative
            stepx[rows, :] = step_x
            tailx[pl.ds((i + 2) * CHUNK, CHUNK), :] = jnp.exp(last - cum_x)
            return carry

        for turn in range(chunks):
            prepare(turn, 0)

        def chunk(turn, carry):
            later, g_bias, g_rate, g_skip = carry
            i = chunks - 1 - turn
            rows = pl.ds(i * CHUNK, CHUNK)
            rows_near = pl.ds((i + 1) * CHUNK, CHUNK)
            rows_own = pl.ds((i + 2) * CHUNK, CHUNK)
            window = pl.ds(i * CHUNK, 3 * CHUNK)
            v_pre = pre_ref[rows, :width]
            v_sig = jax.nn.sigmoid(v_pre)
            v = v_pre * v_sig
            c_pre = pre_ref[rows, width + STATE :]
            c_sig = jax.nn.sigmoid(c_pre)
            c = c_pre * c_sig
            raw = proj_ref[rows, channels:]
            step, decay = decays(raw, heads)
            cumulative = cums[rows, :]
            cumulative_t = cumulative.T
            far, near, own = masks_of(seg_col, seg_row, i)
            b_window = bpad[window, :]
            scores = mm_nt(c, b_window)
            s_far = scores[:, :CHUNK] * far
            s_near = scores[:, CHUNK : 2 * CHUNK] * near
            s_own = scores[:, 2 * CHUNK :]
            dy = dy_ref[rows, :]
            dye = dy * ecx[pl.ds(i * CHUNK + 8, CHUNK), :]
            dye_far = dye * ecx[pl.ds(i * CHUNK, 8), :][7:8]
            ds_far = mm_nt(dye_far, vt[rows, :]) * far
            ds_near = mm_nt(dye, vt[rows_near, :]) * near
            ua[rows, :] = ua[rows, :] + tailx[rows, :] * mm_tn(s_far, dye_far)
            ua[rows_near, :] = ua[rows_near, :] + tailx[rows_near, :] * mm_tn(s_near, dye)
            ds_own = jnp.zeros((CHUNK, CHUNK), F32)
            for pair in range(heads_here // 2):
                lanes = slice(pair * LANES, (pair + 1) * LANES)
                d0 = head_decay(cumulative, cumulative_t, own, 2 * pair)
                d1 = head_decay(cumulative, cumulative_t, own, 2 * pair + 1)
                dyp = dy_ref[rows, lanes]
                split = jnp.concatenate([dyp * low, dyp * high], 0)
                dm = mm_nt(split, vd[rows, lanes])
                ds_own = ds_own + dm[:CHUNK] * d0 + dm[CHUNK:] * d1
                u_pair = mm_tn(jnp.concatenate([s_own * d0, s_own * d1], 0), split)
                ua[rows_own, lanes] = ua[rows_own, lanes] + u_pair
            ds_all = jnp.concatenate([ds_far, ds_near, ds_own], 1)
            dc = mm(ds_all, b_window)
            db[window, :] = db[window, :] + mm_tn(ds_all, c)
            u_total = ua[rows_own, :]
            received = mm_nt(dy * (y_ref[rows, :] - skip_x * v), expand)
            d_step = mm_nt(v * u_total, expand)
            gap = received - step * d_step
            d_decay = exact(triangle(False).astype(F32), gap) + later
            d_step = d_step - d_decay * rate
            d_raw = d_step * jax.nn.sigmoid(raw + heads[0:1])
            draw[rows, :] = d_raw.astype(BF16)
            dv = stepx[rows, :] * u_total + skip_x * dy
            dpre[rows, :width] = dv * (v_sig * (1.0 + v_pre * (1.0 - v_sig)))
            b_pre = pre_ref[rows, width : width + STATE]
            b_sig = jax.nn.sigmoid(b_pre)
            dpre[rows, width : width + STATE] = db[rows_own, :] * (b_sig * (1.0 + b_pre * (1.0 - b_sig)))
            dpre[rows, width + STATE :] = dc * (c_sig * (1.0 + c_pre * (1.0 - c_sig)))
            g_skip = g_skip + jnp.sum(dy * v, axis=0, keepdims=True)
            g_bias = g_bias + jnp.sum(d_raw, axis=0, keepdims=True)
            g_rate = g_rate + jnp.sum(d_decay * decay, axis=0, keepdims=True)
            return (later + jnp.sum(gap, axis=0, keepdims=True), g_bias, g_rate, g_skip)

        none = jnp.zeros((1, LANES), F32)
        none_wide = jnp.zeros((1, heads_here * HEAD_DIM), F32)
        start = (none, none, none, none_wide)
        state = start
        for turn in range(chunks):
            state = chunk(turn, state)
        _, g_bias, g_rate, g_skip = state
        g_skip = dot(jnp.broadcast_to(g_skip, (8, g_skip.shape[1])), expand, 1, 1, FULL)[:1]
        head_grad_ref[...] = jnp.concatenate([g_bias, g_rate, g_skip, jnp.zeros((5, LANES), F32)], 0)
        u = proj_ref[:, :channels]
        d = dpre[...]
        du = conv_ref[CONV - 1 : CONV, :] * d
        taps = [jnp.sum(d * u, axis=0, keepdims=True)]
        for back in range(1, CONV):
            masked = d * same_segment(seg_col, back, channels)
            taps.insert(0, jnp.sum(masked * pltpu.roll(u, back, 0), axis=0, keepdims=True))
            du = du + conv_ref[CONV - 1 - back : CONV - back, :] * pltpu.roll(masked, length - back, 0)
        taps.append(jnp.sum(d, axis=0, keepdims=True))
        taps.append(jnp.zeros((8 - CONV - 1, channels), F32))
        conv_grad_ref[...] = jnp.concatenate(taps, 0)
        dconv_ref[...] = du.astype(BF16)

    return body


def weight_back_kernel(x_count, w_count, slab_count):
    def body(*refs):
        x_pieces, refs = refs[:x_count], refs[x_count:]
        w_pieces, refs = refs[:w_count], refs[w_count:]
        g_pieces, refs = refs[:w_count], refs[w_count:]
        normed_ref, dconv_ref, draw_ref, dgate_ref = refs[:4]
        slabs, refs = refs[4 : 4 + slab_count], refs[4 + slab_count :]
        dn_refs, refs = refs[:x_count], refs[x_count:]
        norm_grad_ref, x_ref, w_ref, wg_ref, dn_all, gin_ref = refs
        put_in_order(x_pieces, lax.axis_index("seq"), x_ref)
        put_in_order(w_pieces, dp_index(w_pieces), w_ref)
        put_second(g_pieces, dp_index(w_pieces), wg_ref)
        channels = dconv_ref.shape[1]
        dconv, draw = dconv_ref[...], draw_ref[...]
        dn = dot(dconv, w_ref[:, :channels], 1, 1) + dot(draw, w_ref[:, channels:], 1, 1)
        dn = dn + dot(dgate_ref[...], wg_ref[...], 1, 1)
        dn_all[...] = dn
        store_pieces(dn_all, dn_refs)
        gin_ref[:, :channels] = dot(normed_ref[...], dconv, 0, 0)
        x = x_ref[...].astype(F32)
        along = jnp.sum(dn * (x * rms_inverse(x)), axis=0, keepdims=True)
        norm_grad_ref[...] = along
        gin_ref[:, channels:] = dot(normed_ref[...], draw, 0, 0)
        store_slabs(gin_ref, slabs)

    return body


def call(body, outs, scratch, *operands):
    vmem = pl.BlockSpec(memory_space=pltpu.VMEM)
    return pl.pallas_call(
        body,
        out_shape=[jax.ShapeDtypeStruct(shape, kind) for shape, kind in outs],
        in_specs=[vmem] * len(operands),
        out_specs=[vmem] * len(outs),
        scratch_shapes=[
            pltpu.VMEM(*shape) if isinstance(shape[0], tuple) else pltpu.VMEM(shape, F32)
            for shape in scratch
        ],
        compiler_params=pltpu.CompilerParams(vmem_limit_bytes=VMEM_LIMIT),
    )(*operands)


def on_device(
    hidden_in,
    segments,
    norm_gain,
    in_weight,
    conv_weight,
    conv_bias,
    step_bias,
    decay_log,
    skip_weight,
    gate_gain,
    out_weight,
    out_grad,
):
    row_count, piece, model = hidden_in.shape
    assert row_count == 1
    seq_n, dp_n = lax.axis_size("seq"), lax.axis_size("dp")
    owners = seq_n * dp_n
    place, dp_place = lax.axis_index("seq"), lax.axis_index("dp")
    length = piece * seq_n
    head_count = step_bias.shape[0]
    inner = head_count * HEAD_DIM
    heads_here = head_count // seq_n
    width = inner // seq_n
    channels = width + 2 * STATE
    cols = channels + LANES
    rows = in_weight.shape[0]
    conv_here = conv_bias.shape[0]
    gate_here = gate_gain.shape[0]

    stride = -(-rows // 16) * 16
    blocks = call(
        pack_kernel(width, inner, heads_here, seq_n),
        [((rows, cols + width), BF16)] * seq_n,
        [(seq_n * stride, cols + width)],
        in_weight, conv_weight, conv_bias[None], gate_gain[None], norm_gain[None],
    )
    blocks = [b if k == 0 else swap(b, "seq", k) for k, b in enumerate(blocks)]
    mine = jnp.concatenate(in_order(blocks, place), 0)
    first_part, gate_part = mine[:, :cols], mine[:, cols:]
    far_first = gather_far(first_part)
    x_pieces = gather_xor(hidden_in[0], "seq")
    og_pieces = gather_xor(out_grad[0], "seq")

    def linear(d, s):
        return d * seq_n + s

    to_heads = [(b, linear(b % dp_n, b // dp_n)) for b in range(owners)]
    out_block = lax.ppermute(out_weight, ("dp", "seq"), to_heads)
    out_rows = out_block.shape[0]
    folded = jnp.concatenate(
        [out_block[:, k * width : (k + 1) * width] for k in range(model // width)], 0
    )
    second = jnp.concatenate([gate_part, folded], 1)
    far_second = gather_far(second)
    w_first = gather_near(far_first)
    w_second = gather_near(far_second)
    split_here = not out_rows % 16
    if not split_here:
        w_first = [jnp.concatenate(in_order(w_first, dp_place), 0)]
        w_second = in_order(w_second, dp_place)
        folds = [slice(k * out_rows, (k + 1) * out_rows) for k in range(model // width)]
        w_out = jnp.concatenate([p[f, width:] for f in folds for p in w_second], 0)
        w_second = [
            jnp.concatenate([jnp.concatenate([p[:, :width] for p in w_second], 0), w_out], 1)
        ]
    if len(w_first) > 1:
        tail = jnp.concatenate(in_order([p[:, channels:] for p in w_first], dp_place), 0)
    else:
        tail = w_first[0][:, channels:]
    tail = tail.reshape(owners, rows, LANES)
    lengths = [conv_here] * (CONV + 1) + [gate_here]
    spots = small_spots(rows, lengths)
    if rows >= len(lengths):
        conv_all = tail[:, : CONV + 1, heads_here + 1 : heads_here + 1 + conv_here]
        conv_all = conv_all.transpose(1, 0, 2).reshape(CONV + 1, owners * conv_here)
    else:
        conv_all = []
        for r, lane in spots[: CONV + 1]:
            first = heads_here + 1 + lane
            conv_all.append(tail[:, r, first : first + conv_here].reshape(1, -1))
        conv_all = jnp.concatenate(conv_all, 0)
    conv_mine = jnp.concatenate(
        [
            lax.dynamic_slice_in_dim(conv_all[:, :inner], place * width, width, 1),
            conv_all[:, inner:],
        ],
        1,
    )
    conv_mine = jnp.pad(conv_mine.astype(F32), ((0, 8 - CONV - 1), (0, 0)))
    first = heads_here + 1 + spots[-1][1]
    gain_all = tail[:, spots[-1][0], first : first + gate_here]
    gain_mine = lax.dynamic_slice_in_dim(gain_all.reshape(1, inner), place * width, width, 1)
    gain_mine = gain_mine.astype(F32)

    head_params = (step_bias[None], decay_log[None], skip_weight[None])

    chunks = length // CHUNK
    tall = length + 2 * CHUNK
    sources = [(tall, STATE), (length, width), (tall, width), (length + 8, width)]
    sources += [(length, LANES), (8, tall)]
    normed, proj, pre, y = call(
        forward_kernel(width, heads_here, len(x_pieces), len(w_first)),
        [((length, model), BF16)]
        + [((length, cols), F32), ((length, channels), F32), ((length, width), F32)],
        sources + [((length, model), BF16), ((model, cols), BF16)],
        *x_pieces, *w_first, conv_mine, segments, *head_params,
    )
    og_scratch, wg_scratch = ((length, model), BF16), ((model, width), BF16)
    wo_scratch = ((width, model), BF16)
    gate, d_gated, stats = call(
        gate_kernel(len(og_pieces), len(w_second)),
        [((length, width), F32), ((length, width), F32), ((chunks, 8, LANES), F32)],
        [og_scratch, wg_scratch, wo_scratch],
        *og_pieces, *w_second, normed, y, gain_mine,
    )
    stats = gather_xor(stats, "seq")
    block_rows = rows * seq_n
    dp_inner = inner_of(dp_n)
    if split_here:
        slabs = [((dp_n // dp_inner, block_rows, cols), BF16)] * dp_inner
    else:
        slabs = [((model, cols), BF16)]
    pieces = [((piece, model), BF16)] * seq_n

    def near_sum(made):
        if split_here:
            return reduce_slabs(made)
        return reduce_near(made[0].reshape(dp_n, -1, made[0].shape[-1]))

    second_slabs = [((*shape[:-1], 2 * width), kind) for shape, kind in slabs]
    made = call(
        out_kernel(width, inner, len(og_pieces), len(w_second), len(slabs), block_rows),
        pieces + second_slabs
        + [((length, width), BF16), ((length, width), F32), ((8, width), F32)],
        [og_scratch, wo_scratch, (length, model), (model, 2 * width)],
        *og_pieces, *w_second, *stats, normed, gate, d_gated, y, gain_mine,
    )
    out_parts, made = made[:seq_n], made[seq_n:]
    near_early = near_sum(made[: len(slabs)])
    d_gate, dy, g_gain = made[len(slabs) :]
    result = tree_sum(
        [(swap(p, "seq", k) if k else p).astype(F32) for k, p in enumerate(out_parts)]
    )
    result = hidden_in[0].astype(F32) + result

    dconv, draw, conv_grad, head_grad = call(
        mixer_back_kernel(width),
        [((length, channels), BF16), ((length, LANES), BF16)]
        + [((8, channels), F32), ((8, LANES), F32)],
        sources
        + [(tall, width), (length, width), (length, LANES), (tall, width), (tall, STATE)]
        + [(length, channels)],
        conv_mine, segments, *head_params, proj, pre, y, dy,
    )

    made = call(
        weight_back_kernel(len(x_pieces), len(w_first), len(slabs)),
        slabs + pieces + [((1, model), F32)],
        [((length, model), BF16), ((model, cols), BF16), wg_scratch, (length, model), (model, cols)],
        *x_pieces, *w_first, *w_second, normed, dconv, draw, d_gate,
    )
    dn_pieces, norm_grad = made[len(slabs) : -1], made[-1]
    near_late = near_sum(made[: len(slabs)])
    early = reduce_far(near_early)
    conv_full = jnp.zeros((CONV + 1, inner), F32)
    conv_full = lax.dynamic_update_slice_in_dim(
        conv_full, conv_grad[: CONV + 1, :width], place * width, 1
    )
    conv_full = jnp.concatenate([conv_full, conv_grad[: CONV + 1, width:]], 1)
    conv_full = conv_full.reshape(CONV + 1, owners, conv_here).transpose(1, 0, 2)
    gain_full = lax.dynamic_update_slice_in_dim(
        jnp.zeros((inner,), F32), g_gain[0], place * width, 0
    )
    heads_full = lax.dynamic_update_slice_in_dim(
        jnp.zeros((3, head_count), F32), head_grad[:3, :heads_here], place * heads_here, 1
    )
    heads_rows = jnp.broadcast_to(heads_full[None], (owners, 3, head_count))
    lengths = [conv_here] * (CONV + 1) + [gate_here, rows] + [head_count] * 3
    small_at = small_spots(rows, lengths)
    group, longest = min(rows, len(lengths)), max(lengths)

    def fit(vectors):
        return jnp.pad(vectors, ((0, 0), (0, 0), (0, longest - vectors.shape[2])))

    small = jnp.concatenate(
        [fit(conv_full), fit(gain_full.reshape(owners, 1, gate_here))]
        + [fit(norm_grad.reshape(owners, 1, rows)), fit(heads_rows)],
        1,
    )
    sets = -(-len(lengths) // group)
    small = jnp.pad(small, ((0, 0), (0, sets * group - len(lengths)), (0, 0)))
    small = jnp.concatenate([small[:, g * group : (g + 1) * group] for g in range(sets)], 2)
    small = jnp.pad(
        small,
        ((0, 0), (0, rows - group), (heads_here, LANES - heads_here - small.shape[2])),
    ).astype(BF16)
    near_small = reduce_near(small.reshape(dp_n, -1, LANES))
    near_late = near_late + jnp.pad(near_small, ((0, 0), (0, 0), (channels, 0)))
    late = reduce_far(near_late)
    own_out = early[:, width:]
    own_out = jnp.concatenate(
        [own_out[k * out_rows : (k + 1) * out_rows] for k in range(model // width)], 1
    )
    back_pairs = [(target, source) for source, target in to_heads]
    grad_out_w = lax.ppermute(own_out, ("dp", "seq"), back_pairs)
    dn_parts = [swap(p, "seq", k) if k else p for k, p in enumerate(dn_pieces)]
    d_normed = tree_sum([p.astype(F32) for p in dn_parts])

    both = jnp.concatenate([late, early[:, :width]], 1).reshape(seq_n, rows, cols + width)
    parts = scatter_xor(both.astype(BF16), "seq")
    short = [((CONV, conv_here), F32)] + [((1, n), F32) for n in lengths[CONV:]]
    grad_in_w, *short = call(
        finish_kernel(width, inner, heads_here, lengths, small_at),
        [((rows, in_weight.shape[1]), F32)] + short,
        [(seq_n * stride, cols + width)],
        *parts,
    )

    widened = hidden_in[0].astype(F32)
    inverse = lax.rsqrt(jnp.mean(widened * widened, axis=-1, keepdims=True) + EPSILON)
    gain_full_row = tail[:, :, heads_here].reshape(1, -1).astype(F32)
    scaled = d_normed * gain_full_row
    along = jnp.mean(scaled * widened, axis=-1, keepdims=True)
    grad_hidden = out_grad[0].astype(F32) + inverse * (scaled - widened * (inverse * inverse * along))
    return (
        result[None],
        grad_hidden[None],
        short[3][0],
        grad_in_w,
        short[0],
        short[1][0],
        short[4][0],
        short[5][0],
        short[6][0],
        short[2][0],
        grad_out_w,
    )


def solution(mesh):
    in_specs = (
        P("dp", "seq", None),
        P("dp", None),
        P(("dp", "seq")),
        P(("dp", "seq"), None),
        P(None, ("dp", "seq")),
        P(("dp", "seq")),
        P(),
        P(),
        P(),
        P(("dp", "seq")),
        P(("dp", "seq"), None),
        P("dp", "seq", None),
    )
    out_specs = (
        P("dp", "seq", None),
        P("dp", "seq", None),
        P(("dp", "seq")),
        P(("dp", "seq"), None),
        P(None, ("dp", "seq")),
        P(("dp", "seq")),
        P(),
        P(),
        P(),
        P(("dp", "seq")),
        P(("dp", "seq"), None),
    )

    return jax.shard_map(
        on_device, mesh=mesh, in_specs=in_specs, out_specs=out_specs, check_vma=False
    )
```

```python
import jax
import jax.numpy as jnp
from jax import lax
from jax.experimental import pallas as pl
from jax.experimental.pallas import tpu as pltpu
from jax.sharding import PartitionSpec as P

HEAD_DIM = 64
STATE = 128
CONV = 4
CHUNK = 128
VMEM_LIMIT = 56 * 2**20
LANES = 128
EPSILON = 1e-05
FULL = lax.Precision.HIGHEST
MOST = lax.Precision.HIGH
F32 = jnp.float32
BF16 = jnp.bfloat16


def swap(x, axis, offset):
    count = lax.axis_size(axis)
    return lax.ppermute(x, axis, [(i, i ^ offset) for i in range(count)])


def tree_sum(parts):
    while len(parts) > 1:
        parts = [parts[i] + parts[i + 1] for i in range(0, len(parts), 2)]
    return parts[0]


def in_order(pieces, place):
    stacked = jnp.stack(pieces)
    return [lax.dynamic_index_in_dim(stacked, j ^ place, 0, False) for j in range(len(pieces))]


def gather_xor(x, axis):
    return [x] + [swap(x, axis, k) for k in range(1, lax.axis_size(axis))]


def scatter_xor(blocks, axis):
    place = lax.axis_index(axis)
    return [
        swap(lax.dynamic_index_in_dim(blocks, place ^ k, 0, False), axis, k)
        if k
        else lax.dynamic_index_in_dim(blocks, place, 0, False)
        for k in range(lax.axis_size(axis))
    ]


def inner_of(count):
    inner = 1
    while 2 * inner * inner < count:
        inner *= 2
    return inner


def far_offsets():
    count = lax.axis_size("dp")
    inner = inner_of(count)
    return [k * inner for k in range(1, count // inner)]


def gather_far(x):
    return [x] + [swap(x, "dp", k) for k in far_offsets()]


def gather_near(far):
    inner = inner_of(lax.axis_size("dp"))
    near = [[piece] + [swap(piece, "dp", j) for j in range(1, inner)] for piece in far]
    return [piece for group in near for piece in group]


def reduce_slabs(slabs):
    parts = [swap(p, "dp", j) if j else p for j, p in enumerate(slabs)]
    return tree_sum([p.astype(F32) for p in parts]).astype(BF16)


def reduce_near(grads):
    count = lax.axis_size("dp")
    inner = inner_of(count)
    inner_place = lax.axis_index("dp") % inner
    shaped = grads.reshape(count // inner, inner, *grads.shape[1:])
    parts = []
    for j in range(inner):
        slab = lax.dynamic_index_in_dim(shaped, inner_place ^ j, 1, False)
        parts.append(swap(slab, "dp", j) if j else slab)
    return tree_sum([p.astype(F32) for p in parts]).astype(BF16)


def reduce_far(near):
    outer_place = lax.axis_index("dp") // inner_of(lax.axis_size("dp"))
    parts = [lax.dynamic_index_in_dim(near, outer_place, 0, False)]
    for k, offset in enumerate(far_offsets()):
        slab = lax.dynamic_index_in_dim(near, outer_place ^ (k + 1), 0, False)
        parts.append(swap(slab, "dp", offset))
    return tree_sum([p.astype(F32) for p in parts])


def dot(a, b, ca, cb, precision=None):
    return lax.dot_general(
        a, b, (((ca,), (cb,)), ((), ())), precision=precision, preferred_element_type=F32
    )


def exact(a, b):
    return dot(a, b, 1, 0, FULL)


def mm(a, b):
    return dot(a, b, 1, 0, MOST)


def mm_nt(a, b):
    return dot(a, b, 1, 1, MOST)


def mm_tn(a, b):
    return dot(a, b, 0, 0, MOST)


def softplus(x):
    small = jnp.exp(-jnp.abs(x))
    up = 1.0 + small
    down = up - 1.0
    log1p = jnp.where(down == 0.0, small, jnp.log(up) * (small / jnp.where(down == 0.0, 1.0, down)))
    return jnp.maximum(x, 0.0) + log1p


def expand_matrix(width):
    head = lax.broadcasted_iota(jnp.int32, (LANES, width), 0)
    column = lax.broadcasted_iota(jnp.int32, (LANES, width), 1)
    return (column // HEAD_DIM == head).astype(F32)


def triangle(lower):
    row = lax.broadcasted_iota(jnp.int32, (CHUNK, CHUNK), 0)
    column = lax.broadcasted_iota(jnp.int32, (CHUNK, CHUNK), 1)
    return row >= column if lower else row <= column


def head_rows(bias_ref, decay_ref, skip_ref, heads_here):
    rows = jnp.concatenate([bias_ref[...], decay_ref[...], skip_ref[...]], 0)
    count = rows.shape[1]
    rows = jnp.concatenate([rows, jnp.zeros((3, LANES - count), F32)], 1)
    rows = jnp.concatenate([rows, jnp.zeros((5, LANES), F32)], 0)
    place = lax.axis_index("seq")
    mine = rows
    for j in range(1, count // heads_here):
        moved = jnp.concatenate([rows[:, j * heads_here :], rows[:, : j * heads_here]], 1)
        mine = jnp.where(place == j, moved, mine)
    return mine


def spread_segments(seg_ref, seg_col, seg_row):
    seg_row[:, : 2 * CHUNK] = jnp.full((8, 2 * CHUNK), -1.0, F32)
    for i in range(seg_ref.shape[1] // CHUNK):
        now = seg_ref[:, i * CHUNK : (i + 1) * CHUNK].astype(F32)
        seg_row[:, (i + 2) * CHUNK : (i + 3) * CHUNK] = jnp.broadcast_to(now, (8, CHUNK))
        seg_col[i * CHUNK : (i + 1) * CHUNK, :] = jnp.broadcast_to(now, (CHUNK, CHUNK)).T


def same_segment(seg_col, back, width):
    now = seg_col[...]
    row = lax.broadcasted_iota(jnp.int32, now.shape, 0)
    same = ((now == pltpu.roll(now, back, 0)) & (row >= back)).astype(F32)
    return jnp.concatenate([same] * (width // LANES), 1)


def masks_of(seg_col, seg_row, i):
    column = seg_col[pl.ds(i * CHUNK, CHUNK), :]

    def row(j):
        return seg_row[:, pl.ds((i + j) * CHUNK, CHUNK)][:1]

    far = (column == row(0)).astype(F32)
    near = (column == row(1)).astype(F32)
    own = (column == row(2)) & triangle(True)
    return far, near, own


def lane_halves():
    lane = lax.broadcasted_iota(jnp.int32, (1, LANES), 1)
    low = (lane < HEAD_DIM).astype(F32)
    return low, 1.0 - low


def rms_inverse(x):
    return lax.rsqrt(jnp.mean(x * x, axis=-1, keepdims=True) + EPSILON)


def gain_row(weights, lane_of_gain):
    tail = weights[:, weights.shape[1] - LANES :]
    pick = (lax.broadcasted_iota(jnp.int32, (8, LANES), 1) == lane_of_gain).astype(BF16)
    return dot(pick, tail, 1, 1)[:1]


def decays(raw, heads):
    step = softplus(raw + heads[0:1])
    return step, step * (-jnp.exp(heads[1:2]))


def spread_heads(columns, low, width):
    pairs = []
    for pair in range(width // LANES):
        first = columns[:, 2 * pair : 2 * pair + 1]
        second = columns[:, 2 * pair + 1 : 2 * pair + 2]
        pairs.append(jnp.where(low > 0.0, first, second))
    return jnp.concatenate(pairs, 1)


def fill_sources(i, v, step, decay, low, vd, vt, ecx):
    cumulative = exact(triangle(True).astype(F32), decay)
    step_x = spread_heads(step, low, v.shape[1])
    cum_x = spread_heads(cumulative, low, v.shape[1])
    last = cum_x[CHUNK - 1 :]
    vd_now = v * step_x
    vd[pl.ds(i * CHUNK, CHUNK), :] = vd_now
    vt[pl.ds((i + 2) * CHUNK, CHUNK), :] = vd_now * jnp.exp(last - cum_x)
    ecx[pl.ds(i * CHUNK + 8, CHUNK), :] = jnp.exp(cum_x)
    return cumulative, step_x, cum_x, last


def head_decay(cumulative, cumulative_t, own, h):
    gap = cumulative[:, h : h + 1] - cumulative_t[h : h + 1, :]
    return jnp.exp(jnp.where(own, gap, -1e30))


def put_in_order(pieces, place, target, source=None, lanes=None):
    for m, piece in enumerate(pieces):
        source_rows = slice(0, piece.shape[0]) if source is None else source
        rows = source_rows.stop - source_rows.start
        start = pl.multiple_of((place ^ m) * rows, rows)
        if lanes is None:
            target[pl.ds(start, rows), :] = piece[...]
        else:
            target[pl.ds(start, rows), lanes[0]] = piece[source_rows, lanes[1]]


def dp_index(pieces):
    return lax.axis_index("dp") if len(pieces) > 1 else 0


def put_second(pieces, place, wg_ref=None, wo_ref=None):
    rows, both = pieces[0].shape
    width = both // 2
    if wg_ref is not None:
        put_in_order(pieces, place, wg_ref, slice(0, rows), (slice(0, width), slice(0, width)))
    if wo_ref is not None:
        folds = wo_ref.shape[1] // width
        part = rows // folds
        for k in range(folds):
            to = (slice(k * width, (k + 1) * width), slice(width, 2 * width))
            put_in_order(pieces, place, wo_ref, slice(k * part, (k + 1) * part), to)


def small_spots(rows, lengths):
    group = min(rows, len(lengths))
    return [(i % group, (i // group) * max(lengths)) for i in range(len(lengths))]


def store_slabs(values, outs, lanes):
    if len(outs[0].shape) == 2:
        outs[0][...] = values[:, lanes].astype(BF16)
        return
    inner, (outer, rows, _) = len(outs), outs[0].shape
    place = lax.axis_index("dp") % inner if inner > 1 else 0
    for j, out in enumerate(outs):
        for o in range(outer):
            start = (o * inner + (place ^ j)) * rows
            if inner > 1:
                start = pl.multiple_of(start, rows)
            out[o] = values[pl.ds(start, rows), lanes].astype(BF16)


def store_far(values, outs):
    if len(outs) == 1:
        outs[0][...] = values[...].astype(BF16)
        return
    rows = outs[0].shape[0]
    inner = inner_of(lax.axis_size("dp"))
    for k, out in enumerate(outs):
        start = pl.multiple_of(((lax.axis_index("dp") // inner) ^ k) * rows, rows)
        out[...] = values[pl.ds(start, rows), :].astype(BF16)


def store_pieces(values, outs, behind=0):
    rows = outs[0].shape[0] - behind
    for k, out in enumerate(outs):
        start = pl.multiple_of((lax.axis_index("seq") ^ k) * rows, rows)
        out[behind:, :] = values[pl.ds(start, rows), :].astype(BF16)


def finish_kernel(width, inner, heads_here, lengths, spots):
    def body(*refs):
        count = inner // width
        parts, refs = refs[:count], refs[count:]
        grad_ref, outs, blocks = refs[0], refs[1:-1], refs[-1]
        rows = grad_ref.shape[0]
        stride = blocks.shape[0] // count
        states, tail = width, width + 2 * STATE
        for k, part in enumerate(parts):
            start = pl.multiple_of((lax.axis_index("seq") ^ k) * stride, stride)
            blocks[pl.ds(start, rows), :] = part[...].astype(F32)
        steps = []
        for j in range(count):
            at = slice(j * stride, j * stride + rows)
            grad_ref[:, j * width : (j + 1) * width] = blocks[at, tail + LANES :]
            grad_ref[:, inner + j * width : inner + (j + 1) * width] = blocks[at, :width]
            steps.append(blocks[at, tail : tail + heads_here])
        both = tree_sum([part[:, states:tail].astype(F32) for part in parts])
        grad_ref[:, 2 * inner : 2 * inner + 2 * STATE] = both
        grad_ref[:, 2 * inner + 2 * STATE :] = jnp.concatenate(steps, 1)
        total = tree_sum([part[:, tail : tail + LANES].astype(F32) for part in parts])
        found = []
        for length, (row, lane) in zip(lengths, spots):
            first = heads_here + lane
            found.append(total[row : row + 1, first : first + length])
        outs[0][...] = jnp.concatenate(found[:CONV], 0)
        for out, vector in zip(outs[1:], found[CONV:]):
            out[...] = vector

    return body


def pack_kernel(width, inner, heads_here, count):
    def body(w_ref, taps_ref, shift_ref, gate_ref, norm_ref, *refs):
        outs, blocks = refs[:-1], refs[-1]
        rows = w_ref.shape[0]
        stride = blocks.shape[0] // count
        states = 2 * inner + 2 * STATE
        norm = jnp.concatenate([norm_ref[...].astype(F32), jnp.zeros((1, LANES - rows), F32)], 1)
        column = jnp.broadcast_to(norm, (LANES, LANES)).T[:rows]
        taps = taps_ref[...].astype(F32)
        vectors = [taps[i : i + 1] for i in range(CONV)]
        vectors += [shift_ref[...].astype(F32), gate_ref[...].astype(F32)]
        spots = small_spots(rows, [v.shape[1] for v in vectors])
        lane = lax.broadcasted_iota(jnp.int32, (rows, LANES), 1)
        row = lax.broadcasted_iota(jnp.int32, (rows, LANES), 0)
        shared = jnp.where(lane == heads_here, column, 0.0)
        for vector, (at_row, at_lane) in zip(vectors, spots):
            start = heads_here + 1 + at_lane
            pieces = [jnp.zeros((1, start), F32), vector]
            pieces.append(jnp.zeros((1, LANES - start - vector.shape[1]), F32))
            shared = shared + jnp.where(row == at_row, jnp.concatenate(pieces, 1), 0.0)
        for j in range(count):
            at = slice(j * stride, j * stride + rows)
            first = states + j * heads_here
            blocks[at, :width] = w_ref[:, inner + j * width : inner + (j + 1) * width].astype(F32)
            blocks[at, width : width + 2 * STATE] = w_ref[:, 2 * inner : states].astype(F32)
            steps = w_ref[:, first : first + heads_here].astype(F32)
            tail = jnp.concatenate([steps, shared[:, heads_here:]], 1)
            blocks[at, width + 2 * STATE : width + 2 * STATE + LANES] = tail
            gate = w_ref[:, j * width : (j + 1) * width].astype(F32)
            blocks[at, width + 2 * STATE + LANES :] = gate
        for k in range(count):
            start = pl.multiple_of((lax.axis_index("seq") ^ k) * stride, stride)
            outs[k][...] = blocks[pl.ds(start, rows), :].astype(BF16)

    return body


def forward_kernel(width, lane_of_gain, x_count, w_count):
    heads_here = width // HEAD_DIM

    def body(*refs):
        x_pieces, refs = refs[:x_count], refs[x_count:]
        w_pieces, refs = refs[:w_count], refs[w_count:]
        conv_ref, seg_ref, bias_ref, decay_ref, skip_ref, normed_ref, proj_ref, pre_ref, y_ref, bpad, vd, vt, ecx, seg_col, seg_row, x_ref, w_ref = refs
        put_in_order(x_pieces, lax.axis_index("seq"), x_ref)
        put_in_order(w_pieces, dp_index(w_pieces), w_ref)
        x = x_ref[...].astype(F32)
        gain = gain_row(w_ref[...], lane_of_gain)
        normed_ref[...] = (x * rms_inverse(x) * gain).astype(BF16)
        proj_ref[...] = dot(normed_ref[...], w_ref[...], 1, 0)
        spread_segments(seg_ref, seg_col, seg_row)
        channels = width + 2 * STATE
        u = proj_ref[:, :channels]
        running = conv_ref[CONV : CONV + 1, :] + conv_ref[CONV - 1 : CONV, :] * u
        for back in range(1, CONV):
            tap = conv_ref[CONV - 1 - back : CONV - back, :]
            running = running + tap * pltpu.roll(u, back, 0) * same_segment(seg_col, back, channels)
        pre_ref[...] = running
        bpad[pl.ds(0, 2 * CHUNK), :] = jnp.zeros((2 * CHUNK, STATE), F32)
        vt[pl.ds(0, 2 * CHUNK), :] = jnp.zeros((2 * CHUNK, width), F32)
        ecx[pl.ds(0, 8), :] = jnp.zeros((8, width), F32)
        b_pre = running[:, width : width + STATE]
        bpad[pl.ds(2 * CHUNK, x.shape[0]), :] = b_pre * jax.nn.sigmoid(b_pre)
        expand = expand_matrix(width)
        low, high = lane_halves()
        heads = head_rows(bias_ref, decay_ref, skip_ref, heads_here)
        skip_x = exact(jnp.broadcast_to(heads[2:3], (8, LANES)), expand)[:1]

        def chunk(i, carry):
            rows = pl.ds(i * CHUNK, CHUNK)
            v_pre = pre_ref[rows, :width]
            c_pre = pre_ref[rows, width + STATE :]
            v = v_pre * jax.nn.sigmoid(v_pre)
            c = c_pre * jax.nn.sigmoid(c_pre)
            step, decay = decays(proj_ref[rows, channels:], heads)
            cumulative, _, _, _ = fill_sources(i, v, step, decay, low, vd, vt, ecx)
            cumulative_t = cumulative.T
            far, near, own = masks_of(seg_col, seg_row, i)
            window = pl.ds(i * CHUNK, 3 * CHUNK)
            scores = mm_nt(c, bpad[window, :])
            s_far = scores[:, :CHUNK] * far
            s_near = scores[:, CHUNK : 2 * CHUNK] * near
            s_own = scores[:, 2 * CHUNK :]
            ecx_now = ecx[pl.ds(i * CHUNK + 8, CHUNK), :]
            last_before = ecx[pl.ds(i * CHUNK, 8), :][7:8]
            vt_far = vt[rows, :] * last_before
            vt_near = vt[pl.ds((i + 1) * CHUNK, CHUNK), :]
            off = mm(s_far, vt_far) + mm(s_near, vt_near)
            y_ref[rows, :] = off * ecx_now + skip_x * v
            for pair in range(heads_here // 2):
                lanes = slice(pair * LANES, (pair + 1) * LANES)
                n0 = s_own * head_decay(cumulative, cumulative_t, own, 2 * pair)
                n1 = s_own * head_decay(cumulative, cumulative_t, own, 2 * pair + 1)
                vp = vd[rows, lanes]
                both = mm(jnp.concatenate([n0, n1], 1), jnp.concatenate([vp * low, vp * high], 0))
                y_ref[rows, lanes] = y_ref[rows, lanes] + both
            return carry

        for turn in range(x.shape[0] // CHUNK):
            chunk(turn, 0)

    return body


def gate_kernel(og_count, w_count):
    def body(*refs):
        og_pieces, refs = refs[:og_count], refs[og_count:]
        w_pieces, refs = refs[:w_count], refs[w_count:]
        normed_ref, y_ref, gain_ref, gate_ref, dg_ref, stats_ref, og_ref, wg_ref, wo_ref = refs
        put_in_order(og_pieces, lax.axis_index("seq"), og_ref)
        put_second(w_pieces, dp_index(w_pieces), wg_ref, wo_ref)
        gate = dot(normed_ref[...], wg_ref[...], 1, 0)
        gate_ref[...] = gate
        d_gated = dot(og_ref[...], wo_ref[...], 1, 1)
        dg_ref[...] = d_gated
        v = y_ref[...] * (gate * jax.nn.sigmoid(gate))
        squares = jnp.sum(v * v, axis=1, keepdims=True)
        cross = jnp.sum(v * (d_gated * gain_ref[...]), axis=1, keepdims=True)
        lane = lax.broadcasted_iota(jnp.int32, (CHUNK, LANES), 1)
        for i in range(stats_ref.shape[0]):
            rows = slice(i * CHUNK, (i + 1) * CHUNK)
            both = jnp.where(lane == 0, squares[rows], jnp.where(lane == 1, cross[rows], 0.0))
            stats_ref[i] = both.T[:8]

    return body


def out_kernel(width, whole_width, og_count, w_count, slab_count, block_rows):
    def body(*refs):
        og_pieces, refs = refs[:og_count], refs[og_count:]
        w_pieces, refs = refs[:w_count], refs[w_count:]
        stats, refs = refs[:og_count], refs[og_count:]
        normed_ref, gate_ref, dg_ref, y_ref, gain_ref = refs[:5]
        out_refs, refs = refs[5 : 5 + og_count], refs[5 + og_count :]
        slabs, refs = refs[:slab_count], refs[slab_count:]
        dgate_ref, dy_ref, ggain_ref, og_ref, wo_ref, out_all, grad_all = refs
        put_in_order(og_pieces, lax.axis_index("seq"), og_ref)
        put_second(w_pieces, dp_index(w_pieces), None, wo_ref)
        columns = []
        for i in range(stats[0].shape[0]):
            total = tree_sum([part[i] for part in stats])
            square = jnp.concatenate([total, jnp.zeros((CHUNK - 8, LANES), F32)], 0)
            columns.append(square.T)
        columns = jnp.concatenate(columns, 0)
        inverse = lax.rsqrt(columns[:, 0:1] / whole_width + EPSILON)
        cross = columns[:, 1:2] / whole_width
        gate = gate_ref[...]
        sig = jax.nn.sigmoid(gate)
        silu = gate * sig
        y = y_ref[...]
        v = y * silu
        gain = gain_ref[...]
        scaled = v * inverse
        gated = (scaled * gain).astype(BF16)
        out_all[...] = dot(gated, wo_ref[...], 1, 0)
        store_pieces(out_all, out_refs)
        rows = block_rows
        folds = og_ref.shape[1] // width
        part = rows // folds
        g_out = dot(gated, og_ref[...], 0, 0)
        for d in range(grad_all.shape[0] // rows):
            for k in range(folds):
                to = slice(d * rows + k * part, d * rows + (k + 1) * part)
                grad_all[to, width:] = g_out[d * part : (d + 1) * part, k * width : (k + 1) * width]
        d_gated = dg_ref[...]
        ggain_ref[...] = jnp.broadcast_to(jnp.sum(d_gated * scaled, axis=0, keepdims=True), (8, width))
        dv = inverse * (d_gated * gain - v * (inverse * inverse * cross))
        dy_ref[...] = dv * silu
        dgate = (dv * y * (sig * (1.0 + gate * (1.0 - sig)))).astype(BF16)
        dgate_ref[...] = dgate
        grad_all[:, :width] = dot(normed_ref[...], dgate, 0, 0)
        store_far(grad_all, slabs)

    return body


def mixer_back_kernel(width):
    heads_here = width // HEAD_DIM

    def body(conv_ref, seg_ref, bias_ref, decay_ref, skip_ref, proj_ref, pre_ref, y_ref, dy_ref, dconv_ref, draw, conv_grad_ref, head_grad_ref, bpad, vd, vt, ecx, seg_col, seg_row, tailx, stepx, cums, ua, db, dpre):
        length = proj_ref.shape[0]
        spread_segments(seg_ref, seg_col, seg_row)
        chunks = length // CHUNK
        channels = width + 2 * STATE
        expand = expand_matrix(width)
        low, high = lane_halves()
        heads = head_rows(bias_ref, decay_ref, skip_ref, heads_here)
        rate = jnp.exp(heads[1:2])
        skip_x = exact(jnp.broadcast_to(heads[2:3], (8, LANES)), expand)[:1]
        bpad[pl.ds(0, 2 * CHUNK), :] = jnp.zeros((2 * CHUNK, STATE), F32)
        vt[pl.ds(0, 2 * CHUNK), :] = jnp.zeros((2 * CHUNK, width), F32)
        tailx[pl.ds(0, 2 * CHUNK), :] = jnp.zeros((2 * CHUNK, width), F32)
        ecx[pl.ds(0, 8), :] = jnp.zeros((8, width), F32)
        b_pre = pre_ref[:, width : width + STATE]
        bpad[pl.ds(2 * CHUNK, length), :] = b_pre * jax.nn.sigmoid(b_pre)
        ua[...] = jnp.zeros(ua.shape, F32)
        db[...] = jnp.zeros(db.shape, F32)

        def prepare(i, carry):
            rows = pl.ds(i * CHUNK, CHUNK)
            v_pre = pre_ref[rows, :width]
            v = v_pre * jax.nn.sigmoid(v_pre)
            step, decay = decays(proj_ref[rows, channels:], heads)
            cumulative, step_x, cum_x, last = fill_sources(i, v, step, decay, low, vd, vt, ecx)
            cums[rows, :] = cumulative
            stepx[rows, :] = step_x
            tailx[pl.ds((i + 2) * CHUNK, CHUNK), :] = jnp.exp(last - cum_x)
            return carry

        for turn in range(chunks):
            prepare(turn, 0)

        def chunk(turn, carry):
            later, g_bias, g_rate, g_skip = carry
            i = chunks - 1 - turn
            rows = pl.ds(i * CHUNK, CHUNK)
            rows_near = pl.ds((i + 1) * CHUNK, CHUNK)
            rows_own = pl.ds((i + 2) * CHUNK, CHUNK)
            window = pl.ds(i * CHUNK, 3 * CHUNK)
            v_pre = pre_ref[rows, :width]
            v_sig = jax.nn.sigmoid(v_pre)
            v = v_pre * v_sig
            c_pre = pre_ref[rows, width + STATE :]
            c_sig = jax.nn.sigmoid(c_pre)
            c = c_pre * c_sig
            raw = proj_ref[rows, channels:]
            step, decay = decays(raw, heads)
            cumulative = cums[rows, :]
            cumulative_t = cumulative.T
            far, near, own = masks_of(seg_col, seg_row, i)
            b_window = bpad[window, :]
            scores = mm_nt(c, b_window)
            s_far = scores[:, :CHUNK] * far
            s_near = scores[:, CHUNK : 2 * CHUNK] * near
            s_own = scores[:, 2 * CHUNK :]
            dy = dy_ref[rows, :]
            dye = dy * ecx[pl.ds(i * CHUNK + 8, CHUNK), :]
            dye_far = dye * ecx[pl.ds(i * CHUNK, 8), :][7:8]
            ds_far = mm_nt(dye_far, vt[rows, :]) * far
            ds_near = mm_nt(dye, vt[rows_near, :]) * near
            ua[rows, :] = ua[rows, :] + tailx[rows, :] * mm_tn(s_far, dye_far)
            ua[rows_near, :] = ua[rows_near, :] + tailx[rows_near, :] * mm_tn(s_near, dye)
            ds_own = jnp.zeros((CHUNK, CHUNK), F32)
            for pair in range(heads_here // 2):
                lanes = slice(pair * LANES, (pair + 1) * LANES)
                d0 = head_decay(cumulative, cumulative_t, own, 2 * pair)
                d1 = head_decay(cumulative, cumulative_t, own, 2 * pair + 1)
                dyp = dy_ref[rows, lanes]
                split = jnp.concatenate([dyp * low, dyp * high], 0)
                dm = mm_nt(split, vd[rows, lanes])
                ds_own = ds_own + dm[:CHUNK] * d0 + dm[CHUNK:] * d1
                u_pair = mm_tn(jnp.concatenate([s_own * d0, s_own * d1], 0), split)
                ua[rows_own, lanes] = ua[rows_own, lanes] + u_pair
            ds_all = jnp.concatenate([ds_far, ds_near, ds_own], 1)
            dc = mm(ds_all, b_window)
            db[window, :] = db[window, :] + mm_tn(ds_all, c)
            u_total = ua[rows_own, :]
            received = mm_nt(dy * (y_ref[rows, :] - skip_x * v), expand)
            d_step = mm_nt(v * u_total, expand)
            gap = received - step * d_step
            d_decay = exact(triangle(False).astype(F32), gap) + later
            d_step = d_step - d_decay * rate
            d_raw = d_step * jax.nn.sigmoid(raw + heads[0:1])
            draw[rows, :] = d_raw.astype(BF16)
            dv = stepx[rows, :] * u_total + skip_x * dy
            dpre[rows, :width] = dv * (v_sig * (1.0 + v_pre * (1.0 - v_sig)))
            b_pre = pre_ref[rows, width : width + STATE]
            b_sig = jax.nn.sigmoid(b_pre)
            dpre[rows, width : width + STATE] = db[rows_own, :] * (b_sig * (1.0 + b_pre * (1.0 - b_sig)))
            dpre[rows, width + STATE :] = dc * (c_sig * (1.0 + c_pre * (1.0 - c_sig)))
            g_skip = g_skip + jnp.sum(dy * v, axis=0, keepdims=True)
            g_bias = g_bias + jnp.sum(d_raw, axis=0, keepdims=True)
            g_rate = g_rate + jnp.sum(d_decay * decay, axis=0, keepdims=True)
            return (later + jnp.sum(gap, axis=0, keepdims=True), g_bias, g_rate, g_skip)

        none = jnp.zeros((1, LANES), F32)
        none_wide = jnp.zeros((1, heads_here * HEAD_DIM), F32)
        start = (none, none, none, none_wide)
        state = start
        for turn in range(chunks):
            state = chunk(turn, state)
        _, g_bias, g_rate, g_skip = state
        g_skip = dot(jnp.broadcast_to(g_skip, (8, g_skip.shape[1])), expand, 1, 1, FULL)[:1]
        head_grad_ref[...] = jnp.concatenate([g_bias, g_rate, g_skip, jnp.zeros((5, LANES), F32)], 0)
        u = proj_ref[:, :channels]
        d = dpre[...]
        du = conv_ref[CONV - 1 : CONV, :] * d
        taps = [jnp.sum(d * u, axis=0, keepdims=True)]
        for back in range(1, CONV):
            masked = d * same_segment(seg_col, back, channels)
            taps.insert(0, jnp.sum(masked * pltpu.roll(u, back, 0), axis=0, keepdims=True))
            du = du + conv_ref[CONV - 1 - back : CONV - back, :] * pltpu.roll(masked, length - back, 0)
        taps.append(jnp.sum(d, axis=0, keepdims=True))
        taps.append(jnp.zeros((8 - CONV - 1, channels), F32))
        conv_grad_ref[...] = jnp.concatenate(taps, 0)
        dconv_ref[...] = du.astype(BF16)

    return body


def weight_back_kernel(x_count, w_count, slab_count):
    def body(*refs):
        x_pieces, refs = refs[:x_count], refs[x_count:]
        w_pieces, refs = refs[:w_count], refs[w_count:]
        g_pieces, refs = refs[:w_count], refs[w_count:]
        out_parts, refs = refs[:x_count], refs[x_count:]
        normed_ref, dconv_ref, draw_ref, dgate_ref = refs[:4]
        slabs, refs = refs[4 : 4 + slab_count], refs[4 + slab_count :]
        dn_refs, refs = refs[:x_count], refs[x_count:]
        norm_grad_ref, x_ref, w_ref, wg_ref, dn_all, gin_ref = refs
        put_in_order(x_pieces, lax.axis_index("seq"), x_ref)
        put_in_order(w_pieces, dp_index(w_pieces), w_ref)
        put_second(g_pieces, dp_index(w_pieces), wg_ref)
        channels = dconv_ref.shape[1]
        dconv, draw = dconv_ref[...], draw_ref[...]
        dn = dot(dconv, w_ref[:, :channels], 1, 1) + dot(draw, w_ref[:, channels:], 1, 1)
        dn = dn + dot(dgate_ref[...], wg_ref[...], 1, 1)
        dn_all[...] = dn
        store_pieces(dn_all, dn_refs, out_parts[0].shape[0])
        for out_part, both_ref in zip(out_parts, dn_refs):
            both_ref[: out_part.shape[0], :] = out_part[...]
        gin_ref[:, :channels] = dot(normed_ref[...], dconv, 0, 0)
        x = x_ref[...].astype(F32)
        along = jnp.sum(dn * (x * rms_inverse(x)), axis=0, keepdims=True)
        norm_grad_ref[...] = along
        gin_ref[:, channels:] = dot(normed_ref[...], draw, 0, 0)
        half = gin_ref.shape[1] // 2
        store_slabs(gin_ref, slabs[: slab_count // 2], slice(0, half))
        store_slabs(gin_ref, slabs[slab_count // 2 :], slice(half, 2 * half))

    return body


def call(body, outs, scratch, *operands):
    vmem = pl.BlockSpec(memory_space=pltpu.VMEM)
    return pl.pallas_call(
        body,
        out_shape=[jax.ShapeDtypeStruct(shape, kind) for shape, kind in outs],
        in_specs=[vmem] * len(operands),
        out_specs=[vmem] * len(outs),
        scratch_shapes=[
            pltpu.VMEM(*shape) if isinstance(shape[0], tuple) else pltpu.VMEM(shape, F32)
            for shape in scratch
        ],
        compiler_params=pltpu.CompilerParams(vmem_limit_bytes=VMEM_LIMIT),
    )(*operands)


def on_device(
    hidden_in,
    segments,
    norm_gain,
    in_weight,
    conv_weight,
    conv_bias,
    step_bias,
    decay_log,
    skip_weight,
    gate_gain,
    out_weight,
    out_grad,
):
    row_count, piece, model = hidden_in.shape
    assert row_count == 1
    seq_n, dp_n = lax.axis_size("seq"), lax.axis_size("dp")
    owners = seq_n * dp_n
    place, dp_place = lax.axis_index("seq"), lax.axis_index("dp")
    length = piece * seq_n
    head_count = step_bias.shape[0]
    inner = head_count * HEAD_DIM
    heads_here = head_count // seq_n
    width = inner // seq_n
    channels = width + 2 * STATE
    cols = channels + LANES
    rows = in_weight.shape[0]
    conv_here = conv_bias.shape[0]
    gate_here = gate_gain.shape[0]

    stride = -(-rows // 16) * 16
    blocks = call(
        pack_kernel(width, inner, heads_here, seq_n),
        [((rows, cols + width), BF16)] * seq_n,
        [(seq_n * stride, cols + width)],
        in_weight, conv_weight, conv_bias[None], gate_gain[None], norm_gain[None],
    )
    blocks = [b if k == 0 else swap(b, "seq", k) for k, b in enumerate(blocks)]
    mine = jnp.concatenate(in_order(blocks, place), 0)
    first_part, gate_part = mine[:, :cols], mine[:, cols:]
    far_first = gather_far(first_part)
    x_pieces = gather_xor(hidden_in[0], "seq")
    og_pieces = gather_xor(out_grad[0], "seq")

    def linear(d, s):
        return d * seq_n + s

    to_heads = [(b, linear(b % dp_n, b // dp_n)) for b in range(owners)]
    out_block = lax.ppermute(out_weight, ("dp", "seq"), to_heads)
    out_rows = out_block.shape[0]
    folded = jnp.concatenate(
        [out_block[:, k * width : (k + 1) * width] for k in range(model // width)], 0
    )
    second = jnp.concatenate([gate_part, folded], 1)
    far_second = gather_far(second)
    w_first = gather_near(far_first)
    w_second = gather_near(far_second)
    split_here = not out_rows % 16
    if not split_here:
        w_first = [jnp.concatenate(in_order(w_first, dp_place), 0)]
        w_second = in_order(w_second, dp_place)
        folds = [slice(k * out_rows, (k + 1) * out_rows) for k in range(model // width)]
        w_out = jnp.concatenate([p[f, width:] for f in folds for p in w_second], 0)
        w_second = [
            jnp.concatenate([jnp.concatenate([p[:, :width] for p in w_second], 0), w_out], 1)
        ]
    if len(w_first) > 1:
        tail = jnp.concatenate(in_order([p[:, channels:] for p in w_first], dp_place), 0)
    else:
        tail = w_first[0][:, channels:]
    tail = tail.reshape(owners, rows, LANES)
    lengths = [conv_here] * (CONV + 1) + [gate_here]
    spots = small_spots(rows, lengths)
    if rows >= len(lengths):
        conv_all = tail[:, : CONV + 1, heads_here + 1 : heads_here + 1 + conv_here]
        conv_all = conv_all.transpose(1, 0, 2).reshape(CONV + 1, owners * conv_here)
    else:
        conv_all = []
        for r, lane in spots[: CONV + 1]:
            first = heads_here + 1 + lane
            conv_all.append(tail[:, r, first : first + conv_here].reshape(1, -1))
        conv_all = jnp.concatenate(conv_all, 0)
    conv_mine = jnp.concatenate(
        [
            lax.dynamic_slice_in_dim(conv_all[:, :inner], place * width, width, 1),
            conv_all[:, inner:],
        ],
        1,
    )
    conv_mine = jnp.pad(conv_mine.astype(F32), ((0, 8 - CONV - 1), (0, 0)))
    first = heads_here + 1 + spots[-1][1]
    gain_all = tail[:, spots[-1][0], first : first + gate_here]
    gain_mine = lax.dynamic_slice_in_dim(gain_all.reshape(1, inner), place * width, width, 1)
    gain_mine = gain_mine.astype(F32)

    head_params = (step_bias[None], decay_log[None], skip_weight[None])

    chunks = length // CHUNK
    tall = length + 2 * CHUNK
    sources = [(tall, STATE), (length, width), (tall, width), (length + 8, width)]
    sources += [(length, LANES), (8, tall)]
    normed, proj, pre, y = call(
        forward_kernel(width, heads_here, len(x_pieces), len(w_first)),
        [((length, model), BF16)]
        + [((length, cols), F32), ((length, channels), F32), ((length, width), F32)],
        sources + [((length, model), BF16), ((model, cols), BF16)],
        *x_pieces, *w_first, conv_mine, segments, *head_params,
    )
    og_scratch, wg_scratch = ((length, model), BF16), ((model, width), BF16)
    wo_scratch = ((width, model), BF16)
    gate, d_gated, stats = call(
        gate_kernel(len(og_pieces), len(w_second)),
        [((length, width), F32), ((length, width), F32), ((chunks, 8, LANES), F32)],
        [og_scratch, wg_scratch, wo_scratch],
        *og_pieces, *w_second, normed, y, gain_mine,
    )
    stats = gather_xor(stats, "seq")
    block_rows = rows * seq_n
    dp_inner = inner_of(dp_n)
    dp_outer = dp_n // dp_inner
    half = cols // 2
    if split_here:
        halves = [((dp_outer, block_rows, half), BF16)] * dp_inner
        far_blocks = [((dp_inner * block_rows, 2 * width), BF16)] * dp_outer
    else:
        halves = [((model, half), BF16)]
        far_blocks = [((model, 2 * width), BF16)]
    pieces = [((piece, model), BF16)] * seq_n

    def near_sum(made):
        if split_here:
            return reduce_slabs(made)
        return reduce_near(made[0].reshape(dp_n, -1, made[0].shape[-1]))

    def far_sum(made):
        if not split_here:
            outer_place = dp_place // dp_inner
            blocks = made[0].reshape(dp_outer, dp_inner * block_rows, 2 * width)
            made = [
                lax.dynamic_index_in_dim(blocks, outer_place ^ k, 0, False)
                for k in range(dp_outer)
            ]
        parts = [made[0]]
        for k, offset in enumerate(far_offsets()):
            parts.append(swap(made[k + 1], "dp", offset))
        return tree_sum([p.astype(F32) for p in parts]).astype(BF16)

    made = call(
        out_kernel(width, inner, len(og_pieces), len(w_second), len(far_blocks), block_rows),
        pieces + far_blocks
        + [((length, width), BF16), ((length, width), F32), ((8, width), F32)],
        [og_scratch, wo_scratch, (length, model), (model, 2 * width)],
        *og_pieces, *w_second, *stats, normed, gate, d_gated, y, gain_mine,
    )
    out_parts, made = made[:seq_n], made[seq_n:]
    far_early = far_sum(made[: len(far_blocks)])
    d_gate, dy, g_gain = made[len(far_blocks) :]
    dconv, draw, conv_grad, head_grad = call(
        mixer_back_kernel(width),
        [((length, channels), BF16), ((length, LANES), BF16)]
        + [((8, channels), F32), ((8, LANES), F32)],
        sources
        + [(tall, width), (length, width), (length, LANES), (tall, width), (tall, STATE)]
        + [(length, channels)],
        conv_mine, segments, *head_params, proj, pre, y, dy,
    )

    made = call(
        weight_back_kernel(len(x_pieces), len(w_first), 2 * len(halves)),
        halves + halves + [((2 * piece, model), BF16)] * seq_n + [((1, model), F32)],
        [((length, model), BF16), ((model, cols), BF16), wg_scratch, (length, model), (model, cols)],
        *x_pieces, *w_first, *w_second, *out_parts, normed, dconv, draw, d_gate,
    )
    dn_pieces, norm_grad = made[2 * len(halves) : -1], made[-1]
    near_values = near_sum(made[: len(halves)])
    rest = made[len(halves) : 2 * len(halves)]
    conv_full = jnp.zeros((CONV + 1, inner), F32)
    conv_full = lax.dynamic_update_slice_in_dim(
        conv_full, conv_grad[: CONV + 1, :width], place * width, 1
    )
    conv_full = jnp.concatenate([conv_full, conv_grad[: CONV + 1, width:]], 1)
    conv_full = conv_full.reshape(CONV + 1, owners, conv_here).transpose(1, 0, 2)
    gain_full = lax.dynamic_update_slice_in_dim(
        jnp.zeros((inner,), F32), g_gain[0], place * width, 0
    )
    heads_full = lax.dynamic_update_slice_in_dim(
        jnp.zeros((3, head_count), F32), head_grad[:3, :heads_here], place * heads_here, 1
    )
    heads_rows = jnp.broadcast_to(heads_full[None], (owners, 3, head_count))
    lengths = [conv_here] * (CONV + 1) + [gate_here, rows] + [head_count] * 3
    small_at = small_spots(rows, lengths)
    group, longest = min(rows, len(lengths)), max(lengths)

    def fit(vectors):
        return jnp.pad(vectors, ((0, 0), (0, 0), (0, longest - vectors.shape[2])))

    small = jnp.concatenate(
        [fit(conv_full), fit(gain_full.reshape(owners, 1, gate_here))]
        + [fit(norm_grad.reshape(owners, 1, rows)), fit(heads_rows)],
        1,
    )
    sets = -(-len(lengths) // group)
    small = jnp.pad(small, ((0, 0), (0, sets * group - len(lengths)), (0, 0)))
    small = jnp.concatenate([small[:, g * group : (g + 1) * group] for g in range(sets)], 2)
    small = jnp.pad(
        small,
        ((0, 0), (0, rows - group), (heads_here, LANES - heads_here - small.shape[2])),
    ).astype(BF16)
    inner_place = dp_place % dp_inner
    small = small.reshape(dp_outer, dp_inner, block_rows, LANES)
    far_early = far_early.reshape(dp_inner, block_rows, 2 * width)
    if not split_here:
        rest = rest[0].reshape(dp_outer, dp_inner, block_rows, half)
        rest = [lax.dynamic_index_in_dim(rest, inner_place ^ j, 1, False) for j in range(dp_inner)]
    together = []
    for j, slab in enumerate(rest):
        short = lax.dynamic_index_in_dim(small, inner_place ^ j, 1, False)
        slab = slab + jnp.pad(short, ((0, 0), (0, 0), (half - LANES, 0)))
        block = lax.dynamic_index_in_dim(far_early, inner_place ^ j, 0, False)
        block = jnp.stack([block[:, :width], block[:, width:]])
        together.append(jnp.concatenate([slab, block], 0))
    together = [swap(t, "dp", j) if j else t for j, t in enumerate(together)]
    together = tree_sum([t.astype(F32) for t in together])
    near_rest = together[:dp_outer].astype(BF16)
    early = jnp.concatenate([together[dp_outer], together[dp_outer + 1]], 1)
    late = [reduce_far(near_values), reduce_far(near_rest)]
    own_out = early[:, width:]
    own_out = jnp.concatenate(
        [own_out[k * out_rows : (k + 1) * out_rows] for k in range(model // width)], 1
    )
    back_pairs = [(target, source) for source, target in to_heads]
    grad_out_w = lax.ppermute(own_out.astype(BF16), ("dp", "seq"), back_pairs)
    dn_parts = [swap(p, "seq", k) if k else p for k, p in enumerate(dn_pieces)]
    rows_total = tree_sum([p.astype(F32) for p in dn_parts])
    result = hidden_in[0].astype(F32) + rows_total[:piece]
    d_normed = rows_total[piece:]

    both = jnp.concatenate([*late, early[:, :width]], 1).reshape(seq_n, rows, cols + width)
    parts = scatter_xor(both.astype(BF16), "seq")
    short = [((CONV, conv_here), F32)] + [((1, n), F32) for n in lengths[CONV:]]
    grad_in_w, *short = call(
        finish_kernel(width, inner, heads_here, lengths, small_at),
        [((rows, in_weight.shape[1]), F32)] + short,
        [(seq_n * stride, cols + width)],
        *parts,
    )

    widened = hidden_in[0].astype(F32)
    inverse = lax.rsqrt(jnp.mean(widened * widened, axis=-1, keepdims=True) + EPSILON)
    gain_full_row = tail[:, :, heads_here].reshape(1, -1).astype(F32)
    scaled = d_normed * gain_full_row
    along = jnp.mean(scaled * widened, axis=-1, keepdims=True)
    grad_hidden = out_grad[0].astype(F32) + inverse * (scaled - widened * (inverse * inverse * along))
    return (
        result[None],
        grad_hidden[None],
        short[3][0],
        grad_in_w,
        short[0],
        short[1][0],
        short[4][0],
        short[5][0],
        short[6][0],
        short[2][0],
        grad_out_w.astype(F32),
    )


def solution(mesh):
    in_specs = (
        P("dp", "seq", None),
        P("dp", None),
        P(("dp", "seq")),
        P(("dp", "seq"), None),
        P(None, ("dp", "seq")),
        P(("dp", "seq")),
        P(),
        P(),
        P(),
        P(("dp", "seq")),
        P(("dp", "seq"), None),
        P("dp", "seq", None),
    )
    out_specs = (
        P("dp", "seq", None),
        P("dp", "seq", None),
        P(("dp", "seq")),
        P(("dp", "seq"), None),
        P(None, ("dp", "seq")),
        P(("dp", "seq")),
        P(),
        P(),
        P(),
        P(("dp", "seq")),
        P(("dp", "seq"), None),
    )

    return jax.shard_map(
        on_device, mesh=mesh, in_specs=in_specs, out_specs=out_specs, check_vma=False
    )
```

```python
import jax
import jax.numpy as jnp
from jax import lax
from jax.experimental import pallas as pl
from jax.experimental.pallas import tpu as pltpu
from jax.sharding import PartitionSpec as P

HEAD_DIM = 64
STATE = 128
CONV = 4
CHUNK = 128
VMEM_LIMIT = 60 * 2**20
SMALL_LIMIT = 12 * 2**20
SMALL = ("kernel_6",)
LANES = 128
EPSILON = 1e-05
FULL = lax.Precision.HIGHEST
MOST = lax.Precision.HIGH
F32 = jnp.float32
BF16 = jnp.bfloat16


def swap(x, axis, offset):
    count = lax.axis_size(axis)
    return lax.ppermute(x, axis, [(i, i ^ offset) for i in range(count)])


def tree_sum(parts):
    while len(parts) > 1:
        parts = [parts[i] + parts[i + 1] for i in range(0, len(parts), 2)]
    return parts[0]


def in_order(pieces, place):
    stacked = jnp.stack(pieces)
    return [lax.dynamic_index_in_dim(stacked, j ^ place, 0, False) for j in range(len(pieces))]


def gather_xor(x, axis):
    return [x] + [swap(x, axis, k) for k in range(1, lax.axis_size(axis))]


def scatter_xor(blocks, axis):
    place = lax.axis_index(axis)
    return [
        swap(lax.dynamic_index_in_dim(blocks, place ^ k, 0, False), axis, k)
        if k
        else lax.dynamic_index_in_dim(blocks, place, 0, False)
        for k in range(lax.axis_size(axis))
    ]


def inner_of(count):
    inner = 1
    while 2 * inner * inner < count:
        inner *= 2
    return inner


def far_offsets():
    count = lax.axis_size("dp")
    inner = inner_of(count)
    return [k * inner for k in range(1, count // inner)]


def gather_far(x):
    return [x] + [swap(x, "dp", k) for k in far_offsets()]


def gather_near(far):
    inner = inner_of(lax.axis_size("dp"))
    near = [[piece] + [swap(piece, "dp", j) for j in range(1, inner)] for piece in far]
    return [piece for group in near for piece in group]


def reduce_slabs(slabs):
    parts = [swap(p, "dp", j) if j else p for j, p in enumerate(slabs)]
    return tree_sum([p.astype(F32) for p in parts]).astype(BF16)


def reduce_near(grads):
    count = lax.axis_size("dp")
    inner = inner_of(count)
    inner_place = lax.axis_index("dp") % inner
    shaped = grads.reshape(count // inner, inner, *grads.shape[1:])
    parts = []
    for j in range(inner):
        slab = lax.dynamic_index_in_dim(shaped, inner_place ^ j, 1, False)
        parts.append(swap(slab, "dp", j) if j else slab)
    return tree_sum([p.astype(F32) for p in parts]).astype(BF16)


def reduce_far(near):
    outer_place = lax.axis_index("dp") // inner_of(lax.axis_size("dp"))
    parts = [lax.dynamic_index_in_dim(near, outer_place, 0, False)]
    for k, offset in enumerate(far_offsets()):
        slab = lax.dynamic_index_in_dim(near, outer_place ^ (k + 1), 0, False)
        parts.append(swap(slab, "dp", offset))
    return tree_sum([p.astype(F32) for p in parts])


def dot(a, b, ca, cb, precision=None):
    return lax.dot_general(
        a, b, (((ca,), (cb,)), ((), ())), precision=precision, preferred_element_type=F32
    )


def exact(a, b):
    return dot(a, b, 1, 0, FULL)


def mm(a, b):
    return dot(a, b, 1, 0, MOST)


def mm_nt(a, b):
    return dot(a, b, 1, 1, MOST)


def mm_tn(a, b):
    return dot(a, b, 0, 0, MOST)


def softplus(x):
    small = jnp.exp(-jnp.abs(x))
    up = 1.0 + small
    down = up - 1.0
    log1p = jnp.where(down == 0.0, small, jnp.log(up) * (small / jnp.where(down == 0.0, 1.0, down)))
    return jnp.maximum(x, 0.0) + log1p


def expand_matrix(width):
    head = lax.broadcasted_iota(jnp.int32, (LANES, width), 0)
    column = lax.broadcasted_iota(jnp.int32, (LANES, width), 1)
    return (column // HEAD_DIM == head).astype(F32)


def triangle(lower):
    row = lax.broadcasted_iota(jnp.int32, (CHUNK, CHUNK), 0)
    column = lax.broadcasted_iota(jnp.int32, (CHUNK, CHUNK), 1)
    return row >= column if lower else row <= column


def head_rows(bias_ref, decay_ref, skip_ref, heads_here):
    rows = jnp.concatenate([bias_ref[...], decay_ref[...], skip_ref[...]], 0)
    count = rows.shape[1]
    rows = jnp.concatenate([rows, jnp.zeros((3, LANES - count), F32)], 1)
    rows = jnp.concatenate([rows, jnp.zeros((5, LANES), F32)], 0)
    place = lax.axis_index("seq")
    mine = rows
    for j in range(1, count // heads_here):
        moved = jnp.concatenate([rows[:, j * heads_here :], rows[:, : j * heads_here]], 1)
        mine = jnp.where(place == j, moved, mine)
    return mine


def spread_segments(seg_ref, seg_col, seg_row):
    seg_row[:, : 2 * CHUNK] = jnp.full((8, 2 * CHUNK), -1.0, F32)
    for i in range(seg_ref.shape[1] // CHUNK):
        now = seg_ref[:, i * CHUNK : (i + 1) * CHUNK].astype(F32)
        seg_row[:, (i + 2) * CHUNK : (i + 3) * CHUNK] = jnp.broadcast_to(now, (8, CHUNK))
        seg_col[i * CHUNK : (i + 1) * CHUNK, :] = jnp.broadcast_to(now, (CHUNK, CHUNK)).T


def same_segment(seg_col, back, width):
    now = seg_col[...]
    row = lax.broadcasted_iota(jnp.int32, now.shape, 0)
    same = ((now == pltpu.roll(now, back, 0)) & (row >= back)).astype(F32)
    return jnp.concatenate([same] * (width // LANES), 1)


def masks_of(seg_col, seg_row, i):
    column = seg_col[pl.ds(i * CHUNK, CHUNK), :]

    def row(j):
        return seg_row[:, pl.ds((i + j) * CHUNK, CHUNK)][:1]

    far = (column == row(0)).astype(F32)
    near = (column == row(1)).astype(F32)
    own = (column == row(2)) & triangle(True)
    return far, near, own


def lane_halves():
    lane = lax.broadcasted_iota(jnp.int32, (1, LANES), 1)
    low = (lane < HEAD_DIM).astype(F32)
    return low, 1.0 - low


def rms_inverse(x):
    return lax.rsqrt(jnp.mean(x * x, axis=-1, keepdims=True) + EPSILON)


def gain_row(weights, lane_of_gain):
    tail = weights[:, weights.shape[1] - LANES :]
    pick = (lax.broadcasted_iota(jnp.int32, (8, LANES), 1) == lane_of_gain).astype(BF16)
    return dot(pick, tail, 1, 1)[:1]


def decays(raw, heads):
    step = softplus(raw + heads[0:1])
    return step, step * (-jnp.exp(heads[1:2]))


def spread_heads(columns, low, width):
    pairs = []
    for pair in range(width // LANES):
        first = columns[:, 2 * pair : 2 * pair + 1]
        second = columns[:, 2 * pair + 1 : 2 * pair + 2]
        pairs.append(jnp.where(low > 0.0, first, second))
    return jnp.concatenate(pairs, 1)


def fill_sources(i, v, step, decay, low, vd, vt, ecx):
    cumulative = exact(triangle(True).astype(F32), decay)
    step_x = spread_heads(step, low, v.shape[1])
    cum_x = spread_heads(cumulative, low, v.shape[1])
    last = cum_x[CHUNK - 1 :]
    vd_now = v * step_x
    vd[pl.ds(i * CHUNK, CHUNK), :] = vd_now
    vt[pl.ds((i + 2) * CHUNK, CHUNK), :] = vd_now * jnp.exp(last - cum_x)
    ecx[pl.ds(i * CHUNK + 8, CHUNK), :] = jnp.exp(cum_x)
    return cumulative, step_x, cum_x, last


def head_decay(cumulative, cumulative_t, own, h):
    gap = cumulative[:, h : h + 1] - cumulative_t[h : h + 1, :]
    return jnp.exp(jnp.where(own, gap, -1e30))


def put_in_order(pieces, place, target, source=None, lanes=None):
    for m, piece in enumerate(pieces):
        source_rows = slice(0, piece.shape[0]) if source is None else source
        rows = source_rows.stop - source_rows.start
        start = pl.multiple_of((place ^ m) * rows, rows)
        if lanes is None:
            target[pl.ds(start, rows), :] = piece[...]
        else:
            target[pl.ds(start, rows), lanes[0]] = piece[source_rows, lanes[1]]


def dp_index(pieces):
    return lax.axis_index("dp") if len(pieces) > 1 else 0


def put_second(pieces, place, wg_ref=None, wo_ref=None):
    rows, both = pieces[0].shape
    width = both // 2
    if wg_ref is not None:
        put_in_order(pieces, place, wg_ref, slice(0, rows), (slice(0, width), slice(0, width)))
    if wo_ref is not None:
        folds = wo_ref.shape[1] // width
        part = rows // folds
        for k in range(folds):
            to = (slice(k * width, (k + 1) * width), slice(width, 2 * width))
            put_in_order(pieces, place, wo_ref, slice(k * part, (k + 1) * part), to)


def small_spots(rows, lengths):
    group = min(rows, len(lengths))
    return [(i % group, (i // group) * max(lengths)) for i in range(len(lengths))]


def store_slabs(values, outs, lanes):
    if len(outs[0].shape) == 2:
        outs[0][...] = values[:, lanes].astype(BF16)
        return
    inner, (outer, rows, _) = len(outs), outs[0].shape
    place = lax.axis_index("dp") % inner if inner > 1 else 0
    for j, out in enumerate(outs):
        for o in range(outer):
            start = (o * inner + (place ^ j)) * rows
            if inner > 1:
                start = pl.multiple_of(start, rows)
            out[o] = values[pl.ds(start, rows), lanes].astype(BF16)


def store_far(values, outs):
    if len(outs) == 1:
        outs[0][...] = values[...].astype(BF16)
        return
    rows = outs[0].shape[0]
    inner = inner_of(lax.axis_size("dp"))
    for k, out in enumerate(outs):
        start = pl.multiple_of(((lax.axis_index("dp") // inner) ^ k) * rows, rows)
        out[...] = values[pl.ds(start, rows), :].astype(BF16)


def store_pieces(values, outs, behind=0):
    rows = outs[0].shape[0] - behind
    for k, out in enumerate(outs):
        start = pl.multiple_of((lax.axis_index("seq") ^ k) * rows, rows)
        out[behind:, :] = values[pl.ds(start, rows), :].astype(BF16)


def finish_kernel(width, inner, heads_here, lengths, spots):
    def body(*refs):
        count = inner // width
        parts, refs = refs[:count], refs[count:]
        grad_ref, outs, blocks = refs[0], refs[1:-1], refs[-1]
        rows = grad_ref.shape[0]
        stride = blocks.shape[0] // count
        states, tail = width, width + 2 * STATE
        for k, part in enumerate(parts):
            start = pl.multiple_of((lax.axis_index("seq") ^ k) * stride, stride)
            blocks[pl.ds(start, rows), :] = part[...].astype(F32)
        steps = []
        for j in range(count):
            at = slice(j * stride, j * stride + rows)
            grad_ref[:, j * width : (j + 1) * width] = blocks[at, tail + LANES :]
            grad_ref[:, inner + j * width : inner + (j + 1) * width] = blocks[at, :width]
            steps.append(blocks[at, tail : tail + heads_here])
        both = tree_sum([part[:, states:tail].astype(F32) for part in parts])
        grad_ref[:, 2 * inner : 2 * inner + 2 * STATE] = both
        grad_ref[:, 2 * inner + 2 * STATE :] = jnp.concatenate(steps, 1)
        total = tree_sum([part[:, tail : tail + LANES].astype(F32) for part in parts])
        found = []
        for length, (row, lane) in zip(lengths, spots):
            first = heads_here + lane
            found.append(total[row : row + 1, first : first + length])
        outs[0][...] = jnp.concatenate(found[:CONV], 0)
        for out, vector in zip(outs[1:], found[CONV:]):
            out[...] = vector

    return body


def pack_kernel(width, inner, heads_here, count):
    def body(w_ref, taps_ref, shift_ref, gate_ref, norm_ref, *refs):
        outs, blocks = refs[:-1], refs[-1]
        rows = w_ref.shape[0]
        stride = blocks.shape[0] // count
        states = 2 * inner + 2 * STATE
        norm = jnp.concatenate([norm_ref[...].astype(F32), jnp.zeros((1, LANES - rows), F32)], 1)
        column = jnp.broadcast_to(norm, (LANES, LANES)).T[:rows]
        taps = taps_ref[...].astype(F32)
        vectors = [taps[i : i + 1] for i in range(CONV)]
        vectors += [shift_ref[...].astype(F32), gate_ref[...].astype(F32)]
        spots = small_spots(rows, [v.shape[1] for v in vectors])
        lane = lax.broadcasted_iota(jnp.int32, (rows, LANES), 1)
        row = lax.broadcasted_iota(jnp.int32, (rows, LANES), 0)
        shared = jnp.where(lane == heads_here, column, 0.0)
        for vector, (at_row, at_lane) in zip(vectors, spots):
            start = heads_here + 1 + at_lane
            pieces = [jnp.zeros((1, start), F32), vector]
            pieces.append(jnp.zeros((1, LANES - start - vector.shape[1]), F32))
            shared = shared + jnp.where(row == at_row, jnp.concatenate(pieces, 1), 0.0)
        for j in range(count):
            at = slice(j * stride, j * stride + rows)
            first = states + j * heads_here
            blocks[at, :width] = w_ref[:, inner + j * width : inner + (j + 1) * width].astype(F32)
            blocks[at, width : width + 2 * STATE] = w_ref[:, 2 * inner : states].astype(F32)
            steps = w_ref[:, first : first + heads_here].astype(F32)
            tail = jnp.concatenate([steps, shared[:, heads_here:]], 1)
            blocks[at, width + 2 * STATE : width + 2 * STATE + LANES] = tail
            gate = w_ref[:, j * width : (j + 1) * width].astype(F32)
            blocks[at, width + 2 * STATE + LANES :] = gate
        for k in range(count):
            start = pl.multiple_of((lax.axis_index("seq") ^ k) * stride, stride)
            outs[k][...] = blocks[pl.ds(start, rows), :].astype(BF16)

    return body


def forward_kernel(width, lane_of_gain, x_count, w_count):
    heads_here = width // HEAD_DIM

    def body(*refs):
        x_pieces, refs = refs[:x_count], refs[x_count:]
        w_pieces, refs = refs[:w_count], refs[w_count:]
        conv_ref, seg_ref, bias_ref, decay_ref, skip_ref, normed_ref, proj_ref, pre_ref, y_ref, bpad, vd, vt, ecx, seg_col, seg_row, x_ref, w_ref = refs
        put_in_order(x_pieces, lax.axis_index("seq"), x_ref)
        put_in_order(w_pieces, dp_index(w_pieces), w_ref)
        x = x_ref[...].astype(F32)
        gain = gain_row(w_ref[...], lane_of_gain)
        normed_ref[...] = (x * rms_inverse(x) * gain).astype(BF16)
        proj_ref[...] = dot(normed_ref[...], w_ref[...], 1, 0)
        spread_segments(seg_ref, seg_col, seg_row)
        channels = width + 2 * STATE
        u = proj_ref[:, :channels]
        running = conv_ref[CONV : CONV + 1, :] + conv_ref[CONV - 1 : CONV, :] * u
        for back in range(1, CONV):
            tap = conv_ref[CONV - 1 - back : CONV - back, :]
            running = running + tap * pltpu.roll(u, back, 0) * same_segment(seg_col, back, channels)
        pre_ref[...] = running
        bpad[pl.ds(0, 2 * CHUNK), :] = jnp.zeros((2 * CHUNK, STATE), F32)
        vt[pl.ds(0, 2 * CHUNK), :] = jnp.zeros((2 * CHUNK, width), F32)
        ecx[pl.ds(0, 8), :] = jnp.zeros((8, width), F32)
        b_pre = running[:, width : width + STATE]
        bpad[pl.ds(2 * CHUNK, x.shape[0]), :] = b_pre * jax.nn.sigmoid(b_pre)
        expand = expand_matrix(width)
        low, high = lane_halves()
        heads = head_rows(bias_ref, decay_ref, skip_ref, heads_here)
        skip_x = exact(jnp.broadcast_to(heads[2:3], (8, LANES)), expand)[:1]

        def chunk(i, carry):
            rows = pl.ds(i * CHUNK, CHUNK)
            v_pre = pre_ref[rows, :width]
            c_pre = pre_ref[rows, width + STATE :]
            v = v_pre * jax.nn.sigmoid(v_pre)
            c = c_pre * jax.nn.sigmoid(c_pre)
            step, decay = decays(proj_ref[rows, channels:], heads)
            cumulative, _, _, _ = fill_sources(i, v, step, decay, low, vd, vt, ecx)
            cumulative_t = cumulative.T
            far, near, own = masks_of(seg_col, seg_row, i)
            window = pl.ds(i * CHUNK, 3 * CHUNK)
            scores = mm_nt(c, bpad[window, :])
            s_far = scores[:, :CHUNK] * far
            s_near = scores[:, CHUNK : 2 * CHUNK] * near
            s_own = scores[:, 2 * CHUNK :]
            ecx_now = ecx[pl.ds(i * CHUNK + 8, CHUNK), :]
            last_before = ecx[pl.ds(i * CHUNK, 8), :][7:8]
            vt_far = vt[rows, :] * last_before
            vt_near = vt[pl.ds((i + 1) * CHUNK, CHUNK), :]
            off = mm(s_far, vt_far) + mm(s_near, vt_near)
            y_ref[rows, :] = off * ecx_now + skip_x * v
            for pair in range(heads_here // 2):
                lanes = slice(pair * LANES, (pair + 1) * LANES)
                n0 = s_own * head_decay(cumulative, cumulative_t, own, 2 * pair)
                n1 = s_own * head_decay(cumulative, cumulative_t, own, 2 * pair + 1)
                vp = vd[rows, lanes]
                both = mm(jnp.concatenate([n0, n1], 1), jnp.concatenate([vp * low, vp * high], 0))
                y_ref[rows, lanes] = y_ref[rows, lanes] + both
            return carry

        for turn in range(x.shape[0] // CHUNK):
            chunk(turn, 0)

    return body


def gate_kernel(og_count, w_count):
    def body(*refs):
        og_pieces, refs = refs[:og_count], refs[og_count:]
        w_pieces, refs = refs[:w_count], refs[w_count:]
        normed_ref, y_ref, gain_ref, gate_ref, dg_ref, stats_ref, og_ref, wg_ref, wo_ref = refs
        put_in_order(og_pieces, lax.axis_index("seq"), og_ref)
        put_second(w_pieces, dp_index(w_pieces), wg_ref, wo_ref)
        gate = dot(normed_ref[...], wg_ref[...], 1, 0)
        gate_ref[...] = gate
        d_gated = dot(og_ref[...], wo_ref[...], 1, 1)
        dg_ref[...] = d_gated
        v = y_ref[...] * (gate * jax.nn.sigmoid(gate))
        squares = jnp.sum(v * v, axis=1, keepdims=True)
        cross = jnp.sum(v * (d_gated * gain_ref[...]), axis=1, keepdims=True)
        lane = lax.broadcasted_iota(jnp.int32, (CHUNK, LANES), 1)
        for i in range(stats_ref.shape[0]):
            rows = slice(i * CHUNK, (i + 1) * CHUNK)
            both = jnp.where(lane == 0, squares[rows], jnp.where(lane == 1, cross[rows], 0.0))
            stats_ref[i] = both.T[:8]

    return body


def out_kernel(width, whole_width, og_count, w_count, slab_count, block_rows):
    def body(*refs):
        og_pieces, refs = refs[:og_count], refs[og_count:]
        w_pieces, refs = refs[:w_count], refs[w_count:]
        stats, refs = refs[:og_count], refs[og_count:]
        normed_ref, gate_ref, dg_ref, y_ref, gain_ref = refs[:5]
        out_refs, refs = refs[5 : 5 + og_count], refs[5 + og_count :]
        slabs, refs = refs[:slab_count], refs[slab_count:]
        dgate_ref, dy_ref, ggain_ref, og_ref, wo_ref, out_all, grad_all = refs
        put_in_order(og_pieces, lax.axis_index("seq"), og_ref)
        put_second(w_pieces, dp_index(w_pieces), None, wo_ref)
        columns = []
        for i in range(stats[0].shape[0]):
            total = tree_sum([part[i] for part in stats])
            square = jnp.concatenate([total, jnp.zeros((CHUNK - 8, LANES), F32)], 0)
            columns.append(square.T)
        columns = jnp.concatenate(columns, 0)
        inverse = lax.rsqrt(columns[:, 0:1] / whole_width + EPSILON)
        cross = columns[:, 1:2] / whole_width
        gate = gate_ref[...]
        sig = jax.nn.sigmoid(gate)
        silu = gate * sig
        y = y_ref[...]
        v = y * silu
        gain = gain_ref[...]
        scaled = v * inverse
        gated = (scaled * gain).astype(BF16)
        out_all[...] = dot(gated, wo_ref[...], 1, 0)
        store_pieces(out_all, out_refs)
        rows = block_rows
        folds = og_ref.shape[1] // width
        part = rows // folds
        g_out = dot(gated, og_ref[...], 0, 0)
        for d in range(grad_all.shape[0] // rows):
            for k in range(folds):
                to = slice(d * rows + k * part, d * rows + (k + 1) * part)
                grad_all[to, width:] = g_out[d * part : (d + 1) * part, k * width : (k + 1) * width]
        d_gated = dg_ref[...]
        ggain_ref[...] = jnp.broadcast_to(jnp.sum(d_gated * scaled, axis=0, keepdims=True), (8, width))
        dv = inverse * (d_gated * gain - v * (inverse * inverse * cross))
        dy_ref[...] = dv * silu
        dgate = (dv * y * (sig * (1.0 + gate * (1.0 - sig)))).astype(BF16)
        dgate_ref[...] = dgate
        grad_all[:, :width] = dot(normed_ref[...], dgate, 0, 0)
        store_far(grad_all, slabs)

    return body


def mixer_back_kernel(width):
    heads_here = width // HEAD_DIM

    def body(conv_ref, seg_ref, bias_ref, decay_ref, skip_ref, proj_ref, pre_ref, y_ref, dy_ref, dconv_ref, draw, conv_grad_ref, head_grad_ref, bpad, vd, vt, ecx, seg_col, seg_row, tailx, stepx, cums, ua, db, dpre):
        length = proj_ref.shape[0]
        spread_segments(seg_ref, seg_col, seg_row)
        chunks = length // CHUNK
        channels = width + 2 * STATE
        expand = expand_matrix(width)
        low, high = lane_halves()
        heads = head_rows(bias_ref, decay_ref, skip_ref, heads_here)
        rate = jnp.exp(heads[1:2])
        skip_x = exact(jnp.broadcast_to(heads[2:3], (8, LANES)), expand)[:1]
        bpad[pl.ds(0, 2 * CHUNK), :] = jnp.zeros((2 * CHUNK, STATE), F32)
        vt[pl.ds(0, 2 * CHUNK), :] = jnp.zeros((2 * CHUNK, width), F32)
        tailx[pl.ds(0, 2 * CHUNK), :] = jnp.zeros((2 * CHUNK, width), F32)
        ecx[pl.ds(0, 8), :] = jnp.zeros((8, width), F32)
        b_pre = pre_ref[:, width : width + STATE]
        bpad[pl.ds(2 * CHUNK, length), :] = b_pre * jax.nn.sigmoid(b_pre)
        ua[...] = jnp.zeros(ua.shape, F32)
        db[...] = jnp.zeros(db.shape, F32)

        def prepare(i, carry):
            rows = pl.ds(i * CHUNK, CHUNK)
            v_pre = pre_ref[rows, :width]
            v = v_pre * jax.nn.sigmoid(v_pre)
            step, decay = decays(proj_ref[rows, channels:], heads)
            cumulative, step_x, cum_x, last = fill_sources(i, v, step, decay, low, vd, vt, ecx)
            cums[rows, :] = cumulative
            stepx[rows, :] = step_x
            tailx[pl.ds((i + 2) * CHUNK, CHUNK), :] = jnp.exp(last - cum_x)
            return carry

        for turn in range(chunks):
            prepare(turn, 0)

        def chunk(turn, carry):
            later, g_bias, g_rate, g_skip = carry
            i = chunks - 1 - turn
            rows = pl.ds(i * CHUNK, CHUNK)
            rows_near = pl.ds((i + 1) * CHUNK, CHUNK)
            rows_own = pl.ds((i + 2) * CHUNK, CHUNK)
            window = pl.ds(i * CHUNK, 3 * CHUNK)
            v_pre = pre_ref[rows, :width]
            v_sig = jax.nn.sigmoid(v_pre)
            v = v_pre * v_sig
            c_pre = pre_ref[rows, width + STATE :]
            c_sig = jax.nn.sigmoid(c_pre)
            c = c_pre * c_sig
            raw = proj_ref[rows, channels:]
            step, decay = decays(raw, heads)
            cumulative = cums[rows, :]
            cumulative_t = cumulative.T
            far, near, own = masks_of(seg_col, seg_row, i)
            b_window = bpad[window, :]
            scores = mm_nt(c, b_window)
            s_far = scores[:, :CHUNK] * far
            s_near = scores[:, CHUNK : 2 * CHUNK] * near
            s_own = scores[:, 2 * CHUNK :]
            dy = dy_ref[rows, :]
            dye = dy * ecx[pl.ds(i * CHUNK + 8, CHUNK), :]
            dye_far = dye * ecx[pl.ds(i * CHUNK, 8), :][7:8]
            ds_far = mm_nt(dye_far, vt[rows, :]) * far
            ds_near = mm_nt(dye, vt[rows_near, :]) * near
            ua[rows, :] = ua[rows, :] + tailx[rows, :] * mm_tn(s_far, dye_far)
            ua[rows_near, :] = ua[rows_near, :] + tailx[rows_near, :] * mm_tn(s_near, dye)
            ds_own = jnp.zeros((CHUNK, CHUNK), F32)
            for pair in range(heads_here // 2):
                lanes = slice(pair * LANES, (pair + 1) * LANES)
                d0 = head_decay(cumulative, cumulative_t, own, 2 * pair)
                d1 = head_decay(cumulative, cumulative_t, own, 2 * pair + 1)
                dyp = dy_ref[rows, lanes]
                split = jnp.concatenate([dyp * low, dyp * high], 0)
                dm = mm_nt(split, vd[rows, lanes])
                ds_own = ds_own + dm[:CHUNK] * d0 + dm[CHUNK:] * d1
                u_pair = mm_tn(jnp.concatenate([s_own * d0, s_own * d1], 0), split)
                ua[rows_own, lanes] = ua[rows_own, lanes] + u_pair
            ds_all = jnp.concatenate([ds_far, ds_near, ds_own], 1)
            dc = mm(ds_all, b_window)
            db[window, :] = db[window, :] + mm_tn(ds_all, c)
            u_total = ua[rows_own, :]
            received = mm_nt(dy * (y_ref[rows, :] - skip_x * v), expand)
            d_step = mm_nt(v * u_total, expand)
            gap = received - step * d_step
            d_decay = exact(triangle(False).astype(F32), gap) + later
            d_step = d_step - d_decay * rate
            d_raw = d_step * jax.nn.sigmoid(raw + heads[0:1])
            draw[rows, :] = d_raw.astype(BF16)
            dv = stepx[rows, :] * u_total + skip_x * dy
            dpre[rows, :width] = dv * (v_sig * (1.0 + v_pre * (1.0 - v_sig)))
            b_pre = pre_ref[rows, width : width + STATE]
            b_sig = jax.nn.sigmoid(b_pre)
            dpre[rows, width : width + STATE] = db[rows_own, :] * (b_sig * (1.0 + b_pre * (1.0 - b_sig)))
            dpre[rows, width + STATE :] = dc * (c_sig * (1.0 + c_pre * (1.0 - c_sig)))
            g_skip = g_skip + jnp.sum(dy * v, axis=0, keepdims=True)
            g_bias = g_bias + jnp.sum(d_raw, axis=0, keepdims=True)
            g_rate = g_rate + jnp.sum(d_decay * decay, axis=0, keepdims=True)
            return (later + jnp.sum(gap, axis=0, keepdims=True), g_bias, g_rate, g_skip)

        none = jnp.zeros((1, LANES), F32)
        none_wide = jnp.zeros((1, heads_here * HEAD_DIM), F32)
        start = (none, none, none, none_wide)
        state = start
        for turn in range(chunks):
            state = chunk(turn, state)
        _, g_bias, g_rate, g_skip = state
        g_skip = dot(jnp.broadcast_to(g_skip, (8, g_skip.shape[1])), expand, 1, 1, FULL)[:1]
        head_grad_ref[...] = jnp.concatenate([g_bias, g_rate, g_skip, jnp.zeros((5, LANES), F32)], 0)
        u = proj_ref[:, :channels]
        d = dpre[...]
        du = conv_ref[CONV - 1 : CONV, :] * d
        taps = [jnp.sum(d * u, axis=0, keepdims=True)]
        for back in range(1, CONV):
            masked = d * same_segment(seg_col, back, channels)
            taps.insert(0, jnp.sum(masked * pltpu.roll(u, back, 0), axis=0, keepdims=True))
            du = du + conv_ref[CONV - 1 - back : CONV - back, :] * pltpu.roll(masked, length - back, 0)
        taps.append(jnp.sum(d, axis=0, keepdims=True))
        taps.append(jnp.zeros((8 - CONV - 1, channels), F32))
        conv_grad_ref[...] = jnp.concatenate(taps, 0)
        dconv_ref[...] = du.astype(BF16)

    return body


def weight_back_kernel(x_count, w_count, slab_count):
    def body(*refs):
        x_pieces, refs = refs[:x_count], refs[x_count:]
        w_pieces, refs = refs[:w_count], refs[w_count:]
        g_pieces, refs = refs[:w_count], refs[w_count:]
        out_parts, refs = refs[:x_count], refs[x_count:]
        normed_ref, dconv_ref, draw_ref, dgate_ref = refs[:4]
        slabs, refs = refs[4 : 4 + slab_count], refs[4 + slab_count :]
        dn_refs, refs = refs[:x_count], refs[x_count:]
        norm_grad_ref, x_ref, w_ref, wg_ref, dn_all, gin_ref = refs
        put_in_order(x_pieces, lax.axis_index("seq"), x_ref)
        put_in_order(w_pieces, dp_index(w_pieces), w_ref)
        put_second(g_pieces, dp_index(w_pieces), wg_ref)
        channels = dconv_ref.shape[1]
        dconv, draw = dconv_ref[...], draw_ref[...]
        dn = dot(dconv, w_ref[:, :channels], 1, 1) + dot(draw, w_ref[:, channels:], 1, 1)
        dn = dn + dot(dgate_ref[...], wg_ref[...], 1, 1)
        dn_all[...] = dn
        store_pieces(dn_all, dn_refs, out_parts[0].shape[0])
        for out_part, both_ref in zip(out_parts, dn_refs):
            both_ref[: out_part.shape[0], :] = out_part[...]
        gin_ref[:, :channels] = dot(normed_ref[...], dconv, 0, 0)
        x = x_ref[...].astype(F32)
        along = jnp.sum(dn * (x * rms_inverse(x)), axis=0, keepdims=True)
        norm_grad_ref[...] = along
        gin_ref[:, channels:] = dot(normed_ref[...], draw, 0, 0)
        early = slabs[0].shape[-1]
        store_slabs(gin_ref, slabs[: slab_count // 2], slice(0, early))
        store_slabs(gin_ref, slabs[slab_count // 2 :], slice(early, gin_ref.shape[1]))

    return body


def call(name, body, outs, scratch, *operands):
    vmem = pl.BlockSpec(memory_space=pltpu.VMEM)
    return pl.pallas_call(
        body,
        out_shape=[jax.ShapeDtypeStruct(shape, kind) for shape, kind in outs],
        in_specs=[vmem] * len(operands),
        out_specs=[vmem] * len(outs),
        scratch_shapes=[
            pltpu.VMEM(*shape) if isinstance(shape[0], tuple) else pltpu.VMEM(shape, F32)
            for shape in scratch
        ],
        compiler_params=pltpu.CompilerParams(vmem_limit_bytes=SMALL_LIMIT if name in SMALL else VMEM_LIMIT),
    )(*operands)


def on_device(
    hidden_in,
    segments,
    norm_gain,
    in_weight,
    conv_weight,
    conv_bias,
    step_bias,
    decay_log,
    skip_weight,
    gate_gain,
    out_weight,
    out_grad,
):
    row_count, piece, model = hidden_in.shape
    assert row_count == 1
    seq_n, dp_n = lax.axis_size("seq"), lax.axis_size("dp")
    owners = seq_n * dp_n
    place, dp_place = lax.axis_index("seq"), lax.axis_index("dp")
    length = piece * seq_n
    head_count = step_bias.shape[0]
    inner = head_count * HEAD_DIM
    heads_here = head_count // seq_n
    width = inner // seq_n
    channels = width + 2 * STATE
    cols = channels + LANES
    rows = in_weight.shape[0]
    conv_here = conv_bias.shape[0]
    gate_here = gate_gain.shape[0]

    stride = -(-rows // 16) * 16
    blocks = call(
        "pack",
        pack_kernel(width, inner, heads_here, seq_n),
        [((rows, cols + width), BF16)] * seq_n,
        [(seq_n * stride, cols + width)],
        in_weight, conv_weight, conv_bias[None], gate_gain[None], norm_gain[None],
    )
    blocks = [b if k == 0 else swap(b, "seq", k) for k, b in enumerate(blocks)]
    mine = jnp.concatenate(in_order(blocks, place), 0)
    first_part, gate_part = mine[:, :cols], mine[:, cols:]
    far_first = gather_far(first_part)
    x_pieces = gather_xor(hidden_in[0], "seq")
    og_pieces = gather_xor(out_grad[0], "seq")

    def linear(d, s):
        return d * seq_n + s

    to_heads = [(b, linear(b % dp_n, b // dp_n)) for b in range(owners)]
    out_block = lax.ppermute(out_weight, ("dp", "seq"), to_heads)
    out_rows = out_block.shape[0]
    folded = jnp.concatenate(
        [out_block[:, k * width : (k + 1) * width] for k in range(model // width)], 0
    )
    second = jnp.concatenate([gate_part, folded], 1)
    far_second = gather_far(second)
    w_first = gather_near(far_first)
    w_second = gather_near(far_second)
    split_here = not out_rows % 16
    if not split_here:
        w_first = [jnp.concatenate(in_order(w_first, dp_place), 0)]
        w_second = in_order(w_second, dp_place)
        folds = [slice(k * out_rows, (k + 1) * out_rows) for k in range(model // width)]
        w_out = jnp.concatenate([p[f, width:] for f in folds for p in w_second], 0)
        w_second = [
            jnp.concatenate([jnp.concatenate([p[:, :width] for p in w_second], 0), w_out], 1)
        ]
    if len(w_first) > 1:
        tail = jnp.concatenate(in_order([p[:, channels:] for p in w_first], dp_place), 0)
    else:
        tail = w_first[0][:, channels:]
    tail = tail.reshape(owners, rows, LANES)
    lengths = [conv_here] * (CONV + 1) + [gate_here]
    spots = small_spots(rows, lengths)
    if rows >= len(lengths):
        conv_all = tail[:, : CONV + 1, heads_here + 1 : heads_here + 1 + conv_here]
        conv_all = conv_all.transpose(1, 0, 2).reshape(CONV + 1, owners * conv_here)
    else:
        conv_all = []
        for r, lane in spots[: CONV + 1]:
            first = heads_here + 1 + lane
            conv_all.append(tail[:, r, first : first + conv_here].reshape(1, -1))
        conv_all = jnp.concatenate(conv_all, 0)
    conv_mine = jnp.concatenate(
        [
            lax.dynamic_slice_in_dim(conv_all[:, :inner], place * width, width, 1),
            conv_all[:, inner:],
        ],
        1,
    )
    conv_mine = jnp.pad(conv_mine.astype(F32), ((0, 8 - CONV - 1), (0, 0)))
    first = heads_here + 1 + spots[-1][1]
    gain_all = tail[:, spots[-1][0], first : first + gate_here]
    gain_mine = lax.dynamic_slice_in_dim(gain_all.reshape(1, inner), place * width, width, 1)
    gain_mine = gain_mine.astype(F32)

    head_params = (step_bias[None], decay_log[None], skip_weight[None])

    chunks = length // CHUNK
    tall = length + 2 * CHUNK
    sources = [(tall, STATE), (length, width), (tall, width), (length + 8, width)]
    sources += [(length, LANES), (8, tall)]
    normed, proj, pre, y = call(
        "kernel_1",
        forward_kernel(width, heads_here, len(x_pieces), len(w_first)),
        [((length, model), BF16)]
        + [((length, cols), F32), ((length, channels), F32), ((length, width), F32)],
        sources + [((length, model), BF16), ((model, cols), BF16)],
        *x_pieces, *w_first, conv_mine, segments, *head_params,
    )
    og_scratch, wg_scratch = ((length, model), BF16), ((model, width), BF16)
    wo_scratch = ((width, model), BF16)
    gate, d_gated, stats = call(
        "kernel_2",
        gate_kernel(len(og_pieces), len(w_second)),
        [((length, width), F32), ((length, width), F32), ((chunks, 8, LANES), F32)],
        [og_scratch, wg_scratch, wo_scratch],
        *og_pieces, *w_second, normed, y, gain_mine,
    )
    stats = gather_xor(stats, "seq")
    block_rows = rows * seq_n
    dp_inner = inner_of(dp_n)
    dp_outer = dp_n // dp_inner
    part_lanes = (width + STATE, STATE + LANES)
    if split_here:
        late_parts = [[((dp_outer, block_rows, n), BF16)] * dp_inner for n in part_lanes]
        far_blocks = [((dp_inner * block_rows, 2 * width), BF16)] * dp_outer
    else:
        late_parts = [[((model, n), BF16)] for n in part_lanes]
        far_blocks = [((model, 2 * width), BF16)]
    pieces = [((piece, model), BF16)] * seq_n

    def near_sum(made):
        if split_here:
            return reduce_slabs(made)
        return reduce_near(made[0].reshape(dp_n, -1, made[0].shape[-1]))

    def far_sum(made):
        if not split_here:
            outer_place = dp_place // dp_inner
            blocks = made[0].reshape(dp_outer, dp_inner * block_rows, 2 * width)
            made = [
                lax.dynamic_index_in_dim(blocks, outer_place ^ k, 0, False)
                for k in range(dp_outer)
            ]
        parts = [made[0]]
        for k, offset in enumerate(far_offsets()):
            parts.append(swap(made[k + 1], "dp", offset))
        return tree_sum([p.astype(F32) for p in parts]).astype(BF16)

    made = call(
        "kernel_3",
        out_kernel(width, inner, len(og_pieces), len(w_second), len(far_blocks), block_rows),
        pieces + far_blocks
        + [((length, width), BF16), ((length, width), F32), ((8, width), F32)],
        [og_scratch, wo_scratch, (length, model), (model, 2 * width)],
        *og_pieces, *w_second, *stats, normed, gate, d_gated, y, gain_mine,
    )
    out_parts, made = made[:seq_n], made[seq_n:]
    far_early = far_sum(made[: len(far_blocks)])
    d_gate, dy, g_gain = made[len(far_blocks) :]
    dconv, draw, conv_grad, head_grad = call(
        "kernel_4",
        mixer_back_kernel(width),
        [((length, channels), BF16), ((length, LANES), BF16)]
        + [((8, channels), F32), ((8, LANES), F32)],
        sources
        + [(tall, width), (length, width), (length, LANES), (tall, width), (tall, STATE)]
        + [(length, channels)],
        conv_mine, segments, *head_params, proj, pre, y, dy,
    )

    made = call(
        "kernel_5",
        weight_back_kernel(len(x_pieces), len(w_first), 2 * len(late_parts[0])),
        late_parts[0] + late_parts[1] + [((2 * piece, model), BF16)] * seq_n + [((1, model), F32)],
        [((length, model), BF16), ((model, cols), BF16), wg_scratch, (length, model), (model, cols)],
        *x_pieces, *w_first, *w_second, *out_parts, normed, dconv, draw, d_gate,
    )
    slab_count = len(late_parts[0])
    dn_pieces, norm_grad = made[2 * slab_count : -1], made[-1]
    near_values = near_sum(made[:slab_count])
    rest = made[slab_count : 2 * slab_count]
    half = part_lanes[1]
    folds = 2 * width // half
    conv_full = jnp.zeros((CONV + 1, inner), F32)
    conv_full = lax.dynamic_update_slice_in_dim(
        conv_full, conv_grad[: CONV + 1, :width], place * width, 1
    )
    conv_full = jnp.concatenate([conv_full, conv_grad[: CONV + 1, width:]], 1)
    conv_full = conv_full.reshape(CONV + 1, owners, conv_here).transpose(1, 0, 2)
    gain_full = lax.dynamic_update_slice_in_dim(
        jnp.zeros((inner,), F32), g_gain[0], place * width, 0
    )
    heads_full = lax.dynamic_update_slice_in_dim(
        jnp.zeros((3, head_count), F32), head_grad[:3, :heads_here], place * heads_here, 1
    )
    heads_rows = jnp.broadcast_to(heads_full[None], (owners, 3, head_count))
    lengths = [conv_here] * (CONV + 1) + [gate_here, rows] + [head_count] * 3
    small_at = small_spots(rows, lengths)
    group, longest = min(rows, len(lengths)), max(lengths)

    def fit(vectors):
        return jnp.pad(vectors, ((0, 0), (0, 0), (0, longest - vectors.shape[2])))

    small = jnp.concatenate(
        [fit(conv_full), fit(gain_full.reshape(owners, 1, gate_here))]
        + [fit(norm_grad.reshape(owners, 1, rows)), fit(heads_rows)],
        1,
    )
    sets = -(-len(lengths) // group)
    small = jnp.pad(small, ((0, 0), (0, sets * group - len(lengths)), (0, 0)))
    small = jnp.concatenate([small[:, g * group : (g + 1) * group] for g in range(sets)], 2)
    small = jnp.pad(
        small,
        ((0, 0), (0, rows - group), (heads_here, LANES - heads_here - small.shape[2])),
    ).astype(BF16)
    inner_place = dp_place % dp_inner
    small = small.reshape(dp_outer, dp_inner, block_rows, LANES)
    far_early = far_early.reshape(dp_inner, block_rows, 2 * width)
    if not split_here:
        rest = rest[0].reshape(dp_outer, dp_inner, block_rows, half)
        rest = [lax.dynamic_index_in_dim(rest, inner_place ^ j, 1, False) for j in range(dp_inner)]
    together = []
    for j, slab in enumerate(rest):
        short = lax.dynamic_index_in_dim(small, inner_place ^ j, 1, False)
        slab = slab + jnp.pad(short, ((0, 0), (0, 0), (half - LANES, 0)))
        block = lax.dynamic_index_in_dim(far_early, inner_place ^ j, 0, False)
        block = jnp.stack([block[:, f * half : (f + 1) * half] for f in range(folds)])
        together.append(jnp.concatenate([slab, block], 0))
    together = [swap(t, "dp", j) if j else t for j, t in enumerate(together)]
    together = tree_sum([t.astype(F32) for t in together])
    near_rest = together[:dp_outer].astype(BF16)
    early = jnp.concatenate([together[dp_outer + f] for f in range(folds)], 1)
    late = [reduce_far(near_values), reduce_far(near_rest)]
    own_out = early[:, width:]
    own_out = jnp.concatenate(
        [own_out[k * out_rows : (k + 1) * out_rows] for k in range(model // width)], 1
    )
    back_pairs = [(target, source) for source, target in to_heads]
    grad_out_w = lax.ppermute(own_out.astype(BF16), ("dp", "seq"), back_pairs)
    dn_parts = [swap(p, "seq", k) if k else p for k, p in enumerate(dn_pieces)]
    rows_total = tree_sum([p.astype(F32) for p in dn_parts])
    result = hidden_in[0].astype(F32) + rows_total[:piece]
    d_normed = rows_total[piece:]

    both = jnp.concatenate([*late, early[:, :width]], 1).reshape(seq_n, rows, cols + width)
    parts = scatter_xor(both.astype(BF16), "seq")
    short = [((CONV, conv_here), F32)] + [((1, n), F32) for n in lengths[CONV:]]
    grad_in_w, *short = call(
        "kernel_6",
        finish_kernel(width, inner, heads_here, lengths, small_at),
        [((rows, in_weight.shape[1]), F32)] + short,
        [(seq_n * stride, cols + width)],
        *parts,
    )

    widened = hidden_in[0].astype(F32)
    inverse = lax.rsqrt(jnp.mean(widened * widened, axis=-1, keepdims=True) + EPSILON)
    gain_full_row = tail[:, :, heads_here].reshape(1, -1).astype(F32)
    scaled = d_normed * gain_full_row
    along = jnp.mean(scaled * widened, axis=-1, keepdims=True)
    grad_hidden = out_grad[0].astype(F32) + inverse * (scaled - widened * (inverse * inverse * along))
    return (
        result[None],
        grad_hidden[None],
        short[3][0],
        grad_in_w,
        short[0],
        short[1][0],
        short[4][0],
        short[5][0],
        short[6][0],
        short[2][0],
        grad_out_w.astype(F32),
    )


def solution(mesh):
    in_specs = (
        P("dp", "seq", None),
        P("dp", None),
        P(("dp", "seq")),
        P(("dp", "seq"), None),
        P(None, ("dp", "seq")),
        P(("dp", "seq")),
        P(),
        P(),
        P(),
        P(("dp", "seq")),
        P(("dp", "seq"), None),
        P("dp", "seq", None),
    )
    out_specs = (
        P("dp", "seq", None),
        P("dp", "seq", None),
        P(("dp", "seq")),
        P(("dp", "seq"), None),
        P(None, ("dp", "seq")),
        P(("dp", "seq")),
        P(),
        P(),
        P(),
        P(("dp", "seq")),
        P(("dp", "seq"), None),
    )

    return jax.shard_map(
        on_device, mesh=mesh, in_specs=in_specs, out_specs=out_specs, check_vma=False
    )
```
